32 devices in a mesh: ga: 8 (over z, y), ha: 4 (over x, core).
Axes of the slice: x: 2, y: 2, z: 4, core: 2. Of those that a mesh axis runs over, the one named last changes fastest.
Arguments:
- patches: bfloat16 [8, 2304, 768], P(None, ('ga', 'ha')), may hold values from -6 to 6
- cotangent: bfloat16 [8, 2304, 768], P(None, ('ga', 'ha')), may hold values from -6 to 6
- sides: int32 [8], replicated, may hold values from 36 to 48, as said below
- norm1_gain: bfloat16 [768], P('ha'), may hold values from 0.5 to 1.5
- norm1_bias: bfloat16 [768], P('ha'), may hold values from -1.75 to 1.75
- qkv_weight: bfloat16 [768, 2304], P('ha', 'ga'), may hold values from -0.21875 to 0.21875
- query_bias: bfloat16 [768], P('ha'), may hold values from -1.75 to 1.75
- value_bias: bfloat16 [768], P('ha'), may hold values from -1.75 to 1.75
- proj_weight: bfloat16 [768, 768], P('ha', 'ga'), may hold values from -1.25 to 1.25
- proj_bias: bfloat16 [768], P('ha'), may hold values from -1.75 to 1.75
- norm2_gain: bfloat16 [768], P('ha'), may hold values from 0.5 to 1.5
- norm2_bias: bfloat16 [768], P('ha'), may hold values from -1.75 to 1.75
- fc1_weight: bfloat16 [768, 3072], P('ha', 'ga'), may hold values from -0.21875 to 0.21875
- fc1_bias: bfloat16 [3072], P('ha'), may hold values from -1.75 to 1.75
- fc2_weight: bfloat16 [3072, 768], P('ha', 'ga'), may hold values from -0.109375 to 0.109375
- fc2_bias: bfloat16 [768], P('ha'), may hold values from -1.75 to 1.75
- rel_height: bfloat16 [95, 64], replicated, may hold values from -0.875 to 0.875
- rel_width: bfloat16 [95, 64], replicated, may hold values from -0.875 to 0.875
Outputs:
- block_out: bfloat16 [8, 2304, 768], P(None, ('ga', 'ha'))
- input_grad: bfloat16 [8, 2304, 768], P(None, ('ga', 'ha'))
- norm1_gain_grad: float32 [768], P('ha')
- norm1_bias_grad: float32 [768], P('ha')
- qkv_weight_grad: float32 [768, 2304], P('ha', 'ga')
- query_bias_grad: float32 [768], P('ha')
- value_bias_grad: float32 [768], P('ha')
- proj_weight_grad: float32 [768, 768], P('ha', 'ga')
- proj_bias_grad: float32 [768], P('ha')
- norm2_gain_grad: float32 [768], P('ha')
- norm2_bias_grad: float32 [768], P('ha')
- fc1_weight_grad: float32 [768, 3072], P('ha', 'ga')
- fc1_bias_grad: float32 [3072], P('ha')
- fc2_weight_grad: float32 [3072, 768], P('ha', 'ga')
- fc2_bias_grad: float32 [768], P('ha')
- rel_height_grad: float32 [95, 64], replicated
- rel_width_grad: float32 [95, 64], replicated
The draws below stay inside these ranges and needn't reach their ends.
Inputs may be any that keep to these rules, and one draw needn't show every extreme that they name: Image i fills the top-left sides[i] x sides[i] patches of its 48 x 48 grid; every entry is 36 or 48, and both values occur in every draw.
All inputs are finite; a program needn't handle non-finite values.
Results may differ from the reference program's by a relative error of at most 0.02.
Values may be sent and summed in bfloat16 or wider, within the bound.
No kernel may reach another device: no remote copies, remote signals or barrier semaphores. Data moves between devices by JAX's collectives and lax.ppermute only.
A program may use at most 192 MiB of HBM per device.

```python
import jax
import jax.numpy as jnp
from jax import lax

D = 768
HEADS = 12
HD = 64
FF = 3072
SMAX = 48
IMAGES = 8
CAP = 2304


def draw_sides(key, part):
    choose_big = jax.random.randint(key, (IMAGES,), 0, 2)
    big_slot = jax.random.randint(jax.random.fold_in(key, 11), (), 0, IMAGES)
    offset_by = jax.random.randint(jax.random.fold_in(key, 12), (), 1, IMAGES)
    small_slot = (big_slot + offset_by) % IMAGES
    slot_index = jnp.arange(IMAGES)
    choose_big = jnp.where(slot_index == big_slot, 1, choose_big)
    choose_big = jnp.where(slot_index == small_slot, 0, choose_big)
    return (3 * SMAX // 4 + choose_big * (SMAX // 4)).astype(jnp.int32)


def shard_levels(key, dims, shards, smallest, largest):
    loudness, own = 1.0, jax.random.fold_in(key, 6)
    for dim, parts in shards:
        heights = jnp.exp(jax.random.uniform(jax.random.fold_in(own, dim), (parts,), jnp.float32, smallest / len(shards), largest / len(shards)))
        loudness = loudness * jnp.repeat(heights, dims[dim] // parts).reshape([-1 if axis == dim else 1 for axis in range(len(dims))])
    return loudness


def gaussian(rng, extent, scale, most, pieces=(), kind=jnp.bfloat16):
    level = shard_levels(rng, extent, pieces, -0.22, 0.18) if pieces else 1.0
    drawn = jax.random.normal(rng, extent, jnp.float32) * scale * level
    return jnp.minimum(jnp.maximum(drawn, -most), most).astype(kind)


def setup_inputs(seed: int = 0) -> dict:
    key_list = jax.random.split(jax.random.key(seed), 19)
    patches = gaussian(key_list[0], (IMAGES, CAP, D), 1.0, 6.0, ((1, 32),))
    cotangent = gaussian(key_list[1], (IMAGES, CAP, D), 1.0, 6.0, ((1, 32),))
    sides = draw_sides(jax.random.fold_in(key_list[18], 71), 0)
    norm1_gain = jnp.clip(1.0 + 0.1 * jax.random.normal(key_list[3], (D,), jnp.float32), 0.5, 1.5).astype(jnp.bfloat16)
    norm1_bias = gaussian(key_list[4], (D,), 0.3, 1.75, ((0, 4),))
    qkv_weight = gaussian(key_list[5], (D, 3 * D), D ** -0.5, 0.21875, ((0, 4), (1, 8)))
    query_bias = gaussian(key_list[6], (D,), 0.3, 1.75, ((0, 4),))
    value_bias = gaussian(key_list[7], (D,), 0.3, 1.75, ((0, 4),))
    proj_weight = gaussian(key_list[8], (D, D), (D * 64 // CAP) ** -0.5, 1.25, ((0, 4), (1, 8)))
    proj_bias = gaussian(key_list[9], (D,), 0.3, 1.75, ((0, 4),))
    norm2_gain = jnp.clip(1.0 + 0.1 * jax.random.normal(key_list[10], (D,), jnp.float32), 0.5, 1.5).astype(jnp.bfloat16)
    norm2_bias = gaussian(key_list[11], (D,), 0.3, 1.75, ((0, 4),))
    fc1_weight = gaussian(key_list[12], (D, FF), D ** -0.5, 0.21875, ((0, 4), (1, 8)))
    fc1_bias = gaussian(key_list[13], (FF,), 0.3, 1.75, ((0, 4),))
    fc2_weight = gaussian(key_list[14], (FF, D), FF ** -0.5, 0.109375, ((0, 4), (1, 8)))
    fc2_bias = gaussian(key_list[15], (D,), 0.3, 1.75, ((0, 4),))
    rel_height = gaussian(key_list[16], (2 * SMAX - 1, HD), 0.15, 0.875)
    rel_width = gaussian(key_list[17], (2 * SMAX - 1, HD), 0.15, 0.875)
    return {"patches": patches, "cotangent": cotangent, "sides": sides, "norm1_gain": norm1_gain, "norm1_bias": norm1_bias, "qkv_weight": qkv_weight, "query_bias": query_bias, "value_bias": value_bias, "proj_weight": proj_weight, "proj_bias": proj_bias, "norm2_gain": norm2_gain, "norm2_bias": norm2_bias, "fc1_weight": fc1_weight, "fc1_bias": fc1_bias, "fc2_weight": fc2_weight, "fc2_bias": fc2_bias, "rel_height": rel_height, "rel_width": rel_width}


exact_mode = lax.Precision.HIGHEST

@jax.custom_vjp
def low(v):
    return lax.optimization_barrier(v.astype(jnp.bfloat16)).astype(jnp.float32)

@jax.custom_vjp
def low_back(v):
    return v

def low_keep(v):
    return (low(v), None)

def low_pass(kept, grad):
    return (grad,)

def back_keep(v):
    return (v, None)

def back_low(kept, grad):
    return (low(grad),)
low.defvjp(low_keep, low_pass)
low_back.defvjp(back_keep, back_low)

def layer_norm(values, gain, shift):
    center = values - lax.optimization_barrier(jnp.mean(values, axis=-1, keepdims=True))
    spread = lax.optimization_barrier(jnp.mean(center * center, axis=-1, keepdims=True))
    return center * lax.rsqrt(spread + 1e-06) * gain + shift

def interp_matrix(img_side):
    coord = jnp.arange(SMAX, dtype=jnp.int32)
    length_in = 2 * SMAX - 1
    length_out = 2 * img_side - 1
    offset = jnp.clip(coord[:, None] - coord[None, :] + img_side - 1, 0, length_out - 1)
    numer = jnp.maximum((2 * offset + 1) * length_in - length_out, 0)
    lower = numer // (2 * length_out)
    weight_hi = (numer - lower * 2 * length_out).astype(jnp.float32) / (2 * length_out).astype(jnp.float32)
    upper = jnp.minimum(lower + 1, length_in - 1)
    target = jnp.arange(length_in, dtype=jnp.int32)
    lower_hot = (target == lower[..., None]).astype(jnp.float32)
    upper_hot = (target == upper[..., None]).astype(jnp.float32)
    return (1.0 - weight_hi)[..., None] * lower_hot + weight_hi[..., None] * upper_hot

def attend(queries, key_rows, value_rows, table_h, table_w, key_valid):
    row_count = SMAX // 4
    block_count = SMAX // row_count
    score_scale = HD ** (-0.5)
    q_blocks = queries.reshape(block_count, row_count, SMAX, HEADS, HD)
    h_blocks = table_h.reshape(block_count, row_count, SMAX, HD)

    def one_block(inputs):
        q_rows, h_rows = inputs
        dot_part = jnp.einsum('rwhd,khd->hrwk', q_rows, key_rows, precision=exact_mode) * score_scale
        rel_h = jnp.einsum('rwhd,rkd->hrwk', q_rows, h_rows, precision=exact_mode)
        rel_w = jnp.einsum('rwhd,wkd->hrwk', q_rows, table_w, precision=exact_mode)
        combined = dot_part.reshape(HEADS, row_count, SMAX, SMAX, SMAX) + rel_h[..., None] + rel_w[..., None, :]
        combined = jnp.where(key_valid, combined.reshape(HEADS, row_count, SMAX, CAP), -1e+30)
        combined = low_back(combined)
        probs = low(jax.nn.softmax(combined, axis=-1))
        return jnp.einsum('hrwk,khd->rwhd', probs, value_rows, precision=exact_mode)
    result = lax.map(jax.checkpoint(one_block), (q_blocks, h_blocks))
    return result.reshape(CAP, HEADS * HD)

def forward(image_in, img_side, weight_set):
    norm1_gain, norm1_bias, qkv_weight, query_bias, value_bias, proj_weight, proj_bias, norm2_gain, norm2_bias, fc1_weight, fc1_bias, fc2_weight, fc2_bias, rel_height, rel_width = weight_set
    index_all = jnp.arange(CAP, dtype=jnp.int32)
    valid = (index_all // SMAX < img_side) & (index_all % SMAX < img_side)
    tok_mask = valid.astype(jnp.float32)[:, None]
    matrix = interp_matrix(img_side)
    table_h = low(jnp.einsum('qkj,jd->qkd', matrix, rel_height, precision=exact_mode))
    table_w = low(jnp.einsum('qkj,jd->qkd', matrix, rel_width, precision=exact_mode))
    normed = low(layer_norm(image_in, norm1_gain, norm1_bias))
    bias_all = jnp.concatenate([query_bias, jnp.zeros_like(query_bias), value_bias])
    mixed = jnp.dot(normed, qkv_weight, precision=exact_mode) + bias_all
    mixed = low_back(low(mixed))
    queries = mixed[:, :D].reshape(CAP, HEADS, HD)
    key_rows = mixed[:, D:2 * D].reshape(CAP, HEADS, HD)
    value_rows = mixed[:, 2 * D:].reshape(CAP, HEADS, HD)
    attended = low_back(low(attend(queries, key_rows, value_rows, table_h, table_w, valid)))
    branch = low_back(jnp.dot(attended, proj_weight, precision=exact_mode) + proj_bias)
    middle = image_in + tok_mask * branch
    normed2 = low(layer_norm(middle, norm2_gain, norm2_bias))
    hidden = low_back(jnp.dot(normed2, fc1_weight, precision=exact_mode) + fc1_bias)
    activated = low(jax.nn.gelu(hidden, approximate=False))
    return middle + tok_mask * (jnp.dot(activated, fc2_weight, precision=exact_mode) + fc2_bias)

def reference(patches, cotangent, sides, norm1_gain, norm1_bias, qkv_weight, query_bias, value_bias, proj_weight, proj_bias, norm2_gain, norm2_bias, fc1_weight, fc1_bias, fc2_weight, fc2_bias, rel_height, rel_width):
    weight_set = jax.tree.map(lambda weight: weight.astype(jnp.float32), (norm1_gain, norm1_bias, qkv_weight, query_bias, value_bias, proj_weight, proj_bias, norm2_gain, norm2_bias, fc1_weight, fc1_bias, fc2_weight, fc2_bias, rel_height, rel_width))
    zero_grads = jax.tree.map(jnp.zeros_like, weight_set)

    def per_image(carry, inputs):
        image_in, image_cot, img_side = inputs
        output, pullback = jax.vjp(lambda image_value, weights_now: forward(image_value, img_side, weights_now), image_in.astype(jnp.float32), weight_set)
        grad_in, grad_weights = pullback(image_cot.astype(jnp.float32))
        carry = jax.tree.map(jnp.add, carry, grad_weights)
        return (carry, (output.astype(jnp.bfloat16), grad_in.astype(jnp.bfloat16)))
    totals, (outputs, grads_in) = lax.scan(per_image, zero_grads, (patches, cotangent, sides))
    return (outputs, grads_in, totals[0], totals[1], totals[2], totals[3], totals[4], totals[5], totals[6], totals[7], totals[8], totals[9], totals[10], totals[11], totals[12], totals[13], totals[14])
```

```python
from functools import partial

import jax
import jax.numpy as jnp
from jax import lax
from jax.experimental import pallas as pl
from jax.experimental.pallas import tpu as pltpu
from jax.sharding import PartitionSpec as P

HEADS = 12
HD = 64
SMAX = 48
BOTH = ("ga", "ha")


exact_mode = lax.Precision.HIGHEST


TBLK = 256
UBLK = 768

NT = (((1,), (1,)), ((), ()))


def mm(left, right):
    return jnp.dot(left, right, preferred_element_type=jnp.float32)


def mm_nt(left, right):
    return lax.dot_general(left, right, NT, preferred_element_type=jnp.float32)


def forward_kernel(q_ref, k_ref, v_ref, out_ref, lse_ref):
    heads = q_ref.shape[0]
    dim = 64
    outs = []
    for h in range(heads):
        scores = mm_nt(k_ref[h], q_ref[h])
        top = jnp.max(scores, axis=0, keepdims=True)
        expo = jnp.exp(scores - top).astype(jnp.bfloat16)
        mixed = mm(v_ref[h], expo)
        total = mixed[dim : dim + 1]
        outs.append((mixed[:dim] / total).T.astype(jnp.bfloat16))
        lse_ref[h] = top + jnp.log(total)
    out_ref[...] = jnp.concatenate(outs, axis=1)


def attend_forward(q_aug, k_aug, v_aug):
    heads, tokens, depth = q_aug.shape
    dim = 64
    return pl.pallas_call(
        forward_kernel,
        grid=(tokens // TBLK,),
        in_specs=[
            pl.BlockSpec((heads, TBLK, depth), lambda t: (0, t, 0)),
            pl.BlockSpec((heads, tokens, depth), lambda t: (0, 0, 0)),
            pl.BlockSpec((heads, v_aug.shape[1], tokens), lambda t: (0, 0, 0)),
        ],
        out_specs=[
            pl.BlockSpec((TBLK, heads * dim), lambda t: (t, 0)),
            pl.BlockSpec((heads, 1, TBLK), lambda t: (0, 0, t)),
        ],
        out_shape=[
            jax.ShapeDtypeStruct((tokens, heads * dim), jnp.bfloat16),
            jax.ShapeDtypeStruct((heads, 1, tokens), jnp.float32),
        ],
        name="attend_forward",
        compiler_params=pltpu.CompilerParams(dimension_semantics=("arbitrary",)),
    )(q_aug, k_aug, v_aug)


def backward_kernel(
    q_ref, g_ref, lse_ref, delta_ref, k_ref, v_ref, kt_ref, dq_ref, line_ref, dkv_ref
):
    heads, tokens, depth = k_ref.shape
    dim = 64
    blk = q_ref.shape[1]

    @pl.when(pl.program_id(0) == 0)
    def _():
        dkv_ref[...] = jnp.zeros_like(dkv_ref)

    for h in range(heads):
        q_here = q_ref[h]
        g_here = g_ref[h]
        zero = jnp.zeros((blk, dim), jnp.bfloat16)
        g_wide = jnp.concatenate([g_here, zero], axis=1)
        q_wide = jnp.concatenate([zero, q_here[:, :dim]], axis=1)
        lse = lse_ref[h]
        delta = delta_ref[h]
        total = None
        for c in range(tokens // UBLK):
            span = pl.ds(c * UBLK, UBLK)
            scores = mm_nt(k_ref[h, span, :], q_here)
            probs = jnp.exp(scores - lse)
            pgrad = mm_nt(v_ref[h, span, :], g_here)
            sgrad = (probs * (pgrad - delta)).astype(jnp.bfloat16)
            dkv_ref[h, span, :] += mm(probs.astype(jnp.bfloat16), g_wide) + mm(sgrad, q_wide)
            part = mm(kt_ref[h, :, span], sgrad)
            total = part if total is None else total + part
        dq_ref[h] = total[:dim].T
        line_ref[h] = total[dim:].T.astype(jnp.bfloat16)


def attend_backward(q_aug, grads, lse, delta, k_aug, values, k_turn):
    heads, tokens, depth = q_aug.shape
    dim = 64
    lines = k_turn.shape[1] - dim
    return pl.pallas_call(
        backward_kernel,
        grid=(tokens // TBLK,),
        in_specs=[
            pl.BlockSpec((heads, TBLK, depth), lambda t: (0, t, 0)),
            pl.BlockSpec((heads, TBLK, dim), lambda t: (0, t, 0)),
            pl.BlockSpec((heads, 1, TBLK), lambda t: (0, 0, t)),
            pl.BlockSpec((heads, 1, TBLK), lambda t: (0, 0, t)),
            pl.BlockSpec((heads, tokens, depth), lambda t: (0, 0, 0)),
            pl.BlockSpec((heads, tokens, dim), lambda t: (0, 0, 0)),
            pl.BlockSpec((heads, dim + lines, tokens), lambda t: (0, 0, 0)),
        ],
        out_specs=[
            pl.BlockSpec((heads, TBLK, dim), lambda t: (0, t, 0)),
            pl.BlockSpec((heads, TBLK, lines), lambda t: (0, t, 0)),
            pl.BlockSpec((heads, tokens, 2 * dim), lambda t: (0, 0, 0)),
        ],
        out_shape=[
            jax.ShapeDtypeStruct((heads, tokens, dim), jnp.float32),
            jax.ShapeDtypeStruct((heads, tokens, lines), jnp.bfloat16),
            jax.ShapeDtypeStruct((heads, tokens, 2 * dim), jnp.float32),
        ],
        name="attend_backward",
        compiler_params=pltpu.CompilerParams(dimension_semantics=("arbitrary",)),
    )(q_aug, grads, lse, delta, k_aug, values, k_turn)


def layer_norm(values, gain, shift):
    center = values - jnp.mean(values, axis=-1, keepdims=True)
    spread = jnp.mean(center * center, axis=-1, keepdims=True)
    return center * lax.rsqrt(spread + 1e-06) * gain + shift


def interp_matrix(img_side):
    coord = jnp.arange(SMAX, dtype=jnp.int32)
    length_in = 2 * SMAX - 1
    length_out = 2 * img_side - 1
    offset = jnp.clip(coord[:, None] - coord[None, :] + img_side - 1, 0, length_out - 1)
    numer = jnp.maximum((2 * offset + 1) * length_in - length_out, 0)
    lower = numer // (2 * length_out)
    weight_hi = (numer - lower * 2 * length_out).astype(jnp.float32) / (2 * length_out).astype(
        jnp.float32
    )
    upper = jnp.minimum(lower + 1, length_in - 1)
    target = jnp.arange(length_in, dtype=jnp.int32)
    lower_hot = (target == lower[..., None]).astype(jnp.float32)
    upper_hot = (target == upper[..., None]).astype(jnp.float32)
    return (1.0 - weight_hi)[..., None] * lower_hot + weight_hi[..., None] * upper_hot


def contract_rows(left, right):
    return lax.dot_general(
        left, right, (((0,), (0,)), ((), ())), preferred_element_type=jnp.float32
    )


def contract_cols(left, right):
    return lax.dot_general(
        left, right, (((1,), (1,)), ((), ())), preferred_element_type=jnp.float32
    )


def exchange(values, axis):
    return lax.all_to_all(values, axis, split_axis=0, concat_axis=0, tiled=True)


def spread(values, axis):
    count = lax.axis_size(axis)
    return exchange(jnp.broadcast_to(values, (count,) + values.shape), axis)


def pack_up(piece):
    rows, width = piece.shape[-2:]
    lead = piece.shape[:-2]
    fold = 4 * rows // width
    cut = piece.reshape(lead + (fold, rows // fold, width))
    return jnp.swapaxes(cut, -3, -2).reshape(lead + (rows // fold, fold * width))


def unpack_up(packed, rows, width):
    fold = packed.shape[-1] // width
    lead = packed.shape[:-2]
    cut = packed.reshape(lead + (rows // fold, fold, width))
    return jnp.swapaxes(cut, -3, -2).reshape(lead + (rows, width))


def local(
    patches,
    cotangent,
    sides,
    norm1_gain,
    norm1_bias,
    qkv_weight,
    query_bias,
    value_bias,
    proj_weight,
    proj_bias,
    norm2_gain,
    norm2_bias,
    fc1_weight,
    fc1_bias,
    fc2_weight,
    fc2_bias,
    rel_height,
    rel_width,
):
    group_count = lax.axis_size("ga")
    head_groups = lax.axis_size("ha")
    group_index = lax.axis_index("ga")
    head_index = lax.axis_index("ha")
    device_count = group_count * head_groups
    block_len = patches.shape[1]
    model_width = patches.shape[2]
    hidden_width = fc1_bias.shape[0] * head_groups
    local_tokens = group_count * block_len
    group_width = model_width // head_groups
    group_heads = HEADS // head_groups
    cap_tokens = SMAX * SMAX
    f32 = jnp.float32
    bf16 = jnp.bfloat16

    triple_rows = lax.all_gather(qkv_weight, "ga", axis=1, tiled=True)
    triple_cut = triple_rows.reshape(group_width, 3, head_groups, group_width).transpose(2, 0, 1, 3)
    triple_own = exchange(
        triple_cut.reshape(head_groups, group_width, 3 * group_width), "ha"
    ).reshape(model_width, 3 * group_width)

    up_rows, up_cols = fc1_weight.shape
    out_cols = fc2_weight.shape[1]
    packed = jnp.concatenate(
        [
            pack_up(fc1_weight),
            fc2_weight.T,
            proj_weight.T.reshape(out_cols // head_groups, model_width),
        ],
        axis=0,
    )
    pack_rows = packed.shape[0]
    up_height = up_rows * up_cols // model_width

    vectors = jnp.concatenate(
        [norm1_gain, norm1_bias, proj_bias, norm2_gain, norm2_bias, fc2_bias, fc1_bias]
    )
    vectors_all = lax.all_gather(vectors, "ha", axis=0, tiled=False)
    wide = model_width // head_groups

    def vector_at(slot, width):
        return vectors_all[:, slot * wide : slot * wide + width].reshape(-1)

    first_gain = vector_at(0, wide)
    first_shift = vector_at(1, wide)
    proj_shift = vector_at(2, wide)
    second_gain = vector_at(3, wide)
    second_shift = vector_at(4, wide)
    down_shift = vector_at(5, wide)
    up_shift = vector_at(6, 4 * wide)

    tokens_in = lax.all_to_all(patches, "ga", split_axis=0, concat_axis=1, tiled=True)[0]
    cot_in = lax.all_to_all(cotangent, "ga", split_axis=0, concat_axis=1, tiled=True)[0]
    tokens32 = tokens_in.astype(f32)
    cot32 = cot_in.astype(f32)
    slot_index = jnp.arange(local_tokens, dtype=jnp.int32)
    grid_index = (
        slot_index // block_len * head_groups + head_index
    ) * block_len + slot_index % block_len
    img_side = lax.dynamic_index_in_dim(sides, group_index, 0, keepdims=False)
    tok_mask = ((grid_index // SMAX < img_side) & (grid_index % SMAX < img_side)).astype(f32)[
        :, None
    ]
    all_index = jnp.arange(cap_tokens, dtype=jnp.int32)[:, None]
    line_index = jnp.arange(2 * SMAX, dtype=jnp.int32)[None, :]
    expand = jnp.where(
        line_index < SMAX,
        all_index // SMAX == line_index,
        all_index % SMAX == line_index - SMAX,
    ).astype(bf16)
    line_valid = line_index[0] % SMAX < img_side
    matrix = interp_matrix(img_side)
    table_h = jnp.einsum(
        "qkj,jd->qkd", matrix, rel_height.astype(f32), precision=exact_mode
    ).astype(bf16)
    table_w = jnp.einsum("qkj,jd->qkd", matrix, rel_width.astype(f32), precision=exact_mode).astype(
        bf16
    )

    normed = layer_norm(tokens32, first_gain.astype(f32), first_shift.astype(f32)).astype(bf16)
    normed_all = (
        spread(normed, "ha")
        .reshape(head_groups, group_count, block_len, model_width)
        .transpose(1, 0, 2, 3)
        .reshape(cap_tokens, model_width)
    )
    bias_own = jnp.concatenate([query_bias, jnp.zeros_like(query_bias), value_bias]).astype(f32)
    mixed = (jnp.dot(normed_all, triple_own, preferred_element_type=f32) + bias_own).astype(bf16)
    by_head = mixed.reshape(cap_tokens, 3, group_heads, HD).transpose(1, 2, 0, 3)
    q_all, key_all, value_all = by_head[0], by_head[1], by_head[2]

    q_grid = q_all.reshape(group_heads, SMAX, SMAX, HD)
    rel_h = jnp.einsum("hrwd,rkd->hrwk", q_grid, table_h, preferred_element_type=f32)
    rel_w = jnp.einsum("hrwd,wkd->hrwk", q_grid, table_w, preferred_element_type=f32)
    rel_both = jnp.concatenate([rel_h, rel_w], axis=-1).reshape(
        group_heads, cap_tokens, 2 * SMAX
    )
    rel_upper = lax.reduce_precision(rel_both, 8, 7)
    rel_lower = jnp.where(line_valid, rel_both - rel_upper, 0.0).astype(bf16)
    rel_upper = jnp.where(line_valid, rel_upper, -1e30).astype(bf16)
    q_aug = jnp.concatenate([q_all * jnp.asarray(HD**-0.5, bf16), rel_upper, rel_lower], axis=-1)
    expand_all = jnp.broadcast_to(expand, (group_heads,) + expand.shape)
    k_aug = jnp.concatenate([key_all, expand_all, expand_all], axis=-1)
    v_aug = jnp.concatenate(
        [
            value_all.swapaxes(1, 2),
            jnp.ones((group_heads, 1, cap_tokens), bf16),
            jnp.zeros((group_heads, 15, cap_tokens), bf16),
        ],
        axis=1,
    )
    k_turn = jnp.concatenate([key_all, expand_all], axis=-1).swapaxes(1, 2)
    att_heads, log_sums = attend_forward(q_aug, k_aug, v_aug)

    gathered = lax.all_gather(packed, BOTH, axis=0, tiled=False).reshape(
        group_count, head_groups, pack_rows, model_width
    )
    up_full = (
        unpack_up(gathered[:, :, :up_height], up_rows, up_cols)
        .transpose(1, 2, 0, 3)
        .reshape(model_width, hidden_width)
    )
    down_turn = (
        gathered[:, :, up_height : up_height + out_cols]
        .transpose(0, 2, 1, 3)
        .reshape(model_width, hidden_width)
    )
    proj_turn = (
        gathered[:, :, up_height + out_cols :]
        .reshape(group_count, head_groups, out_cols, group_width)
        .transpose(0, 2, 1, 3)
        .reshape(model_width, model_width)
    )

    att_back = lax.all_to_all(
        att_heads.reshape(group_count, head_groups, block_len, 1, group_width),
        "ha",
        split_axis=1,
        concat_axis=3,
        tiled=True,
    )
    att_tok = att_back.reshape(local_tokens, model_width)
    branch = contract_cols(att_tok, proj_turn) + proj_shift.astype(f32)
    middle = tokens32 + tok_mask * branch
    normed2 = layer_norm(middle, second_gain.astype(f32), second_shift.astype(f32)).astype(bf16)
    hidden = jnp.dot(normed2, up_full, preferred_element_type=f32) + up_shift.astype(f32)
    activated = jax.nn.gelu(hidden, approximate=False).astype(bf16)
    block_out = (
        middle + tok_mask * (contract_cols(activated, down_turn) + down_shift.astype(f32))
    ).astype(bf16)
    out_back = exchange(block_out.reshape(group_count, block_len, model_width), "ga")

    masked_cot = tok_mask * cot32
    down_in = masked_cot.astype(bf16)
    down_grad = contract_rows(down_in, activated).astype(bf16)
    down_bias_grad = jnp.sum(masked_cot, axis=0)
    act_grad = jnp.dot(down_in, down_turn, preferred_element_type=f32)
    gelu_value, gelu_pull = jax.vjp(partial(jax.nn.gelu, approximate=False), hidden)
    hidden_grad = gelu_pull(act_grad)[0].astype(bf16)
    up_grad = contract_rows(normed2, hidden_grad).astype(bf16)
    up_bias_grad = jnp.sum(hidden_grad.astype(f32), axis=0)
    norm2_in = contract_cols(hidden_grad, up_full)
    norm2_value, norm2_pull = jax.vjp(
        layer_norm, middle, second_gain.astype(f32), second_shift.astype(f32)
    )
    mid_grad, second_gain_grad, second_shift_grad = norm2_pull(norm2_in)
    mid_total = cot32 + mid_grad
    branch_grad = (tok_mask * mid_total).astype(bf16)
    proj_grad = contract_rows(branch_grad, att_tok).astype(bf16)
    proj_bias_grad = jnp.sum(branch_grad.astype(f32), axis=0)
    att_grad_tok = jnp.dot(branch_grad, proj_turn, preferred_element_type=f32).astype(bf16)
    att_grad = lax.all_to_all(
        att_grad_tok.reshape(group_count, 1, block_len, head_groups, group_width),
        "ha",
        split_axis=3,
        concat_axis=1,
        tiled=True,
    ).reshape(cap_tokens, group_width)

    grads_packed = jnp.concatenate(
        [
            pack_up(
                up_grad.reshape(head_groups, up_rows, group_count, up_cols).transpose(2, 0, 1, 3)
            ),
            down_grad.reshape(group_count, out_cols, head_groups, model_width).transpose(
                0, 2, 1, 3
            ),
            proj_grad.reshape(group_count, out_cols, head_groups, group_width)
            .transpose(0, 2, 1, 3)
            .reshape(group_count, head_groups, out_cols // head_groups, model_width),
        ],
        axis=2,
    ).reshape(device_count * pack_rows, model_width)
    grads_own = lax.psum_scatter(grads_packed, BOTH, scatter_dimension=0, tiled=True)
    up_own = unpack_up(grads_own[:up_height], up_rows, up_cols).astype(f32)
    down_own = grads_own[up_height : up_height + out_cols].T.astype(f32)
    proj_own = grads_own[up_height + out_cols :].reshape(out_cols, group_width).T.astype(f32)

    def reduce_vectors(vectors_in):
        stacked = jnp.concatenate(
            [
                vector.reshape(head_groups, group_count, -1)
                .transpose(1, 0, 2)
                .reshape(device_count, -1)
                for vector in vectors_in
            ],
            axis=1,
        )
        part = jnp.sum(exchange(stacked[:, None], BOTH), axis=0)
        own = spread(part, "ga")[:, 0]
        result = []
        at = 0
        for vector in vectors_in:
            size = vector.shape[0] // device_count
            result.append(own[:, at : at + size].reshape(-1))
            at += size
        return result

    early = reduce_vectors(
        [proj_bias_grad, second_gain_grad, second_shift_grad, down_bias_grad, up_bias_grad]
    )

    grad_heads = att_grad.reshape(cap_tokens, group_heads, HD)
    delta = (
        jnp.sum(
            grad_heads.astype(f32) * att_heads.reshape(cap_tokens, group_heads, HD).astype(f32),
            axis=-1,
        )
        .transpose(1, 0)
        .reshape(group_heads, 1, cap_tokens)
    )
    query_part, line_sums, dkv = attend_backward(
        q_aug, grad_heads.transpose(1, 0, 2), log_sums, delta, k_aug, value_all, k_turn
    )
    lines = line_sums.reshape(group_heads, SMAX, SMAX, 2 * SMAX)
    height_grad = lines[..., :SMAX]
    width_grad = lines[..., SMAX:]
    query_grad = (
        HD**-0.5 * query_part.reshape(group_heads, SMAX, SMAX, HD)
        + jnp.einsum("hrwj,rjd->hrwd", height_grad, table_h, preferred_element_type=f32)
        + jnp.einsum("hrwj,wjd->hrwd", width_grad, table_w, preferred_element_type=f32)
    ).reshape(group_heads, cap_tokens, HD)
    h_table_grad = jnp.einsum("hrwj,hrwd->rjd", height_grad, q_grid, preferred_element_type=f32)
    w_table_grad = jnp.einsum("hrwj,hrwd->wjd", width_grad, q_grid, preferred_element_type=f32)
    mixed_grad = (
        jnp.stack([query_grad, dkv[..., HD:], dkv[..., :HD]])
        .astype(bf16)
        .transpose(2, 0, 1, 3)
        .reshape(cap_tokens, 3 * group_width)
    )
    norm1_part = contract_cols(mixed_grad, triple_own).astype(bf16)
    norm1_in = jnp.sum(
        exchange(
            norm1_part.reshape(group_count, head_groups, block_len, model_width)
            .transpose(1, 0, 2, 3)
            .reshape(head_groups, local_tokens, model_width),
            "ha",
        ).astype(f32),
        axis=0,
    )
    triple_part = contract_rows(normed_all, mixed_grad).astype(bf16)
    triple_rows_grad = (
        exchange(triple_part.reshape(head_groups, group_width, 3 * group_width), "ha")
        .reshape(head_groups, group_width, 3, group_width)
        .transpose(1, 2, 0, 3)
        .reshape(group_width, group_count, 3 * model_width // group_count)
        .transpose(1, 0, 2)
    )
    triple_grad = jnp.sum(exchange(triple_rows_grad, "ga").astype(f32), axis=0)
    mixed_float = mixed_grad.astype(f32)
    bias_part = jnp.concatenate(
        [
            jnp.sum(mixed_float[:, :group_width], axis=0),
            jnp.sum(mixed_float[:, 2 * group_width :], axis=0),
        ]
    )
    bias_sum = jnp.sum(spread(bias_part[None], "ga"), axis=0)[0]
    height_rel = jnp.einsum("qkj,qkd->jd", matrix, h_table_grad, precision=exact_mode)
    width_rel = jnp.einsum("qkj,qkd->jd", matrix, w_table_grad, precision=exact_mode)
    rel_flat = jnp.concatenate([height_rel, width_rel]).reshape(-1)
    rel_size = rel_flat.shape[0]
    chunk = -(-rel_size // (128 * device_count)) * 128
    rel_flat = jnp.pad(rel_flat, (0, chunk * device_count - rel_size))
    rel_part = jnp.sum(exchange(rel_flat.reshape(device_count, 1, chunk), BOTH), axis=0)
    rel_sum = spread(rel_part, BOTH).reshape(-1)[:rel_size].reshape(2, 2 * SMAX - 1, HD)

    norm1_value, norm1_pull = jax.vjp(
        layer_norm, tokens32, first_gain.astype(f32), first_shift.astype(f32)
    )
    in_grad, first_gain_grad, first_shift_grad = norm1_pull(norm1_in)
    input_grad = (mid_total + in_grad).astype(bf16)
    in_back = exchange(input_grad.reshape(group_count, block_len, model_width), "ga")
    late = reduce_vectors([first_gain_grad, first_shift_grad])
    return (
        out_back,
        in_back,
        late[0],
        late[1],
        triple_grad,
        bias_sum[:group_width],
        bias_sum[group_width:],
        proj_own,
        early[0],
        early[1],
        early[2],
        up_own,
        early[4],
        down_own,
        early[3],
        rel_sum[0],
        rel_sum[1],
    )


def solution(mesh):
    placed = (
        P(None, ("ga", "ha"), None),
        P(None, ("ga", "ha"), None),
        P(),
        P("ha"),
        P("ha"),
        P("ha", "ga"),
        P("ha"),
        P("ha"),
        P("ha", "ga"),
        P("ha"),
        P("ha"),
        P("ha"),
        P("ha", "ga"),
        P("ha"),
        P("ha", "ga"),
        P("ha"),
        P(),
        P(),
    )
    return jax.shard_map(
        local,
        mesh=mesh,
        in_specs=placed,
        out_specs=(
            P(None, ("ga", "ha"), None),
            P(None, ("ga", "ha"), None),
            P("ha"),
            P("ha"),
            P("ha", "ga"),
            P("ha"),
            P("ha"),
            P("ha", "ga"),
            P("ha"),
            P("ha"),
            P("ha"),
            P("ha", "ga"),
            P("ha"),
            P("ha", "ga"),
            P("ha"),
            P(),
            P(),
        ),
        check_vma=False,
    )
```

```python
from functools import partial

import jax
import jax.numpy as jnp
from jax import lax
from jax.experimental import pallas as pl
from jax.experimental.pallas import tpu as pltpu
from jax.sharding import PartitionSpec as P

HEADS = 12
HD = 64
SMAX = 48
BOTH = ("ga", "ha")


exact_mode = lax.Precision.HIGHEST


TBLK = 256
UBLK = 768

NT = (((1,), (1,)), ((), ()))


def mm(left, right):
    return jnp.dot(left, right, preferred_element_type=jnp.float32)


def mm_nt(left, right):
    return lax.dot_general(left, right, NT, preferred_element_type=jnp.float32)


def forward_kernel(q_ref, k_ref, v_ref, out_ref, lse_ref):
    heads = q_ref.shape[0]
    dim = 64
    outs = []
    for h in range(heads):
        scores = mm_nt(k_ref[h], q_ref[h])
        top = jnp.max(scores, axis=0, keepdims=True)
        expo = jnp.exp(scores - top).astype(jnp.bfloat16)
        mixed = mm(v_ref[h], expo)
        total = mixed[dim : dim + 1]
        outs.append((mixed[:dim] / total).T.astype(jnp.bfloat16))
        lse_ref[h] = top + jnp.log(total)
    out_ref[...] = jnp.concatenate(outs, axis=1)


def attend_forward(q_aug, k_aug, v_aug):
    heads, tokens, depth = q_aug.shape
    dim = 64
    return pl.pallas_call(
        forward_kernel,
        grid=(tokens // TBLK,),
        in_specs=[
            pl.BlockSpec((heads, TBLK, depth), lambda t: (0, t, 0)),
            pl.BlockSpec((heads, tokens, depth), lambda t: (0, 0, 0)),
            pl.BlockSpec((heads, v_aug.shape[1], tokens), lambda t: (0, 0, 0)),
        ],
        out_specs=[
            pl.BlockSpec((TBLK, heads * dim), lambda t: (t, 0)),
            pl.BlockSpec((heads, 1, TBLK), lambda t: (0, 0, t)),
        ],
        out_shape=[
            jax.ShapeDtypeStruct((tokens, heads * dim), jnp.bfloat16),
            jax.ShapeDtypeStruct((heads, 1, tokens), jnp.float32),
        ],
        name="attend_forward",
        compiler_params=pltpu.CompilerParams(dimension_semantics=("arbitrary",)),
    )(q_aug, k_aug, v_aug)


def backward_kernel(
    q_ref, g_ref, lse_ref, delta_ref, k_ref, v_ref, kt_ref, dq_ref, line_ref, out_ref, dkv_ref
):
    heads, tokens, depth = k_ref.shape
    dim = 64
    blk = q_ref.shape[1]

    @pl.when(pl.program_id(0) == 0)
    def _():
        dkv_ref[...] = jnp.zeros_like(dkv_ref)

    for h in range(heads):
        q_here = q_ref[h]
        g_here = g_ref[h]
        zero = jnp.zeros((blk, dim), jnp.bfloat16)
        g_wide = jnp.concatenate([g_here, zero], axis=1)
        q_wide = jnp.concatenate([zero, q_here[:, :dim]], axis=1)
        lse = lse_ref[h]
        delta = delta_ref[h]
        total = None
        for c in range(tokens // UBLK):
            span = pl.ds(c * UBLK, UBLK)
            scores = mm_nt(k_ref[h, span, :], q_here)
            probs = jnp.exp(scores - lse)
            pgrad = mm_nt(v_ref[h, span, :], g_here)
            sgrad = (probs * (pgrad - delta)).astype(jnp.bfloat16)
            dkv_ref[h, span, :] += mm(probs.astype(jnp.bfloat16), g_wide) + mm(sgrad, q_wide)
            part = mm(kt_ref[h, :, span], sgrad)
            total = part if total is None else total + part
        dq_ref[h] = total[:dim].T
        line_ref[h] = total[dim:].T.astype(jnp.bfloat16)

    @pl.when(pl.program_id(0) == pl.num_programs(0) - 1)
    def _():
        keys = [dkv_ref[h, :, dim:] for h in range(heads)]
        values = [dkv_ref[h, :, :dim] for h in range(heads)]
        out_ref[...] = jnp.concatenate(keys + values, axis=1).astype(jnp.bfloat16)


def attend_backward(q_aug, grads, lse, delta, k_aug, values, k_turn):
    heads, tokens, depth = q_aug.shape
    dim = 64
    lines = k_turn.shape[1] - dim
    return pl.pallas_call(
        backward_kernel,
        grid=(tokens // TBLK,),
        in_specs=[
            pl.BlockSpec((heads, TBLK, depth), lambda t: (0, t, 0)),
            pl.BlockSpec((heads, TBLK, dim), lambda t: (0, t, 0)),
            pl.BlockSpec((heads, 1, TBLK), lambda t: (0, 0, t)),
            pl.BlockSpec((heads, 1, TBLK), lambda t: (0, 0, t)),
            pl.BlockSpec((heads, tokens, depth), lambda t: (0, 0, 0)),
            pl.BlockSpec((heads, tokens, dim), lambda t: (0, 0, 0)),
            pl.BlockSpec((heads, dim + lines, tokens), lambda t: (0, 0, 0)),
        ],
        out_specs=[
            pl.BlockSpec((heads, TBLK, dim), lambda t: (0, t, 0)),
            pl.BlockSpec((heads, TBLK, lines), lambda t: (0, t, 0)),
            pl.BlockSpec((tokens, 2 * heads * dim), lambda t: (0, 0)),
        ],
        scratch_shapes=[pltpu.VMEM((heads, tokens, 2 * dim), jnp.float32)],
        out_shape=[
            jax.ShapeDtypeStruct((heads, tokens, dim), jnp.float32),
            jax.ShapeDtypeStruct((heads, tokens, lines), jnp.bfloat16),
            jax.ShapeDtypeStruct((tokens, 2 * heads * dim), jnp.bfloat16),
        ],
        name="attend_backward",
        compiler_params=pltpu.CompilerParams(dimension_semantics=("arbitrary",)),
    )(q_aug, grads, lse, delta, k_aug, values, k_turn)


def layer_norm(values, gain, shift):
    center = values - jnp.mean(values, axis=-1, keepdims=True)
    spread = jnp.mean(center * center, axis=-1, keepdims=True)
    return center * lax.rsqrt(spread + 1e-06) * gain + shift


def interp_matrix(img_side):
    coord = jnp.arange(SMAX, dtype=jnp.int32)
    length_in = 2 * SMAX - 1
    length_out = 2 * img_side - 1
    offset = jnp.clip(coord[:, None] - coord[None, :] + img_side - 1, 0, length_out - 1)
    numer = jnp.maximum((2 * offset + 1) * length_in - length_out, 0)
    lower = numer // (2 * length_out)
    weight_hi = (numer - lower * 2 * length_out).astype(jnp.float32) / (2 * length_out).astype(
        jnp.float32
    )
    upper = jnp.minimum(lower + 1, length_in - 1)
    target = jnp.arange(length_in, dtype=jnp.int32)
    lower_hot = (target == lower[..., None]).astype(jnp.float32)
    upper_hot = (target == upper[..., None]).astype(jnp.float32)
    return (1.0 - weight_hi)[..., None] * lower_hot + weight_hi[..., None] * upper_hot


def contract_rows(left, right):
    return lax.dot_general(
        left, right, (((0,), (0,)), ((), ())), preferred_element_type=jnp.float32
    )


def contract_cols(left, right):
    return lax.dot_general(
        left, right, (((1,), (1,)), ((), ())), preferred_element_type=jnp.float32
    )


def exchange(values, axis):
    return lax.all_to_all(values, axis, split_axis=0, concat_axis=0, tiled=True)


def spread(values, axis):
    count = lax.axis_size(axis)
    return exchange(jnp.broadcast_to(values, (count,) + values.shape), axis)


def swap(values, step):
    pairs = [(i, i ^ step) for i in range(lax.axis_size("ha"))]
    return lax.ppermute(values, "ha", pairs)


def gather_heads(values):
    me = lax.axis_index("ha")
    far = swap(values, 2)
    near = swap(values, 1)
    corner = swap(far, 1)
    blocks = jnp.stack([values, near, far, corner])
    return [lax.dynamic_index_in_dim(blocks, jnp.bitwise_xor(me, i), 0, False) for i in range(4)]


def scatter_heads(parts):
    me = lax.axis_index("ha")
    other = [lax.dynamic_index_in_dim(parts, jnp.bitwise_xor(me, i), 0, False) for i in range(4)]
    arrived = swap(jnp.stack([other[3], other[1]]), 1).astype(jnp.float32)
    far = (other[2].astype(jnp.float32) + arrived[0]).astype(jnp.bfloat16)
    near = other[0].astype(jnp.float32) + arrived[1]
    return near + swap(far, 2).astype(jnp.float32)


def pack_up(piece):
    rows, width = piece.shape[-2:]
    lead = piece.shape[:-2]
    fold = 4 * rows // width
    cut = piece.reshape(lead + (fold, rows // fold, width))
    return jnp.swapaxes(cut, -3, -2).reshape(lead + (rows // fold, fold * width))


def unpack_up(packed, rows, width):
    fold = packed.shape[-1] // width
    lead = packed.shape[:-2]
    cut = packed.reshape(lead + (rows // fold, fold, width))
    return jnp.swapaxes(cut, -3, -2).reshape(lead + (rows, width))


def local(
    patches,
    cotangent,
    sides,
    norm1_gain,
    norm1_bias,
    qkv_weight,
    query_bias,
    value_bias,
    proj_weight,
    proj_bias,
    norm2_gain,
    norm2_bias,
    fc1_weight,
    fc1_bias,
    fc2_weight,
    fc2_bias,
    rel_height,
    rel_width,
):
    group_count = lax.axis_size("ga")
    head_groups = lax.axis_size("ha")
    group_index = lax.axis_index("ga")
    head_index = lax.axis_index("ha")
    device_count = group_count * head_groups
    block_len = patches.shape[1]
    model_width = patches.shape[2]
    hidden_width = fc1_bias.shape[0] * head_groups
    local_tokens = group_count * block_len
    group_width = model_width // head_groups
    group_heads = HEADS // head_groups
    cap_tokens = SMAX * SMAX
    f32 = jnp.float32
    bf16 = jnp.bfloat16

    triple_rows = lax.all_gather(qkv_weight, "ga", axis=1, tiled=True)
    up_rows, up_cols = fc1_weight.shape
    out_cols = fc2_weight.shape[1]
    packed = jnp.concatenate(
        [
            pack_up(fc1_weight),
            fc2_weight.T,
            proj_weight.T.reshape(out_cols // head_groups, model_width),
        ],
        axis=0,
    )
    pack_rows = packed.shape[0]
    up_height = up_rows * up_cols // model_width

    vectors = jnp.concatenate(
        [norm1_gain, norm1_bias, proj_bias, norm2_gain, norm2_bias, fc2_bias, fc1_bias]
    )
    vectors_all = lax.all_gather(vectors, "ha", axis=0, tiled=False)
    wide = model_width // head_groups

    def vector_at(slot, width):
        return vectors_all[:, slot * wide : slot * wide + width].reshape(-1)

    first_gain = vector_at(0, wide)
    first_shift = vector_at(1, wide)
    proj_shift = vector_at(2, wide)
    second_gain = vector_at(3, wide)
    second_shift = vector_at(4, wide)
    down_shift = vector_at(5, wide)
    up_shift = vector_at(6, 4 * wide)

    tokens_in = lax.all_to_all(patches, "ga", split_axis=0, concat_axis=1, tiled=True)[0]
    tokens_in, triple_rows = lax.optimization_barrier((tokens_in, triple_rows))
    cot_in = lax.all_to_all(cotangent, "ga", split_axis=0, concat_axis=1, tiled=True)[0]
    triple_cut = triple_rows.reshape(group_width, 3, head_groups, group_width).transpose(2, 0, 1, 3)
    triple_own = exchange(
        triple_cut.reshape(head_groups, group_width, 3 * group_width), "ha"
    ).reshape(model_width, 3 * group_width)
    tokens32 = tokens_in.astype(f32)
    cot32 = cot_in.astype(f32)
    slot_index = jnp.arange(local_tokens, dtype=jnp.int32)
    grid_index = (
        slot_index // block_len * head_groups + head_index
    ) * block_len + slot_index % block_len
    img_side = lax.dynamic_index_in_dim(sides, group_index, 0, keepdims=False)
    tok_mask = ((grid_index // SMAX < img_side) & (grid_index % SMAX < img_side)).astype(f32)[
        :, None
    ]
    all_index = jnp.arange(cap_tokens, dtype=jnp.int32)[:, None]
    line_index = jnp.arange(2 * SMAX, dtype=jnp.int32)[None, :]
    expand = jnp.where(
        line_index < SMAX,
        all_index // SMAX == line_index,
        all_index % SMAX == line_index - SMAX,
    ).astype(bf16)
    line_valid = line_index[0] % SMAX < img_side
    matrix = interp_matrix(img_side)
    table_h = jnp.einsum(
        "qkj,jd->qkd", matrix, rel_height.astype(f32), precision=exact_mode
    ).astype(bf16)
    table_w = jnp.einsum("qkj,jd->qkd", matrix, rel_width.astype(f32), precision=exact_mode).astype(
        bf16
    )

    tokens_all = (
        jnp.stack(
            [block.reshape(group_count, block_len, model_width) for block in gather_heads(tokens_in)],
            axis=1,
        )
        .reshape(cap_tokens, model_width)
        .astype(f32)
    )
    gain32 = first_gain.astype(f32)
    shift32 = first_shift.astype(f32)
    normed_all = layer_norm(tokens_all, gain32, shift32).astype(bf16)
    bias_own = jnp.concatenate([query_bias, jnp.zeros_like(query_bias), value_bias]).astype(f32)
    mixed = (jnp.dot(normed_all, triple_own, preferred_element_type=f32) + bias_own).astype(bf16)
    by_head = mixed.reshape(cap_tokens, 3, group_heads, HD).transpose(1, 2, 0, 3)
    q_all, key_all, value_all = by_head[0], by_head[1], by_head[2]

    q_grid = q_all.reshape(group_heads, SMAX, SMAX, HD)
    rel_h = jnp.einsum("hrwd,rkd->hrwk", q_grid, table_h, preferred_element_type=f32)
    rel_w = jnp.einsum("hrwd,wkd->hrwk", q_grid, table_w, preferred_element_type=f32)
    rel_both = jnp.concatenate([rel_h, rel_w], axis=-1).reshape(
        group_heads, cap_tokens, 2 * SMAX
    )
    rel_upper = lax.reduce_precision(rel_both, 8, 7)
    rel_lower = jnp.where(line_valid, rel_both - rel_upper, 0.0).astype(bf16)
    rel_upper = jnp.where(line_valid, rel_upper, -1e30).astype(bf16)
    q_aug = jnp.concatenate([q_all * jnp.asarray(HD**-0.5, bf16), rel_upper, rel_lower], axis=-1)
    expand_all = jnp.broadcast_to(expand, (group_heads,) + expand.shape)
    k_aug = jnp.concatenate([key_all, expand_all, expand_all], axis=-1)
    v_aug = jnp.concatenate(
        [
            value_all.swapaxes(1, 2),
            jnp.ones((group_heads, 1, cap_tokens), bf16),
            jnp.zeros((group_heads, 15, cap_tokens), bf16),
        ],
        axis=1,
    )
    k_turn = jnp.concatenate([key_all, expand_all], axis=-1).swapaxes(1, 2)
    att_heads, log_sums = attend_forward(q_aug, k_aug, v_aug)

    gathered = lax.all_gather(packed, BOTH, axis=0, tiled=False).reshape(
        group_count, head_groups, pack_rows, model_width
    )
    up_full = (
        unpack_up(gathered[:, :, :up_height], up_rows, up_cols)
        .transpose(1, 2, 0, 3)
        .reshape(model_width, hidden_width)
    )
    down_turn = (
        gathered[:, :, up_height : up_height + out_cols]
        .transpose(0, 2, 1, 3)
        .reshape(model_width, hidden_width)
    )
    proj_turn = (
        gathered[:, :, up_height + out_cols :]
        .reshape(group_count, head_groups, out_cols, group_width)
        .transpose(0, 2, 1, 3)
        .reshape(model_width, model_width)
    )

    att_back = lax.all_to_all(
        att_heads.reshape(group_count, head_groups, block_len, 1, group_width),
        "ha",
        split_axis=1,
        concat_axis=3,
        tiled=True,
    )
    att_tok = att_back.reshape(local_tokens, model_width)
    branch = contract_cols(att_tok, proj_turn) + proj_shift.astype(f32)
    middle = tokens32 + tok_mask * branch
    normed2 = layer_norm(middle, second_gain.astype(f32), second_shift.astype(f32)).astype(bf16)
    hidden = jnp.dot(normed2, up_full, preferred_element_type=f32) + up_shift.astype(f32)
    activated = jax.nn.gelu(hidden, approximate=False).astype(bf16)
    block_out = (
        middle + tok_mask * (contract_cols(activated, down_turn) + down_shift.astype(f32))
    ).astype(bf16)
    out_back = exchange(block_out.reshape(group_count, block_len, model_width), "ga")

    masked_cot = tok_mask * cot32
    down_in = masked_cot.astype(bf16)
    down_grad = contract_rows(down_in, activated).astype(bf16)
    down_bias_grad = jnp.sum(masked_cot, axis=0)
    act_grad = jnp.dot(down_in, down_turn, preferred_element_type=f32)
    gelu_value, gelu_pull = jax.vjp(partial(jax.nn.gelu, approximate=False), hidden)
    hidden_grad = gelu_pull(act_grad)[0].astype(bf16)
    up_grad = contract_rows(normed2, hidden_grad).astype(bf16)
    up_bias_grad = jnp.sum(hidden_grad.astype(f32), axis=0)
    norm2_in = contract_cols(hidden_grad, up_full)
    norm2_value, norm2_pull = jax.vjp(
        layer_norm, middle, second_gain.astype(f32), second_shift.astype(f32)
    )
    mid_grad, second_gain_grad, second_shift_grad = norm2_pull(norm2_in)
    mid_total = cot32 + mid_grad
    branch_grad = (tok_mask * mid_total).astype(bf16)
    proj_grad = contract_rows(branch_grad, att_tok).astype(bf16)
    proj_bias_grad = jnp.sum(branch_grad.astype(f32), axis=0)
    att_grad_tok = jnp.dot(branch_grad, proj_turn, preferred_element_type=f32).astype(bf16)
    att_grad = lax.all_to_all(
        att_grad_tok.reshape(group_count, 1, block_len, head_groups, group_width),
        "ha",
        split_axis=3,
        concat_axis=1,
        tiled=True,
    ).reshape(cap_tokens, group_width)

    grads_packed = jnp.concatenate(
        [
            pack_up(
                up_grad.reshape(head_groups, up_rows, group_count, up_cols).transpose(2, 0, 1, 3)
            ),
            down_grad.reshape(group_count, out_cols, head_groups, model_width).transpose(
                0, 2, 1, 3
            ),
            proj_grad.reshape(group_count, out_cols, head_groups, group_width)
            .transpose(0, 2, 1, 3)
            .reshape(group_count, head_groups, out_cols // head_groups, model_width),
        ],
        axis=2,
    ).reshape(device_count * pack_rows, model_width)
    grads_own = lax.psum_scatter(grads_packed, BOTH, scatter_dimension=0, tiled=True)
    up_own = unpack_up(grads_own[:up_height], up_rows, up_cols).astype(f32)
    down_own = grads_own[up_height : up_height + out_cols].T.astype(f32)
    proj_own = grads_own[up_height + out_cols :].reshape(out_cols, group_width).T.astype(f32)

    def reduce_vectors(vectors_in):
        stacked = jnp.concatenate(
            [
                vector.reshape(head_groups, group_count, -1)
                .transpose(1, 0, 2)
                .reshape(device_count, -1)
                for vector in vectors_in
            ],
            axis=1,
        )
        part = jnp.sum(exchange(stacked[:, None], BOTH), axis=0)
        own = spread(part, "ga")[:, 0]
        result = []
        at = 0
        for vector in vectors_in:
            size = vector.shape[0] // device_count
            result.append(own[:, at : at + size].reshape(-1))
            at += size
        return result

    early = reduce_vectors(
        [proj_bias_grad, second_gain_grad, second_shift_grad, down_bias_grad, up_bias_grad]
    )

    grad_heads = att_grad.reshape(cap_tokens, group_heads, HD)
    delta = (
        jnp.sum(
            grad_heads.astype(f32) * att_heads.reshape(cap_tokens, group_heads, HD).astype(f32),
            axis=-1,
        )
        .transpose(1, 0)
        .reshape(group_heads, 1, cap_tokens)
    )
    delta, out_back = lax.optimization_barrier((delta, out_back))
    query_part, line_sums, key_value_grad = attend_backward(
        q_aug, grad_heads.transpose(1, 0, 2), log_sums, delta, k_aug, value_all, k_turn
    )
    lines = line_sums.reshape(group_heads, SMAX, SMAX, 2 * SMAX)
    height_grad = lines[..., :SMAX]
    width_grad = lines[..., SMAX:]
    query_grad = (
        HD**-0.5 * query_part.reshape(group_heads, SMAX, SMAX, HD)
        + jnp.einsum("hrwj,rjd->hrwd", height_grad, table_h, preferred_element_type=f32)
        + jnp.einsum("hrwj,wjd->hrwd", width_grad, table_w, preferred_element_type=f32)
    ).reshape(group_heads, cap_tokens, HD)
    h_table_grad = jnp.einsum("hrwj,hrwd->rjd", height_grad, q_grid, preferred_element_type=f32)
    w_table_grad = jnp.einsum("hrwj,hrwd->wjd", width_grad, q_grid, preferred_element_type=f32)
    mixed_grad = jnp.concatenate(
        [
            query_grad.astype(bf16).transpose(1, 0, 2).reshape(cap_tokens, group_width),
            key_value_grad,
        ],
        axis=1,
    )
    norm1_wide = contract_cols(mixed_grad, triple_own)
    norm1_part = (
        norm1_wide.astype(bf16)
        .reshape(group_count, head_groups, block_len, model_width)
        .transpose(1, 0, 2, 3)
        .reshape(head_groups, local_tokens, model_width)
    )
    norm1_in = scatter_heads(norm1_part)
    triple_part = contract_rows(normed_all, mixed_grad).astype(bf16)
    triple_rows_grad = (
        exchange(triple_part.reshape(head_groups, group_width, 3 * group_width), "ha")
        .reshape(head_groups, group_width, 3, group_width)
        .transpose(1, 2, 0, 3)
        .reshape(group_width, group_count, 3 * model_width // group_count)
        .transpose(1, 0, 2)
    )
    triple_grad = jnp.sum(exchange(triple_rows_grad, "ga").astype(f32), axis=0)

    center = tokens_all - jnp.mean(tokens_all, axis=-1, keepdims=True)
    unit = center * lax.rsqrt(jnp.mean(center * center, axis=-1, keepdims=True) + 1e-06)
    first_gain_grad = jnp.sum(norm1_wide * unit, axis=0)
    first_shift_grad = jnp.sum(norm1_wide, axis=0)
    mixed_float = mixed_grad.astype(f32)
    zero_wide = jnp.zeros((model_width,), f32)

    def own_slot(vector):
        return lax.dynamic_update_slice(zero_wide, vector, (head_index * group_width,))

    query_bias_grad = own_slot(jnp.sum(mixed_float[:, :group_width], axis=0))
    value_bias_grad = own_slot(jnp.sum(mixed_float[:, 2 * group_width :], axis=0))
    height_rel = jnp.einsum("qkj,qkd->jd", matrix, h_table_grad, precision=exact_mode)
    width_rel = jnp.einsum("qkj,qkd->jd", matrix, w_table_grad, precision=exact_mode)
    rel_flat = jnp.concatenate([height_rel, width_rel]).reshape(-1)
    rel_size = rel_flat.shape[0]
    chunk = -(-rel_size // device_count)
    rel_flat = jnp.pad(rel_flat, (0, chunk * device_count - rel_size))
    piece = model_width // device_count
    last_vectors = [first_gain_grad, first_shift_grad, query_bias_grad, value_bias_grad]
    stacked = jnp.concatenate(
        [
            vector.reshape(head_groups, group_count, piece)
            .transpose(1, 0, 2)
            .reshape(device_count, piece)
            for vector in last_vectors
        ]
        + [rel_flat.reshape(device_count, chunk)],
        axis=1,
    )
    last_part = jnp.sum(exchange(stacked[:, None], BOTH), axis=0)
    last_all = spread(last_part, BOTH)[:, 0].reshape(group_count, head_groups, -1)
    last_here = lax.dynamic_index_in_dim(last_all, head_index, 1, False)
    late = [last_here[:, i * piece : (i + 1) * piece].reshape(-1) for i in range(4)]
    rel_sum = (
        last_all[:, :, 4 * piece :].reshape(-1)[:rel_size].reshape(2, 2 * SMAX - 1, HD)
    )

    norm1_value, norm1_pull = jax.vjp(lambda tokens: layer_norm(tokens, gain32, shift32), tokens32)
    input_grad = (mid_total + norm1_pull(norm1_in)[0]).astype(bf16)
    in_back = exchange(input_grad.reshape(group_count, block_len, model_width), "ga")
    return (
        out_back,
        in_back,
        late[0],
        late[1],
        triple_grad,
        late[2],
        late[3],
        proj_own,
        early[0],
        early[1],
        early[2],
        up_own,
        early[4],
        down_own,
        early[3],
        rel_sum[0],
        rel_sum[1],
    )


def solution(mesh):
    placed = (
        P(None, ("ga", "ha"), None),
        P(None, ("ga", "ha"), None),
        P(),
        P("ha"),
        P("ha"),
        P("ha", "ga"),
        P("ha"),
        P("ha"),
        P("ha", "ga"),
        P("ha"),
        P("ha"),
        P("ha"),
        P("ha", "ga"),
        P("ha"),
        P("ha", "ga"),
        P("ha"),
        P(),
        P(),
    )
    return jax.shard_map(
        local,
        mesh=mesh,
        in_specs=placed,
        out_specs=(
            P(None, ("ga", "ha"), None),
            P(None, ("ga", "ha"), None),
            P("ha"),
            P("ha"),
            P("ha", "ga"),
            P("ha"),
            P("ha"),
            P("ha", "ga"),
            P("ha"),
            P("ha"),
            P("ha"),
            P("ha", "ga"),
            P("ha"),
            P("ha", "ga"),
            P("ha"),
            P(),
            P(),
        ),
        check_vma=False,
    )
```

```python
from functools import partial

import jax
import jax.numpy as jnp
from jax import lax
from jax.experimental import pallas as pl
from jax.experimental.pallas import tpu as pltpu
from jax.sharding import PartitionSpec as P

HEADS = 12
HD = 64
SMAX = 48
BOTH = ("ga", "ha")


exact_mode = lax.Precision.HIGHEST


TBLK = 256
UBLK = 768

NT = (((1,), (1,)), ((), ()))


def mm(left, right):
    return jnp.dot(left, right, preferred_element_type=jnp.float32)


def mm_nt(left, right):
    return lax.dot_general(left, right, NT, preferred_element_type=jnp.float32)


def forward_kernel(q_ref, k_ref, v_ref, out_ref, lse_ref):
    heads = q_ref.shape[0]
    dim = 64
    outs = []
    for h in range(heads):
        scores = mm_nt(k_ref[h], q_ref[h])
        top = jnp.max(scores, axis=0, keepdims=True)
        expo = jnp.exp(scores - top).astype(jnp.bfloat16)
        mixed = mm(v_ref[h], expo)
        total = mixed[dim : dim + 1]
        outs.append((mixed[:dim] / total).T.astype(jnp.bfloat16))
        lse_ref[h] = top + jnp.log(total)
    out_ref[...] = jnp.concatenate(outs, axis=1)


def attend_forward(q_aug, k_aug, v_aug):
    heads, tokens, depth = q_aug.shape
    dim = 64
    return pl.pallas_call(
        forward_kernel,
        grid=(tokens // TBLK,),
        in_specs=[
            pl.BlockSpec((heads, TBLK, depth), lambda t: (0, t, 0)),
            pl.BlockSpec((heads, tokens, depth), lambda t: (0, 0, 0)),
            pl.BlockSpec((heads, v_aug.shape[1], tokens), lambda t: (0, 0, 0)),
        ],
        out_specs=[
            pl.BlockSpec((TBLK, heads * dim), lambda t: (t, 0)),
            pl.BlockSpec((heads, 1, TBLK), lambda t: (0, 0, t)),
        ],
        out_shape=[
            jax.ShapeDtypeStruct((tokens, heads * dim), jnp.bfloat16),
            jax.ShapeDtypeStruct((heads, 1, tokens), jnp.float32),
        ],
        name="attend_forward",
        compiler_params=pltpu.CompilerParams(dimension_semantics=("arbitrary",)),
    )(q_aug, k_aug, v_aug)


def backward_kernel(
    q_ref, g_ref, lse_ref, delta_ref, k_ref, v_ref, kt_ref, dq_ref, line_ref, out_ref, dkv_ref
):
    heads, tokens, depth = k_ref.shape
    dim = 64
    blk = q_ref.shape[1]

    @pl.when(pl.program_id(0) == 0)
    def _():
        dkv_ref[...] = jnp.zeros_like(dkv_ref)

    for h in range(heads):
        q_here = q_ref[h]
        g_here = g_ref[h]
        zero = jnp.zeros((blk, dim), jnp.bfloat16)
        g_wide = jnp.concatenate([g_here, zero], axis=1)
        q_wide = jnp.concatenate([zero, q_here[:, :dim]], axis=1)
        lse = lse_ref[h]
        delta = delta_ref[h]
        total = None
        for c in range(tokens // UBLK):
            span = pl.ds(c * UBLK, UBLK)
            scores = mm_nt(k_ref[h, span, :], q_here)
            probs = jnp.exp(scores - lse)
            pgrad = mm_nt(v_ref[h, span, :], g_here)
            sgrad = (probs * (pgrad - delta)).astype(jnp.bfloat16)
            dkv_ref[h, span, :] += mm(probs.astype(jnp.bfloat16), g_wide) + mm(sgrad, q_wide)
            part = mm(kt_ref[h, :, span], sgrad)
            total = part if total is None else total + part
        dq_ref[h] = total[:dim].T
        line_ref[h] = total[dim:].T.astype(jnp.bfloat16)

    @pl.when(pl.program_id(0) == pl.num_programs(0) - 1)
    def _():
        keys = [dkv_ref[h, :, dim:] for h in range(heads)]
        values = [dkv_ref[h, :, :dim] for h in range(heads)]
        out_ref[...] = jnp.concatenate(keys + values, axis=1).astype(jnp.bfloat16)


def attend_backward(q_aug, grads, lse, delta, k_aug, values, k_turn):
    heads, tokens, depth = q_aug.shape
    dim = 64
    lines = k_turn.shape[1] - dim
    return pl.pallas_call(
        backward_kernel,
        grid=(tokens // TBLK,),
        in_specs=[
            pl.BlockSpec((heads, TBLK, depth), lambda t: (0, t, 0)),
            pl.BlockSpec((heads, TBLK, dim), lambda t: (0, t, 0)),
            pl.BlockSpec((heads, 1, TBLK), lambda t: (0, 0, t)),
            pl.BlockSpec((heads, 1, TBLK), lambda t: (0, 0, t)),
            pl.BlockSpec((heads, tokens, depth), lambda t: (0, 0, 0)),
            pl.BlockSpec((heads, tokens, dim), lambda t: (0, 0, 0)),
            pl.BlockSpec((heads, dim + lines, tokens), lambda t: (0, 0, 0)),
        ],
        out_specs=[
            pl.BlockSpec((heads, TBLK, dim), lambda t: (0, t, 0)),
            pl.BlockSpec((heads, TBLK, lines), lambda t: (0, t, 0)),
            pl.BlockSpec((tokens, 2 * heads * dim), lambda t: (0, 0)),
        ],
        scratch_shapes=[pltpu.VMEM((heads, tokens, 2 * dim), jnp.float32)],
        out_shape=[
            jax.ShapeDtypeStruct((heads, tokens, dim), jnp.float32),
            jax.ShapeDtypeStruct((heads, tokens, lines), jnp.bfloat16),
            jax.ShapeDtypeStruct((tokens, 2 * heads * dim), jnp.bfloat16),
        ],
        name="attend_backward",
        compiler_params=pltpu.CompilerParams(dimension_semantics=("arbitrary",)),
    )(q_aug, grads, lse, delta, k_aug, values, k_turn)


def norm_parts(values):
    center = values - jnp.mean(values, axis=-1, keepdims=True)
    scale = lax.rsqrt(jnp.mean(center * center, axis=-1, keepdims=True) + 1e-06)
    return center * scale, scale


def feed_kernel(
    mid_ref,
    cot_ref,
    mask_ref,
    vec_ref,
    shift_ref,
    up_ref,
    down_ref,
    out_ref,
    total_ref,
    branch_ref,
    sums_ref,
    up_bias_ref,
    up_grad_ref,
    down_grad_ref,
    normed_ref,
    turned_ref,
    down_in_ref,
    down_turn_ref,
    out_acc_ref,
    in_acc_ref,
    weight_ref,
):
    f32 = jnp.float32
    bf16 = jnp.bfloat16
    step = pl.program_id(0)
    groups, heads, height, width = up_ref.shape
    cols = weight_ref.shape[1] // groups
    folds = width // cols
    rows = height * folds
    pieces, _, out_cols, _ = down_ref.shape

    @pl.when(step == 0)
    def _():
        unit, _ = norm_parts(mid_ref[...])
        normed = (unit * vec_ref[1:2] + vec_ref[2:3]).astype(bf16)
        normed_ref[...] = normed
        turned_ref[...] = normed.T
        masked = mask_ref[...] * cot_ref[...].astype(f32)
        down_in_ref[...] = masked.astype(bf16)
        down_turn_ref[...] = masked.astype(bf16).T
        out_acc_ref[...] = jnp.zeros_like(out_acc_ref)
        in_acc_ref[...] = jnp.zeros_like(in_acc_ref)

    for g in range(groups):
        for h in range(heads):
            for s in range(folds):
                top = h * rows + s * height
                weight_ref[top : top + height, g * cols : (g + 1) * cols] = up_ref[
                    g, h, :, s * cols : (s + 1) * cols
                ]
    weight = weight_ref[...]
    down = down_ref[...].reshape(pieces * out_cols, width)
    hidden = mm(normed_ref[...], weight) + shift_ref[0]
    share = 0.5 * (1.0 + lax.erf(hidden * (0.5**0.5)))
    active = (hidden * share).astype(bf16)
    slope = share + hidden * jnp.exp(-0.5 * hidden * hidden) * 0.3989422804014327
    out_acc_ref[...] += mm_nt(active, down)
    hidden_grad = (mm(down_in_ref[...], down) * slope).astype(bf16)
    down_grad_ref[...] = (
        mm(down_turn_ref[...], active).astype(bf16).reshape(pieces, 1, out_cols, width)
    )
    in_acc_ref[...] += mm_nt(hidden_grad, weight)
    up_bias_ref[0] = jnp.sum(hidden_grad.astype(f32), axis=0, keepdims=True)
    up_grad = mm(turned_ref[...], hidden_grad).astype(bf16)
    for g in range(groups):
        for h in range(heads):
            for s in range(folds):
                top = h * rows + s * height
                up_grad_ref[g, h, :, s * cols : (s + 1) * cols] = up_grad[
                    top : top + height, g * cols : (g + 1) * cols
                ]

    @pl.when(step == pl.num_programs(0) - 1)
    def _():
        middle = mid_ref[...]
        mask = mask_ref[...]
        cot = cot_ref[...].astype(f32)
        out_ref[...] = (middle + mask * (out_acc_ref[...] + vec_ref[3:4])).astype(bf16)
        unit, scale = norm_parts(middle)
        grad_in = in_acc_ref[...]
        inner = grad_in * vec_ref[1:2]
        total = cot + scale * (
            inner
            - jnp.mean(inner, axis=-1, keepdims=True)
            - unit * jnp.mean(inner * unit, axis=-1, keepdims=True)
        )
        branch = (mask * total).astype(bf16)
        total_ref[...] = total
        branch_ref[...] = branch
        sums_ref[...] = jnp.concatenate(
            [
                jnp.sum(branch.astype(f32), axis=0, keepdims=True),
                jnp.sum(grad_in * unit, axis=0, keepdims=True),
                jnp.sum(grad_in, axis=0, keepdims=True),
                jnp.sum(mask * cot, axis=0, keepdims=True),
            ],
            axis=0,
        )


def feed_forward(middle, cot, mask, vectors, shift, gathered, up_height, up_cols, out_cols):
    tokens, width = middle.shape
    groups, heads = gathered.shape[:2]
    steps = shift.shape[0]
    per_step = groups // steps
    f32 = jnp.float32
    bf16 = jnp.bfloat16

    def whole(rows, cols):
        return pl.BlockSpec((rows, cols), lambda c: (0, 0))

    up_spec = (per_step, heads, up_height, width)
    down_spec = (groups, 1, out_cols, width)
    return pl.pallas_call(
        feed_kernel,
        grid=(steps,),
        in_specs=[
            whole(tokens, width),
            whole(tokens, width),
            whole(tokens, 1),
            whole(vectors.shape[0], width),
            pl.BlockSpec((1, 1, width), lambda c: (c, 0, 0)),
            pl.BlockSpec(up_spec, lambda c: (c, 0, 0, 0)),
            pl.BlockSpec(down_spec, lambda c: (0, c, 1, 0)),
        ],
        out_specs=[
            whole(tokens, width),
            whole(tokens, width),
            whole(tokens, width),
            whole(4, width),
            pl.BlockSpec((1, 1, width), lambda c: (c, 0, 0)),
            pl.BlockSpec(up_spec, lambda c: (c, 0, 0, 0)),
            pl.BlockSpec(down_spec, lambda c: (0, c, 0, 0)),
        ],
        out_shape=[
            jax.ShapeDtypeStruct((tokens, width), bf16),
            jax.ShapeDtypeStruct((tokens, width), f32),
            jax.ShapeDtypeStruct((tokens, width), bf16),
            jax.ShapeDtypeStruct((4, width), f32),
            jax.ShapeDtypeStruct((steps, 1, width), f32),
            jax.ShapeDtypeStruct((groups, heads, up_height, width), bf16),
            jax.ShapeDtypeStruct((groups, heads, out_cols, width), bf16),
        ],
        scratch_shapes=[
            pltpu.VMEM((tokens, width), bf16),
            pltpu.VMEM((width, tokens), bf16),
            pltpu.VMEM((tokens, width), bf16),
            pltpu.VMEM((width, tokens), bf16),
            pltpu.VMEM((tokens, width), f32),
            pltpu.VMEM((tokens, width), f32),
            pltpu.VMEM((width, width), bf16),
        ],
        name="feed_forward",
        compiler_params=pltpu.CompilerParams(dimension_semantics=("arbitrary",)),
    )(middle, cot, mask, vectors, shift, gathered, gathered)


def layer_norm(values, gain, shift):
    center = values - jnp.mean(values, axis=-1, keepdims=True)
    spread = jnp.mean(center * center, axis=-1, keepdims=True)
    return center * lax.rsqrt(spread + 1e-06) * gain + shift


def interp_matrix(img_side):
    coord = jnp.arange(SMAX, dtype=jnp.int32)
    length_in = 2 * SMAX - 1
    length_out = 2 * img_side - 1
    offset = jnp.clip(coord[:, None] - coord[None, :] + img_side - 1, 0, length_out - 1)
    numer = jnp.maximum((2 * offset + 1) * length_in - length_out, 0)
    lower = numer // (2 * length_out)
    weight_hi = (numer - lower * 2 * length_out).astype(jnp.float32) / (2 * length_out).astype(
        jnp.float32
    )
    upper = jnp.minimum(lower + 1, length_in - 1)
    target = jnp.arange(length_in, dtype=jnp.int32)
    lower_hot = (target == lower[..., None]).astype(jnp.float32)
    upper_hot = (target == upper[..., None]).astype(jnp.float32)
    return (1.0 - weight_hi)[..., None] * lower_hot + weight_hi[..., None] * upper_hot


def contract_rows(left, right):
    return lax.dot_general(
        left, right, (((0,), (0,)), ((), ())), preferred_element_type=jnp.float32
    )


def contract_cols(left, right):
    return lax.dot_general(
        left, right, (((1,), (1,)), ((), ())), preferred_element_type=jnp.float32
    )


def exchange(values, axis):
    return lax.all_to_all(values, axis, split_axis=0, concat_axis=0, tiled=True)


def spread(values, axis):
    count = lax.axis_size(axis)
    return exchange(jnp.broadcast_to(values, (count,) + values.shape), axis)


def swap(values, step):
    pairs = [(i, i ^ step) for i in range(lax.axis_size("ha"))]
    return lax.ppermute(values, "ha", pairs)


def gather_heads(values):
    me = lax.axis_index("ha")
    far = swap(values, 2)
    near = swap(values, 1)
    corner = swap(far, 1)
    blocks = jnp.stack([values, near, far, corner])
    return [lax.dynamic_index_in_dim(blocks, jnp.bitwise_xor(me, i), 0, False) for i in range(4)]


def scatter_heads(parts):
    me = lax.axis_index("ha")
    other = [lax.dynamic_index_in_dim(parts, jnp.bitwise_xor(me, i), 0, False) for i in range(4)]
    arrived = swap(jnp.stack([other[3], other[1]]), 1).astype(jnp.float32)
    far = (other[2].astype(jnp.float32) + arrived[0]).astype(jnp.bfloat16)
    near = other[0].astype(jnp.float32) + arrived[1]
    return near + swap(far, 2).astype(jnp.float32)


def pack_up(piece):
    rows, width = piece.shape[-2:]
    lead = piece.shape[:-2]
    fold = 4 * rows // width
    cut = piece.reshape(lead + (fold, rows // fold, width))
    return jnp.swapaxes(cut, -3, -2).reshape(lead + (rows // fold, fold * width))


def unpack_up(packed, rows, width):
    fold = packed.shape[-1] // width
    lead = packed.shape[:-2]
    cut = packed.reshape(lead + (rows // fold, fold, width))
    return jnp.swapaxes(cut, -3, -2).reshape(lead + (rows, width))


def local(
    patches,
    cotangent,
    sides,
    norm1_gain,
    norm1_bias,
    qkv_weight,
    query_bias,
    value_bias,
    proj_weight,
    proj_bias,
    norm2_gain,
    norm2_bias,
    fc1_weight,
    fc1_bias,
    fc2_weight,
    fc2_bias,
    rel_height,
    rel_width,
):
    group_count = lax.axis_size("ga")
    head_groups = lax.axis_size("ha")
    group_index = lax.axis_index("ga")
    head_index = lax.axis_index("ha")
    device_count = group_count * head_groups
    block_len = patches.shape[1]
    model_width = patches.shape[2]
    hidden_width = fc1_bias.shape[0] * head_groups
    local_tokens = group_count * block_len
    group_width = model_width // head_groups
    group_heads = HEADS // head_groups
    cap_tokens = SMAX * SMAX
    f32 = jnp.float32
    bf16 = jnp.bfloat16

    triple_rows = lax.all_gather(qkv_weight, "ga", axis=1, tiled=True)
    up_rows, up_cols = fc1_weight.shape
    out_cols = fc2_weight.shape[1]
    packed = jnp.concatenate(
        [
            pack_up(fc1_weight),
            fc2_weight.T,
            proj_weight.T.reshape(out_cols // head_groups, model_width),
        ],
        axis=0,
    )
    pack_rows = packed.shape[0]
    up_height = up_rows * up_cols // model_width

    vectors = jnp.concatenate(
        [norm1_gain, norm1_bias, proj_bias, norm2_gain, norm2_bias, fc2_bias, fc1_bias]
    )
    vectors_all = lax.all_gather(vectors, "ha", axis=0, tiled=False)
    tokens_in = lax.all_to_all(patches, "ga", split_axis=0, concat_axis=1, tiled=True)[0]
    tokens_in, triple_rows, vectors_all, packed = lax.optimization_barrier(
        (tokens_in, triple_rows, vectors_all, packed)
    )
    cot_in = lax.all_to_all(cotangent, "ga", split_axis=0, concat_axis=1, tiled=True)[0]
    wide = model_width // head_groups

    def vector_at(slot, width):
        return vectors_all[:, slot * wide : slot * wide + width].reshape(-1)

    first_gain = vector_at(0, wide)
    first_shift = vector_at(1, wide)
    proj_shift = vector_at(2, wide)
    second_gain = vector_at(3, wide)
    second_shift = vector_at(4, wide)
    down_shift = vector_at(5, wide)
    up_shift = vector_at(6, 4 * wide)

    triple_cut = triple_rows.reshape(group_width, 3, head_groups, group_width).transpose(2, 0, 1, 3)
    triple_own = exchange(
        triple_cut.reshape(head_groups, group_width, 3 * group_width), "ha"
    ).reshape(model_width, 3 * group_width)
    tokens32 = tokens_in.astype(f32)
    cot32 = cot_in.astype(f32)
    slot_index = jnp.arange(local_tokens, dtype=jnp.int32)
    grid_index = (
        slot_index // block_len * head_groups + head_index
    ) * block_len + slot_index % block_len
    img_side = lax.dynamic_index_in_dim(sides, group_index, 0, keepdims=False)
    tok_mask = ((grid_index // SMAX < img_side) & (grid_index % SMAX < img_side)).astype(f32)[
        :, None
    ]
    all_index = jnp.arange(cap_tokens, dtype=jnp.int32)[:, None]
    line_index = jnp.arange(2 * SMAX, dtype=jnp.int32)[None, :]
    expand = jnp.where(
        line_index < SMAX,
        all_index // SMAX == line_index,
        all_index % SMAX == line_index - SMAX,
    ).astype(bf16)
    line_valid = line_index[0] % SMAX < img_side
    matrix = interp_matrix(img_side)
    table_h = jnp.einsum(
        "qkj,jd->qkd", matrix, rel_height.astype(f32), precision=exact_mode
    ).astype(bf16)
    table_w = jnp.einsum("qkj,jd->qkd", matrix, rel_width.astype(f32), precision=exact_mode).astype(
        bf16
    )

    tokens_all = (
        jnp.stack(
            [block.reshape(group_count, block_len, model_width) for block in gather_heads(tokens_in)],
            axis=1,
        )
        .reshape(cap_tokens, model_width)
        .astype(f32)
    )
    gain32 = first_gain.astype(f32)
    shift32 = first_shift.astype(f32)
    normed_all = layer_norm(tokens_all, gain32, shift32).astype(bf16)
    bias_own = jnp.concatenate([query_bias, jnp.zeros_like(query_bias), value_bias]).astype(f32)
    mixed = (jnp.dot(normed_all, triple_own, preferred_element_type=f32) + bias_own).astype(bf16)
    by_head = mixed.reshape(cap_tokens, 3, group_heads, HD).transpose(1, 2, 0, 3)
    q_all, key_all, value_all = by_head[0], by_head[1], by_head[2]

    q_grid = q_all.reshape(group_heads, SMAX, SMAX, HD)
    rel_h = jnp.einsum("hrwd,rkd->hrwk", q_grid, table_h, preferred_element_type=f32)
    rel_w = jnp.einsum("hrwd,wkd->hrwk", q_grid, table_w, preferred_element_type=f32)
    rel_both = jnp.concatenate([rel_h, rel_w], axis=-1).reshape(
        group_heads, cap_tokens, 2 * SMAX
    )
    rel_upper = lax.reduce_precision(rel_both, 8, 7)
    rel_lower = jnp.where(line_valid, rel_both - rel_upper, 0.0).astype(bf16)
    rel_upper = jnp.where(line_valid, rel_upper, -1e30).astype(bf16)
    q_aug = jnp.concatenate([q_all * jnp.asarray(HD**-0.5, bf16), rel_upper, rel_lower], axis=-1)
    expand_all = jnp.broadcast_to(expand, (group_heads,) + expand.shape)
    k_aug = jnp.concatenate([key_all, expand_all, expand_all], axis=-1)
    v_aug = jnp.concatenate(
        [
            value_all.swapaxes(1, 2),
            jnp.ones((group_heads, 1, cap_tokens), bf16),
            jnp.zeros((group_heads, 15, cap_tokens), bf16),
        ],
        axis=1,
    )
    k_turn = jnp.concatenate([key_all, expand_all], axis=-1).swapaxes(1, 2)
    att_heads, log_sums = attend_forward(q_aug, k_aug, v_aug)

    gathered = lax.all_gather(packed, BOTH, axis=0, tiled=False).reshape(
        group_count, head_groups, pack_rows, model_width
    )
    proj_turn = (
        gathered[:, :, up_height + out_cols :]
        .reshape(group_count, head_groups, out_cols, group_width)
        .transpose(0, 2, 1, 3)
        .reshape(model_width, model_width)
    )

    att_back = lax.all_to_all(
        att_heads.reshape(group_count, head_groups, block_len, 1, group_width),
        "ha",
        split_axis=1,
        concat_axis=3,
        tiled=True,
    )
    att_tok = att_back.reshape(local_tokens, model_width)
    branch = contract_cols(att_tok, proj_turn) + proj_shift.astype(f32)
    middle = tokens32 + tok_mask * branch
    steps = hidden_width // model_width
    if out_cols % 16 == 0 and up_cols % 128 == 0 and up_height == out_cols and steps == head_groups:
        norm_vectors = jnp.stack([proj_shift, second_gain, second_shift, down_shift]).astype(f32)
        (
            block_out,
            mid_total,
            branch_grad,
            small_sums,
            up_bias_grad,
            up_packed,
            down_packed,
        ) = feed_forward(
            middle,
            cot_in,
            tok_mask,
            norm_vectors,
            up_shift.astype(f32).reshape(steps, 1, model_width),
            gathered,
            up_height,
            up_cols,
            out_cols,
        )
        up_bias_grad = up_bias_grad.reshape(-1)
        proj_bias_grad, second_gain_grad, second_shift_grad, down_bias_grad = small_sums
    else:
        up_full = (
            unpack_up(gathered[:, :, :up_height], up_rows, up_cols)
            .transpose(1, 2, 0, 3)
            .reshape(model_width, hidden_width)
        )
        down_turn = (
            gathered[:, :, up_height : up_height + out_cols]
            .transpose(0, 2, 1, 3)
            .reshape(model_width, hidden_width)
        )
        normed2 = layer_norm(middle, second_gain.astype(f32), second_shift.astype(f32)).astype(bf16)
        hidden = jnp.dot(normed2, up_full, preferred_element_type=f32) + up_shift.astype(f32)
        activated = jax.nn.gelu(hidden, approximate=False).astype(bf16)
        block_out = (
            middle + tok_mask * (contract_cols(activated, down_turn) + down_shift.astype(f32))
        ).astype(bf16)
        masked_cot = tok_mask * cot32
        down_in = masked_cot.astype(bf16)
        down_grad = contract_rows(down_in, activated).astype(bf16)
        down_bias_grad = jnp.sum(masked_cot, axis=0)
        act_grad = jnp.dot(down_in, down_turn, preferred_element_type=f32)
        gelu_value, gelu_pull = jax.vjp(partial(jax.nn.gelu, approximate=False), hidden)
        hidden_grad = gelu_pull(act_grad)[0].astype(bf16)
        up_grad = contract_rows(normed2, hidden_grad).astype(bf16)
        up_bias_grad = jnp.sum(hidden_grad.astype(f32), axis=0)
        norm2_in = contract_cols(hidden_grad, up_full)
        norm2_value, norm2_pull = jax.vjp(
            layer_norm, middle, second_gain.astype(f32), second_shift.astype(f32)
        )
        mid_grad, second_gain_grad, second_shift_grad = norm2_pull(norm2_in)
        mid_total = cot32 + mid_grad
        branch_grad = (tok_mask * mid_total).astype(bf16)
        up_packed = pack_up(
            up_grad.reshape(head_groups, up_rows, group_count, up_cols).transpose(2, 0, 1, 3)
        )
        down_packed = down_grad.reshape(group_count, out_cols, head_groups, model_width).transpose(
            0, 2, 1, 3
        )
        proj_bias_grad = jnp.sum(branch_grad.astype(f32), axis=0)

    proj_grad = contract_rows(branch_grad, att_tok).astype(bf16)
    att_grad_tok = jnp.dot(branch_grad, proj_turn, preferred_element_type=f32).astype(bf16)
    att_grad = lax.all_to_all(
        att_grad_tok.reshape(group_count, 1, block_len, head_groups, group_width),
        "ha",
        split_axis=3,
        concat_axis=1,
        tiled=True,
    ).reshape(cap_tokens, group_width)
    att_grad, block_out, early_in = lax.optimization_barrier(
        (
            att_grad,
            block_out,
            [proj_bias_grad, second_gain_grad, second_shift_grad, down_bias_grad, up_bias_grad],
        )
    )
    out_back = exchange(block_out.reshape(group_count, block_len, model_width), "ga")

    grads_packed = jnp.concatenate(
        [
            up_packed,
            down_packed,
            proj_grad.reshape(group_count, out_cols, head_groups, group_width)
            .transpose(0, 2, 1, 3)
            .reshape(group_count, head_groups, out_cols // head_groups, model_width),
        ],
        axis=2,
    ).reshape(device_count * pack_rows, model_width)
    grads_own = lax.psum_scatter(grads_packed, BOTH, scatter_dimension=0, tiled=True)
    up_own = unpack_up(grads_own[:up_height], up_rows, up_cols).astype(f32)
    down_own = grads_own[up_height : up_height + out_cols].T.astype(f32)
    proj_own = grads_own[up_height + out_cols :].reshape(out_cols, group_width).T.astype(f32)

    def reduce_vectors(vectors_in):
        stacked = jnp.concatenate(
            [
                vector.reshape(head_groups, group_count, -1)
                .transpose(1, 0, 2)
                .reshape(device_count, -1)
                for vector in vectors_in
            ],
            axis=1,
        )
        part = jnp.sum(exchange(stacked[:, None], BOTH), axis=0)
        own = spread(part, "ga")[:, 0]
        result = []
        at = 0
        for vector in vectors_in:
            size = vector.shape[0] // device_count
            result.append(own[:, at : at + size].reshape(-1))
            at += size
        return result

    early = reduce_vectors(early_in)

    grad_heads = att_grad.reshape(cap_tokens, group_heads, HD)
    delta = (
        jnp.sum(
            grad_heads.astype(f32) * att_heads.reshape(cap_tokens, group_heads, HD).astype(f32),
            axis=-1,
        )
        .transpose(1, 0)
        .reshape(group_heads, 1, cap_tokens)
    )
    delta, out_back = lax.optimization_barrier((delta, out_back))
    query_part, line_sums, key_value_grad = attend_backward(
        q_aug, grad_heads.transpose(1, 0, 2), log_sums, delta, k_aug, value_all, k_turn
    )
    lines = line_sums.reshape(group_heads, SMAX, SMAX, 2 * SMAX)
    height_grad = lines[..., :SMAX]
    width_grad = lines[..., SMAX:]
    query_grad = (
        HD**-0.5 * query_part.reshape(group_heads, SMAX, SMAX, HD)
        + jnp.einsum("hrwj,rjd->hrwd", height_grad, table_h, preferred_element_type=f32)
        + jnp.einsum("hrwj,wjd->hrwd", width_grad, table_w, preferred_element_type=f32)
    ).reshape(group_heads, cap_tokens, HD)
    h_table_grad = jnp.einsum("hrwj,hrwd->rjd", height_grad, q_grid, preferred_element_type=f32)
    w_table_grad = jnp.einsum("hrwj,hrwd->wjd", width_grad, q_grid, preferred_element_type=f32)
    mixed_grad = jnp.concatenate(
        [
            query_grad.astype(bf16).transpose(1, 0, 2).reshape(cap_tokens, group_width),
            key_value_grad,
        ],
        axis=1,
    )
    norm1_wide = contract_cols(mixed_grad, triple_own)
    norm1_part = (
        norm1_wide.astype(bf16)
        .reshape(group_count, head_groups, block_len, model_width)
        .transpose(1, 0, 2, 3)
        .reshape(head_groups, local_tokens, model_width)
    )
    norm1_in = scatter_heads(norm1_part)
    triple_part = contract_rows(normed_all, mixed_grad).astype(bf16)
    triple_rows_grad = (
        exchange(triple_part.reshape(head_groups, group_width, 3 * group_width), "ha")
        .reshape(head_groups, group_width, 3, group_width)
        .transpose(1, 2, 0, 3)
        .reshape(group_width, group_count, 3 * model_width // group_count)
        .transpose(1, 0, 2)
    )
    triple_grad = jnp.sum(exchange(triple_rows_grad, "ga").astype(f32), axis=0)

    center = tokens_all - jnp.mean(tokens_all, axis=-1, keepdims=True)
    unit = center * lax.rsqrt(jnp.mean(center * center, axis=-1, keepdims=True) + 1e-06)
    first_gain_grad = jnp.sum(norm1_wide * unit, axis=0)
    first_shift_grad = jnp.sum(norm1_wide, axis=0)
    mixed_float = mixed_grad.astype(f32)
    zero_wide = jnp.zeros((model_width,), f32)

    def own_slot(vector):
        return lax.dynamic_update_slice(zero_wide, vector, (head_index * group_width,))

    query_bias_grad = own_slot(jnp.sum(mixed_float[:, :group_width], axis=0))
    value_bias_grad = own_slot(jnp.sum(mixed_float[:, 2 * group_width :], axis=0))
    height_rel = jnp.einsum("qkj,qkd->jd", matrix, h_table_grad, precision=exact_mode)
    width_rel = jnp.einsum("qkj,qkd->jd", matrix, w_table_grad, precision=exact_mode)
    rel_flat = jnp.concatenate([height_rel, width_rel]).reshape(-1)
    rel_size = rel_flat.shape[0]
    chunk = -(-rel_size // device_count)
    rel_flat = jnp.pad(rel_flat, (0, chunk * device_count - rel_size))
    piece = model_width // device_count
    last_vectors = [first_gain_grad, first_shift_grad, query_bias_grad, value_bias_grad]
    stacked = jnp.concatenate(
        [
            vector.reshape(head_groups, group_count, piece)
            .transpose(1, 0, 2)
            .reshape(device_count, piece)
            for vector in last_vectors
        ]
        + [rel_flat.reshape(device_count, chunk)],
        axis=1,
    )
    last_part = jnp.sum(exchange(stacked[:, None], BOTH), axis=0)
    last_all = spread(last_part, BOTH)[:, 0].reshape(group_count, head_groups, -1)
    last_here = lax.dynamic_index_in_dim(last_all, head_index, 1, False)
    late = [last_here[:, i * piece : (i + 1) * piece].reshape(-1) for i in range(4)]
    rel_sum = (
        last_all[:, :, 4 * piece :].reshape(-1)[:rel_size].reshape(2, 2 * SMAX - 1, HD)
    )

    norm1_value, norm1_pull = jax.vjp(lambda tokens: layer_norm(tokens, gain32, shift32), tokens32)
    input_grad = (mid_total + norm1_pull(norm1_in)[0]).astype(bf16)
    in_back = exchange(input_grad.reshape(group_count, block_len, model_width), "ga")
    return (
        out_back,
        in_back,
        late[0],
        late[1],
        triple_grad,
        late[2],
        late[3],
        proj_own,
        early[0],
        early[1],
        early[2],
        up_own,
        early[4],
        down_own,
        early[3],
        rel_sum[0],
        rel_sum[1],
    )


def solution(mesh):
    placed = (
        P(None, ("ga", "ha"), None),
        P(None, ("ga", "ha"), None),
        P(),
        P("ha"),
        P("ha"),
        P("ha", "ga"),
        P("ha"),
        P("ha"),
        P("ha", "ga"),
        P("ha"),
        P("ha"),
        P("ha"),
        P("ha", "ga"),
        P("ha"),
        P("ha", "ga"),
        P("ha"),
        P(),
        P(),
    )
    return jax.shard_map(
        local,
        mesh=mesh,
        in_specs=placed,
        out_specs=(
            P(None, ("ga", "ha"), None),
            P(None, ("ga", "ha"), None),
            P("ha"),
            P("ha"),
            P("ha", "ga"),
            P("ha"),
            P("ha"),
            P("ha", "ga"),
            P("ha"),
            P("ha"),
            P("ha"),
            P("ha", "ga"),
            P("ha"),
            P("ha", "ga"),
            P("ha"),
            P(),
            P(),
        ),
        check_vma=False,
    )
```

```python
from functools import partial

import jax
import jax.numpy as jnp
from jax import lax
from jax.experimental import pallas as pl
from jax.experimental.pallas import tpu as pltpu
from jax.sharding import PartitionSpec as P

HEADS = 12
HD = 64
SMAX = 48
BOTH = ("ga", "ha")


exact_mode = lax.Precision.HIGHEST


TBLK = 256
UBLK = 768

NT = (((1,), (1,)), ((), ()))


def mm(left, right):
    return jnp.dot(left, right, preferred_element_type=jnp.float32)


def mm_nt(left, right):
    return lax.dot_general(left, right, NT, preferred_element_type=jnp.float32)


def forward_kernel(q_ref, k_ref, v_ref, out_ref, lse_ref):
    heads = q_ref.shape[0]
    dim = 64
    outs = []
    for h in range(heads):
        scores = mm_nt(k_ref[h], q_ref[h])
        top = jnp.max(scores, axis=0, keepdims=True)
        expo = jnp.exp(scores - top).astype(jnp.bfloat16)
        mixed = mm(v_ref[h], expo)
        total = mixed[dim : dim + 1]
        outs.append((mixed[:dim] / total).T.astype(jnp.bfloat16))
        lse_ref[h] = top + jnp.log(total)
    out_ref[...] = jnp.concatenate(outs, axis=1)


def attend_forward(q_aug, k_aug, v_aug):
    heads, tokens, depth = q_aug.shape
    dim = 64
    return pl.pallas_call(
        forward_kernel,
        grid=(tokens // TBLK,),
        in_specs=[
            pl.BlockSpec((heads, TBLK, depth), lambda t: (0, t, 0)),
            pl.BlockSpec((heads, tokens, depth), lambda t: (0, 0, 0)),
            pl.BlockSpec((heads, v_aug.shape[1], tokens), lambda t: (0, 0, 0)),
        ],
        out_specs=[
            pl.BlockSpec((TBLK, heads * dim), lambda t: (t, 0)),
            pl.BlockSpec((heads, 1, TBLK), lambda t: (0, 0, t)),
        ],
        out_shape=[
            jax.ShapeDtypeStruct((tokens, heads * dim), jnp.bfloat16),
            jax.ShapeDtypeStruct((heads, 1, tokens), jnp.float32),
        ],
        name="attend_forward",
        compiler_params=pltpu.CompilerParams(dimension_semantics=("arbitrary",)),
    )(q_aug, k_aug, v_aug)


def backward_kernel(
    q_ref, g_ref, lse_ref, delta_ref, k_ref, v_ref, kt_ref, dq_ref, line_ref, out_ref, dkv_ref
):
    heads, tokens, depth = k_ref.shape
    dim = 64
    blk = q_ref.shape[1]

    @pl.when(pl.program_id(0) == 0)
    def _():
        dkv_ref[...] = jnp.zeros_like(dkv_ref)

    for h in range(heads):
        q_here = q_ref[h]
        g_here = g_ref[h]
        zero = jnp.zeros((blk, dim), jnp.bfloat16)
        g_wide = jnp.concatenate([g_here, zero], axis=1)
        q_wide = jnp.concatenate([zero, q_here[:, :dim]], axis=1)
        lse = lse_ref[h]
        delta = delta_ref[h]
        total = None
        for c in range(tokens // UBLK):
            span = pl.ds(c * UBLK, UBLK)
            scores = mm_nt(k_ref[h, span, :], q_here)
            probs = jnp.exp(scores - lse)
            pgrad = mm_nt(v_ref[h, span, :], g_here)
            sgrad = (probs * (pgrad - delta)).astype(jnp.bfloat16)
            dkv_ref[h, span, :] += mm(probs.astype(jnp.bfloat16), g_wide) + mm(sgrad, q_wide)
            part = mm(kt_ref[h, :, span], sgrad)
            total = part if total is None else total + part
        dq_ref[h] = total[:dim].T
        line_ref[h] = total[dim:].T.astype(jnp.bfloat16)

    @pl.when(pl.program_id(0) == pl.num_programs(0) - 1)
    def _():
        keys = [dkv_ref[h, :, dim:] for h in range(heads)]
        values = [dkv_ref[h, :, :dim] for h in range(heads)]
        out_ref[...] = jnp.concatenate(keys + values, axis=1).astype(jnp.bfloat16)


def attend_backward(q_aug, grads, lse, delta, k_aug, values, k_turn):
    heads, tokens, depth = q_aug.shape
    dim = 64
    lines = k_turn.shape[1] - dim
    return pl.pallas_call(
        backward_kernel,
        grid=(tokens // TBLK,),
        in_specs=[
            pl.BlockSpec((heads, TBLK, depth), lambda t: (0, t, 0)),
            pl.BlockSpec((heads, TBLK, dim), lambda t: (0, t, 0)),
            pl.BlockSpec((heads, 1, TBLK), lambda t: (0, 0, t)),
            pl.BlockSpec((heads, 1, TBLK), lambda t: (0, 0, t)),
            pl.BlockSpec((heads, tokens, depth), lambda t: (0, 0, 0)),
            pl.BlockSpec((heads, tokens, dim), lambda t: (0, 0, 0)),
            pl.BlockSpec((heads, dim + lines, tokens), lambda t: (0, 0, 0)),
        ],
        out_specs=[
            pl.BlockSpec((heads, TBLK, dim), lambda t: (0, t, 0)),
            pl.BlockSpec((heads, TBLK, lines), lambda t: (0, t, 0)),
            pl.BlockSpec((tokens, 2 * heads * dim), lambda t: (0, 0)),
        ],
        scratch_shapes=[pltpu.VMEM((heads, tokens, 2 * dim), jnp.float32)],
        out_shape=[
            jax.ShapeDtypeStruct((heads, tokens, dim), jnp.float32),
            jax.ShapeDtypeStruct((heads, tokens, lines), jnp.bfloat16),
            jax.ShapeDtypeStruct((tokens, 2 * heads * dim), jnp.bfloat16),
        ],
        name="attend_backward",
        compiler_params=pltpu.CompilerParams(dimension_semantics=("arbitrary",)),
    )(q_aug, grads, lse, delta, k_aug, values, k_turn)


def norm_parts(values):
    center = values - jnp.mean(values, axis=-1, keepdims=True)
    scale = lax.rsqrt(jnp.mean(center * center, axis=-1, keepdims=True) + 1e-06)
    return center * scale, scale


def feed_kernel(
    mid_ref,
    cot_ref,
    mask_ref,
    vec_ref,
    shift_ref,
    up_ref,
    down_ref,
    out_ref,
    total_ref,
    branch_ref,
    sums_ref,
    up_bias_ref,
    up_grad_ref,
    down_grad_ref,
    normed_ref,
    turned_ref,
    down_in_ref,
    down_turn_ref,
    out_acc_ref,
    in_acc_ref,
    weight_ref,
):
    f32 = jnp.float32
    bf16 = jnp.bfloat16
    step = pl.program_id(0)
    groups, heads, height, width = up_ref.shape
    cols = weight_ref.shape[1] // groups
    folds = width // cols
    rows = height * folds
    pieces, _, out_cols, _ = down_ref.shape

    @pl.when(step == 0)
    def _():
        unit, _ = norm_parts(mid_ref[...])
        normed = (unit * vec_ref[1:2] + vec_ref[2:3]).astype(bf16)
        normed_ref[...] = normed
        turned_ref[...] = normed.T
        masked = mask_ref[...] * cot_ref[...].astype(f32)
        down_in_ref[...] = masked.astype(bf16)
        down_turn_ref[...] = masked.astype(bf16).T
        out_acc_ref[...] = jnp.zeros_like(out_acc_ref)
        in_acc_ref[...] = jnp.zeros_like(in_acc_ref)

    for g in range(groups):
        for h in range(heads):
            for s in range(folds):
                top = h * rows + s * height
                weight_ref[top : top + height, g * cols : (g + 1) * cols] = up_ref[
                    g, h, :, s * cols : (s + 1) * cols
                ]
    weight = weight_ref[...]
    down = down_ref[...].reshape(pieces * out_cols, width)
    hidden = mm(normed_ref[...], weight) + shift_ref[0]
    share = 0.5 * (1.0 + lax.erf(hidden * (0.5**0.5)))
    active = (hidden * share).astype(bf16)
    slope = share + hidden * jnp.exp(-0.5 * hidden * hidden) * 0.3989422804014327
    out_acc_ref[...] += mm_nt(active, down)
    hidden_grad = (mm(down_in_ref[...], down) * slope).astype(bf16)
    down_grad_ref[...] = (
        mm(down_turn_ref[...], active).astype(bf16).reshape(pieces, 1, out_cols, width)
    )
    in_acc_ref[...] += mm_nt(hidden_grad, weight)
    up_bias_ref[0] = jnp.sum(hidden_grad.astype(f32), axis=0, keepdims=True)
    up_grad = mm(turned_ref[...], hidden_grad).astype(bf16)
    for g in range(groups):
        for h in range(heads):
            for s in range(folds):
                top = h * rows + s * height
                up_grad_ref[g, h, :, s * cols : (s + 1) * cols] = up_grad[
                    top : top + height, g * cols : (g + 1) * cols
                ]

    @pl.when(step == pl.num_programs(0) - 1)
    def _():
        middle = mid_ref[...]
        mask = mask_ref[...]
        cot = cot_ref[...].astype(f32)
        out_ref[...] = (middle + mask * (out_acc_ref[...] + vec_ref[3:4])).astype(bf16)
        unit, scale = norm_parts(middle)
        grad_in = in_acc_ref[...]
        inner = grad_in * vec_ref[1:2]
        total = cot + scale * (
            inner
            - jnp.mean(inner, axis=-1, keepdims=True)
            - unit * jnp.mean(inner * unit, axis=-1, keepdims=True)
        )
        branch = (mask * total).astype(bf16)
        total_ref[...] = total
        branch_ref[...] = branch
        sums_ref[...] = jnp.concatenate(
            [
                jnp.sum(branch.astype(f32), axis=0, keepdims=True),
                jnp.sum(grad_in * unit, axis=0, keepdims=True),
                jnp.sum(grad_in, axis=0, keepdims=True),
                jnp.sum(mask * cot, axis=0, keepdims=True),
            ],
            axis=0,
        )


def feed_forward(middle, cot, mask, vectors, shift, gathered, up_height, up_cols, out_cols):
    tokens, width = middle.shape
    groups, heads = gathered.shape[:2]
    steps = shift.shape[0]
    per_step = groups // steps
    f32 = jnp.float32
    bf16 = jnp.bfloat16

    def whole(rows, cols):
        return pl.BlockSpec((rows, cols), lambda c: (0, 0))

    up_spec = (per_step, heads, up_height, width)
    down_spec = (groups, 1, out_cols, width)
    return pl.pallas_call(
        feed_kernel,
        grid=(steps,),
        in_specs=[
            whole(tokens, width),
            whole(tokens, width),
            whole(tokens, 1),
            whole(vectors.shape[0], width),
            pl.BlockSpec((1, 1, width), lambda c: (c, 0, 0)),
            pl.BlockSpec(up_spec, lambda c: (c, 0, 0, 0)),
            pl.BlockSpec(down_spec, lambda c: (0, c, 1, 0)),
        ],
        out_specs=[
            whole(tokens, width),
            whole(tokens, width),
            whole(tokens, width),
            whole(4, width),
            pl.BlockSpec((1, 1, width), lambda c: (c, 0, 0)),
            pl.BlockSpec(up_spec, lambda c: (c, 0, 0, 0)),
            pl.BlockSpec(down_spec, lambda c: (0, c, 0, 0)),
        ],
        out_shape=[
            jax.ShapeDtypeStruct((tokens, width), bf16),
            jax.ShapeDtypeStruct((tokens, width), f32),
            jax.ShapeDtypeStruct((tokens, width), bf16),
            jax.ShapeDtypeStruct((4, width), f32),
            jax.ShapeDtypeStruct((steps, 1, width), f32),
            jax.ShapeDtypeStruct((groups, heads, up_height, width), bf16),
            jax.ShapeDtypeStruct((groups, heads, out_cols, width), bf16),
        ],
        scratch_shapes=[
            pltpu.VMEM((tokens, width), bf16),
            pltpu.VMEM((width, tokens), bf16),
            pltpu.VMEM((tokens, width), bf16),
            pltpu.VMEM((width, tokens), bf16),
            pltpu.VMEM((tokens, width), f32),
            pltpu.VMEM((tokens, width), f32),
            pltpu.VMEM((width, width), bf16),
        ],
        name="feed_forward",
        compiler_params=pltpu.CompilerParams(dimension_semantics=("arbitrary",)),
    )(middle, cot, mask, vectors, shift, gathered, gathered)


def layer_norm(values, gain, shift):
    center = values - jnp.mean(values, axis=-1, keepdims=True)
    spread = jnp.mean(center * center, axis=-1, keepdims=True)
    return center * lax.rsqrt(spread + 1e-06) * gain + shift


def interp_matrix(img_side):
    coord = jnp.arange(SMAX, dtype=jnp.int32)
    length_in = 2 * SMAX - 1
    length_out = 2 * img_side - 1
    offset = jnp.clip(coord[:, None] - coord[None, :] + img_side - 1, 0, length_out - 1)
    numer = jnp.maximum((2 * offset + 1) * length_in - length_out, 0)
    lower = numer // (2 * length_out)
    weight_hi = (numer - lower * 2 * length_out).astype(jnp.float32) / (2 * length_out).astype(
        jnp.float32
    )
    upper = jnp.minimum(lower + 1, length_in - 1)
    target = jnp.arange(length_in, dtype=jnp.int32)
    lower_hot = (target == lower[..., None]).astype(jnp.float32)
    upper_hot = (target == upper[..., None]).astype(jnp.float32)
    return (1.0 - weight_hi)[..., None] * lower_hot + weight_hi[..., None] * upper_hot


def contract_rows(left, right):
    return lax.dot_general(
        left, right, (((0,), (0,)), ((), ())), preferred_element_type=jnp.float32
    )


def contract_cols(left, right):
    return lax.dot_general(
        left, right, (((1,), (1,)), ((), ())), preferred_element_type=jnp.float32
    )


def exchange(values, axis):
    return lax.all_to_all(values, axis, split_axis=0, concat_axis=0, tiled=True)


def spread(values, axis):
    count = lax.axis_size(axis)
    return exchange(jnp.broadcast_to(values, (count,) + values.shape), axis)


def swap(values, step):
    pairs = [(i, i ^ step) for i in range(lax.axis_size("ha"))]
    return lax.ppermute(values, "ha", pairs)


def gather_heads(values):
    me = lax.axis_index("ha")
    far = swap(values, 2)
    near = swap(values, 1)
    corner = swap(far, 1)
    blocks = jnp.stack([values, near, far, corner])
    return [lax.dynamic_index_in_dim(blocks, jnp.bitwise_xor(me, i), 0, False) for i in range(4)]


def scatter_heads(parts):
    me = lax.axis_index("ha")
    other = [lax.dynamic_index_in_dim(parts, jnp.bitwise_xor(me, i), 0, False) for i in range(4)]
    arrived = swap(jnp.stack([other[3], other[1]]), 1).astype(jnp.float32)
    far = (other[2].astype(jnp.float32) + arrived[0]).astype(jnp.bfloat16)
    near = other[0].astype(jnp.float32) + arrived[1]
    return near + swap(far, 2).astype(jnp.float32)


def pack_up(piece):
    rows, width = piece.shape[-2:]
    lead = piece.shape[:-2]
    fold = 4 * rows // width
    cut = piece.reshape(lead + (fold, rows // fold, width))
    return jnp.swapaxes(cut, -3, -2).reshape(lead + (rows // fold, fold * width))


def unpack_up(packed, rows, width):
    fold = packed.shape[-1] // width
    lead = packed.shape[:-2]
    cut = packed.reshape(lead + (rows // fold, fold, width))
    return jnp.swapaxes(cut, -3, -2).reshape(lead + (rows, width))


def local(
    patches,
    cotangent,
    sides,
    norm1_gain,
    norm1_bias,
    qkv_weight,
    query_bias,
    value_bias,
    proj_weight,
    proj_bias,
    norm2_gain,
    norm2_bias,
    fc1_weight,
    fc1_bias,
    fc2_weight,
    fc2_bias,
    rel_height,
    rel_width,
):
    group_count = lax.axis_size("ga")
    head_groups = lax.axis_size("ha")
    group_index = lax.axis_index("ga")
    head_index = lax.axis_index("ha")
    device_count = group_count * head_groups
    block_len = patches.shape[1]
    model_width = patches.shape[2]
    hidden_width = fc1_bias.shape[0] * head_groups
    local_tokens = group_count * block_len
    group_width = model_width // head_groups
    group_heads = HEADS // head_groups
    cap_tokens = SMAX * SMAX
    f32 = jnp.float32
    bf16 = jnp.bfloat16

    triple_rows = lax.all_gather(qkv_weight, "ga", axis=1, tiled=True)
    up_rows, up_cols = fc1_weight.shape
    out_cols = fc2_weight.shape[1]
    packed = jnp.concatenate(
        [
            pack_up(fc1_weight),
            fc2_weight.T,
            proj_weight.T.reshape(out_cols // head_groups, model_width),
        ],
        axis=0,
    )
    pack_rows = packed.shape[0]
    up_height = up_rows * up_cols // model_width

    vectors = jnp.concatenate(
        [norm1_gain, norm1_bias, proj_bias, norm2_gain, norm2_bias, fc2_bias, fc1_bias]
    )
    vectors_all = lax.all_gather(vectors, "ha", axis=0, tiled=False)
    tokens_in = lax.all_to_all(patches, "ga", split_axis=0, concat_axis=1, tiled=True)[0]
    tokens_in, triple_rows, vectors_all, packed = lax.optimization_barrier(
        (tokens_in, triple_rows, vectors_all, packed)
    )
    cot_in = lax.all_to_all(cotangent, "ga", split_axis=0, concat_axis=1, tiled=True)[0]
    wide = model_width // head_groups

    def vector_at(slot, width):
        return vectors_all[:, slot * wide : slot * wide + width].reshape(-1)

    first_gain = vector_at(0, wide)
    first_shift = vector_at(1, wide)
    proj_shift = vector_at(2, wide)
    second_gain = vector_at(3, wide)
    second_shift = vector_at(4, wide)
    down_shift = vector_at(5, wide)
    up_shift = vector_at(6, 4 * wide)

    triple_cut = triple_rows.reshape(group_width, 3, head_groups, group_width).transpose(2, 0, 1, 3)
    triple_own = exchange(
        triple_cut.reshape(head_groups, group_width, 3 * group_width), "ha"
    ).reshape(model_width, 3 * group_width)
    tokens32 = tokens_in.astype(f32)
    slot_index = jnp.arange(local_tokens, dtype=jnp.int32)
    grid_index = (
        slot_index // block_len * head_groups + head_index
    ) * block_len + slot_index % block_len
    img_side = lax.dynamic_index_in_dim(sides, group_index, 0, keepdims=False)
    tok_mask = ((grid_index // SMAX < img_side) & (grid_index % SMAX < img_side)).astype(f32)[
        :, None
    ]
    all_index = jnp.arange(cap_tokens, dtype=jnp.int32)[:, None]
    line_index = jnp.arange(2 * SMAX, dtype=jnp.int32)[None, :]
    expand = jnp.where(
        line_index < SMAX,
        all_index // SMAX == line_index,
        all_index % SMAX == line_index - SMAX,
    ).astype(bf16)
    line_valid = line_index[0] % SMAX < img_side
    matrix = interp_matrix(img_side)
    table_h = jnp.einsum(
        "qkj,jd->qkd", matrix, rel_height.astype(f32), precision=exact_mode
    ).astype(bf16)
    table_w = jnp.einsum("qkj,jd->qkd", matrix, rel_width.astype(f32), precision=exact_mode).astype(
        bf16
    )

    tokens_all = (
        jnp.stack(
            [block.reshape(group_count, block_len, model_width) for block in gather_heads(tokens_in)],
            axis=1,
        )
        .reshape(cap_tokens, model_width)
        .astype(f32)
    )
    gain32 = first_gain.astype(f32)
    shift32 = first_shift.astype(f32)
    normed_all = layer_norm(tokens_all, gain32, shift32).astype(bf16)
    bias_own = jnp.concatenate([query_bias, jnp.zeros_like(query_bias), value_bias]).astype(f32)
    mixed = (jnp.dot(normed_all, triple_own, preferred_element_type=f32) + bias_own).astype(bf16)
    by_head = mixed.reshape(cap_tokens, 3, group_heads, HD).transpose(1, 2, 0, 3)
    q_all, key_all, value_all = by_head[0], by_head[1], by_head[2]

    q_grid = q_all.reshape(group_heads, SMAX, SMAX, HD)
    rel_h = jnp.einsum("hrwd,rkd->hrwk", q_grid, table_h, preferred_element_type=f32)
    rel_w = jnp.einsum("hrwd,wkd->hrwk", q_grid, table_w, preferred_element_type=f32)
    rel_both = jnp.concatenate([rel_h, rel_w], axis=-1).reshape(
        group_heads, cap_tokens, 2 * SMAX
    )
    rel_upper = lax.reduce_precision(rel_both, 8, 7)
    rel_lower = jnp.where(line_valid, rel_both - rel_upper, 0.0).astype(bf16)
    rel_upper = jnp.where(line_valid, rel_upper, -1e30).astype(bf16)
    q_aug = jnp.concatenate([q_all * jnp.asarray(HD**-0.5, bf16), rel_upper, rel_lower], axis=-1)
    expand_all = jnp.broadcast_to(expand, (group_heads,) + expand.shape)
    k_aug = jnp.concatenate([key_all, expand_all, expand_all], axis=-1)
    v_aug = jnp.concatenate(
        [
            value_all.swapaxes(1, 2),
            jnp.ones((group_heads, 1, cap_tokens), bf16),
            jnp.zeros((group_heads, 15, cap_tokens), bf16),
        ],
        axis=1,
    )
    k_turn = jnp.concatenate([key_all, expand_all], axis=-1).swapaxes(1, 2)
    q_aug, cot_in = lax.optimization_barrier((q_aug, cot_in))
    cot32 = cot_in.astype(f32)
    att_heads, log_sums = attend_forward(q_aug, k_aug, v_aug)

    gathered = lax.all_gather(packed, BOTH, axis=0, tiled=False).reshape(
        group_count, head_groups, pack_rows, model_width
    )
    proj_turn = (
        gathered[:, :, up_height + out_cols :]
        .reshape(group_count, head_groups, out_cols, group_width)
        .transpose(0, 2, 1, 3)
        .reshape(model_width, model_width)
    )

    att_back = lax.all_to_all(
        att_heads.reshape(group_count, head_groups, block_len, 1, group_width),
        "ha",
        split_axis=1,
        concat_axis=3,
        tiled=True,
    )
    att_tok = att_back.reshape(local_tokens, model_width)
    branch = contract_cols(att_tok, proj_turn) + proj_shift.astype(f32)
    middle = tokens32 + tok_mask * branch
    steps = hidden_width // model_width
    if out_cols % 16 == 0 and up_cols % 128 == 0 and up_height == out_cols and steps == head_groups:
        norm_vectors = jnp.stack([proj_shift, second_gain, second_shift, down_shift]).astype(f32)
        (
            block_out,
            mid_total,
            branch_grad,
            small_sums,
            up_bias_grad,
            up_packed,
            down_packed,
        ) = feed_forward(
            middle,
            cot_in,
            tok_mask,
            norm_vectors,
            up_shift.astype(f32).reshape(steps, 1, model_width),
            gathered,
            up_height,
            up_cols,
            out_cols,
        )
        up_bias_grad = up_bias_grad.reshape(-1)
        proj_bias_grad, second_gain_grad, second_shift_grad, down_bias_grad = small_sums
    else:
        up_full = (
            unpack_up(gathered[:, :, :up_height], up_rows, up_cols)
            .transpose(1, 2, 0, 3)
            .reshape(model_width, hidden_width)
        )
        down_turn = (
            gathered[:, :, up_height : up_height + out_cols]
            .transpose(0, 2, 1, 3)
            .reshape(model_width, hidden_width)
        )
        normed2 = layer_norm(middle, second_gain.astype(f32), second_shift.astype(f32)).astype(bf16)
        hidden = jnp.dot(normed2, up_full, preferred_element_type=f32) + up_shift.astype(f32)
        activated = jax.nn.gelu(hidden, approximate=False).astype(bf16)
        block_out = (
            middle + tok_mask * (contract_cols(activated, down_turn) + down_shift.astype(f32))
        ).astype(bf16)
        masked_cot = tok_mask * cot32
        down_in = masked_cot.astype(bf16)
        down_grad = contract_rows(down_in, activated).astype(bf16)
        down_bias_grad = jnp.sum(masked_cot, axis=0)
        act_grad = jnp.dot(down_in, down_turn, preferred_element_type=f32)
        gelu_value, gelu_pull = jax.vjp(partial(jax.nn.gelu, approximate=False), hidden)
        hidden_grad = gelu_pull(act_grad)[0].astype(bf16)
        up_grad = contract_rows(normed2, hidden_grad).astype(bf16)
        up_bias_grad = jnp.sum(hidden_grad.astype(f32), axis=0)
        norm2_in = contract_cols(hidden_grad, up_full)
        norm2_value, norm2_pull = jax.vjp(
            layer_norm, middle, second_gain.astype(f32), second_shift.astype(f32)
        )
        mid_grad, second_gain_grad, second_shift_grad = norm2_pull(norm2_in)
        mid_total = cot32 + mid_grad
        branch_grad = (tok_mask * mid_total).astype(bf16)
        up_packed = pack_up(
            up_grad.reshape(head_groups, up_rows, group_count, up_cols).transpose(2, 0, 1, 3)
        )
        down_packed = down_grad.reshape(group_count, out_cols, head_groups, model_width).transpose(
            0, 2, 1, 3
        )
        proj_bias_grad = jnp.sum(branch_grad.astype(f32), axis=0)

    att_grad_tok = jnp.dot(branch_grad, proj_turn, preferred_element_type=f32).astype(bf16)
    att_grad_tok, branch_turn, up_packed, down_packed = lax.optimization_barrier(
        (att_grad_tok, branch_grad, up_packed, down_packed)
    )
    att_grad = lax.all_to_all(
        att_grad_tok.reshape(group_count, 1, block_len, head_groups, group_width),
        "ha",
        split_axis=3,
        concat_axis=1,
        tiled=True,
    ).reshape(cap_tokens, group_width)
    att_grad, block_out = lax.optimization_barrier((att_grad, block_out))
    out_back = exchange(block_out.reshape(group_count, block_len, model_width), "ga")

    proj_grad = contract_rows(branch_turn, att_tok).astype(bf16)
    grads_packed = jnp.concatenate(
        [
            up_packed,
            down_packed,
            proj_grad.reshape(group_count, out_cols, head_groups, group_width)
            .transpose(0, 2, 1, 3)
            .reshape(group_count, head_groups, out_cols // head_groups, model_width),
        ],
        axis=2,
    ).reshape(device_count * pack_rows, model_width)
    grads_own = lax.psum_scatter(grads_packed, BOTH, scatter_dimension=0, tiled=True)
    up_own = unpack_up(grads_own[:up_height], up_rows, up_cols).astype(f32)
    down_own = grads_own[up_height : up_height + out_cols].T.astype(f32)
    proj_own = grads_own[up_height + out_cols :].reshape(out_cols, group_width).T.astype(f32)

    grad_heads = att_grad.reshape(cap_tokens, group_heads, HD)
    delta = (
        jnp.sum(
            grad_heads.astype(f32) * att_heads.reshape(cap_tokens, group_heads, HD).astype(f32),
            axis=-1,
        )
        .transpose(1, 0)
        .reshape(group_heads, 1, cap_tokens)
    )
    query_part, line_sums, key_value_grad = attend_backward(
        q_aug, grad_heads.transpose(1, 0, 2), log_sums, delta, k_aug, value_all, k_turn
    )
    query_part, line_sums, key_value_grad, out_back = lax.optimization_barrier(
        (query_part, line_sums, key_value_grad, out_back)
    )
    lines = line_sums.reshape(group_heads, SMAX, SMAX, 2 * SMAX)
    height_grad = lines[..., :SMAX]
    width_grad = lines[..., SMAX:]
    query_grad = (
        HD**-0.5 * query_part.reshape(group_heads, SMAX, SMAX, HD)
        + jnp.einsum("hrwj,rjd->hrwd", height_grad, table_h, preferred_element_type=f32)
        + jnp.einsum("hrwj,wjd->hrwd", width_grad, table_w, preferred_element_type=f32)
    ).reshape(group_heads, cap_tokens, HD)
    mixed_grad = jnp.concatenate(
        [
            query_grad.astype(bf16).transpose(1, 0, 2).reshape(cap_tokens, group_width),
            key_value_grad,
        ],
        axis=1,
    )
    triple_part = contract_rows(normed_all, mixed_grad).astype(bf16)
    mixed_grad, triple_part, height_grad, width_grad = lax.optimization_barrier(
        (mixed_grad, triple_part, height_grad, width_grad)
    )
    norm1_wide = contract_cols(mixed_grad, triple_own)
    h_table_grad = jnp.einsum("hrwj,hrwd->rjd", height_grad, q_grid, preferred_element_type=f32)
    w_table_grad = jnp.einsum("hrwj,hrwd->wjd", width_grad, q_grid, preferred_element_type=f32)
    norm1_part = (
        norm1_wide.astype(bf16)
        .reshape(group_count, head_groups, block_len, model_width)
        .transpose(1, 0, 2, 3)
        .reshape(head_groups, local_tokens, model_width)
    )
    norm1_in = scatter_heads(norm1_part)
    triple_rows_grad = (
        exchange(triple_part.reshape(head_groups, group_width, 3 * group_width), "ha")
        .reshape(head_groups, group_width, 3, group_width)
        .transpose(1, 2, 0, 3)
        .reshape(group_width, group_count, 3 * model_width // group_count)
        .transpose(1, 0, 2)
    )
    triple_grad = jnp.sum(exchange(triple_rows_grad, "ga").astype(f32), axis=0)

    center = tokens_all - jnp.mean(tokens_all, axis=-1, keepdims=True)
    unit = center * lax.rsqrt(jnp.mean(center * center, axis=-1, keepdims=True) + 1e-06)
    first_gain_grad = jnp.sum(norm1_wide * unit, axis=0)
    first_shift_grad = jnp.sum(norm1_wide, axis=0)
    mixed_float = mixed_grad.astype(f32)
    height_rel = jnp.einsum("qkj,qkd->jd", matrix, h_table_grad, precision=exact_mode)
    width_rel = jnp.einsum("qkj,qkd->jd", matrix, w_table_grad, precision=exact_mode)
    rel_flat = jnp.concatenate([height_rel, width_rel]).reshape(-1)
    rel_size = rel_flat.shape[0]
    grouped = [
        first_gain_grad,
        first_shift_grad,
        proj_bias_grad,
        second_gain_grad,
        second_shift_grad,
        down_bias_grad,
        up_bias_grad,
    ]
    small = jnp.concatenate(
        [vector.reshape(head_groups, -1) for vector in grouped]
        + [rel_flat.reshape(head_groups, -1)],
        axis=1,
    )
    small = small + swap(small, 1)
    small = small + swap(small, 2)
    own_part = lax.dynamic_index_in_dim(small, head_index, 0, False)
    own_size = own_part.shape[0] - rel_size // head_groups
    last_part = jnp.concatenate(
        [
            own_part[:own_size],
            jnp.sum(mixed_float[:, :group_width], axis=0),
            jnp.sum(mixed_float[:, 2 * group_width :], axis=0),
            small[:, own_size:].reshape(-1),
        ]
    )
    last_size = last_part.shape[0]
    last_part = jnp.pad(last_part, (0, -last_size % 128)).reshape(-1, 128)
    last_sum = jnp.sum(spread(last_part, "ga"), axis=0).reshape(-1)[:last_size]
    rel_sum = last_sum[last_size - rel_size :].reshape(2, 2 * SMAX - 1, HD)
    late = []
    at = 0
    for size in [group_width] * 6 + [hidden_width // head_groups] + [group_width] * 2:
        late.append(last_sum[at : at + size])
        at += size

    norm1_value, norm1_pull = jax.vjp(lambda tokens: layer_norm(tokens, gain32, shift32), tokens32)
    input_grad = (mid_total + norm1_pull(norm1_in)[0]).astype(bf16)
    in_back = exchange(input_grad.reshape(group_count, block_len, model_width), "ga")
    return (
        out_back,
        in_back,
        late[0],
        late[1],
        triple_grad,
        late[7],
        late[8],
        proj_own,
        late[2],
        late[3],
        late[4],
        up_own,
        late[6],
        down_own,
        late[5],
        rel_sum[0],
        rel_sum[1],
    )


def solution(mesh):
    placed = (
        P(None, ("ga", "ha"), None),
        P(None, ("ga", "ha"), None),
        P(),
        P("ha"),
        P("ha"),
        P("ha", "ga"),
        P("ha"),
        P("ha"),
        P("ha", "ga"),
        P("ha"),
        P("ha"),
        P("ha"),
        P("ha", "ga"),
        P("ha"),
        P("ha", "ga"),
        P("ha"),
        P(),
        P(),
    )
    return jax.shard_map(
        local,
        mesh=mesh,
        in_specs=placed,
        out_specs=(
            P(None, ("ga", "ha"), None),
            P(None, ("ga", "ha"), None),
            P("ha"),
            P("ha"),
            P("ha", "ga"),
            P("ha"),
            P("ha"),
            P("ha", "ga"),
            P("ha"),
            P("ha"),
            P("ha"),
            P("ha", "ga"),
            P("ha"),
            P("ha", "ga"),
            P("ha"),
            P(),
            P(),
        ),
        check_vma=False,
    )
```

```python
from functools import partial

import jax
import jax.numpy as jnp
from jax import lax
from jax.experimental import pallas as pl
from jax.experimental.pallas import tpu as pltpu
from jax.sharding import PartitionSpec as P

HEADS = 12
HD = 64
SMAX = 48
BOTH = ("ga", "ha")


exact_mode = lax.Precision.HIGHEST


TBLK = 256
UBLK = 768

NT = (((1,), (1,)), ((), ()))


def mm(left, right):
    return jnp.dot(left, right, preferred_element_type=jnp.float32)


def mm_nt(left, right):
    return lax.dot_general(left, right, NT, preferred_element_type=jnp.float32)


def query_rows(mixed_ref, rel_ref, head):
    start = pl.multiple_of(pl.program_id(0) * TBLK, TBLK)
    rows = mixed_ref[pl.ds(start, TBLK), head * HD : (head + 1) * HD]
    return jnp.concatenate([rows * jnp.asarray(HD**-0.5, rows.dtype), rel_ref[head]], axis=1)


def forward_kernel(mixed_ref, rel_ref, lines_ref, out_ref, lse_ref, k_ref, v_ref):
    heads = rel_ref.shape[0]
    tokens = mixed_ref.shape[0]
    width = heads * HD
    bf16 = jnp.bfloat16

    @pl.when(pl.program_id(0) == 0)
    def _():
        lines = lines_ref[...]
        for h in range(heads):
            keys = mixed_ref[:, width + h * HD : width + (h + 1) * HD]
            values = mixed_ref[:, 2 * width + h * HD : 2 * width + (h + 1) * HD]
            k_ref[h] = jnp.concatenate([keys, lines, lines], axis=1)
            v_ref[h, :HD] = values.T
            v_ref[h, HD:] = jnp.ones((16, tokens), bf16)

    outs = []
    for h in range(heads):
        scores = mm_nt(k_ref[h], query_rows(mixed_ref, rel_ref, h))
        top = jnp.max(scores, axis=0, keepdims=True)
        expo = jnp.exp(scores - top).astype(bf16)
        mixed = mm(v_ref[h], expo)
        total = mixed[HD : HD + 1]
        outs.append((mixed[:HD] / total).T.astype(bf16))
        lse_ref[h] = top + jnp.log(total)
    out_ref[...] = jnp.concatenate(outs, axis=1)


def attend_forward(mixed, rel, lines):
    heads, tokens, depth = rel.shape
    return pl.pallas_call(
        forward_kernel,
        grid=(tokens // TBLK,),
        in_specs=[
            pl.BlockSpec(mixed.shape, lambda t: (0, 0)),
            pl.BlockSpec((heads, TBLK, depth), lambda t: (0, t, 0)),
            pl.BlockSpec(lines.shape, lambda t: (0, 0)),
        ],
        out_specs=[
            pl.BlockSpec((TBLK, heads * HD), lambda t: (t, 0)),
            pl.BlockSpec((heads, 1, TBLK), lambda t: (0, 0, t)),
        ],
        out_shape=[
            jax.ShapeDtypeStruct((tokens, heads * HD), jnp.bfloat16),
            jax.ShapeDtypeStruct((heads, 1, tokens), jnp.float32),
        ],
        scratch_shapes=[
            pltpu.VMEM((heads, tokens, HD + depth), jnp.bfloat16),
            pltpu.VMEM((heads, HD + 16, tokens), jnp.bfloat16),
        ],
        name="attend_forward",
        compiler_params=pltpu.CompilerParams(dimension_semantics=("arbitrary",)),
    )(mixed, rel, lines)


def backward_kernel(
    mixed_ref,
    rel_ref,
    lines_ref,
    g_ref,
    att_ref,
    lse_ref,
    dq_ref,
    rows_ref,
    cols_ref,
    out_ref,
    dkv_ref,
    k_ref,
    v_ref,
    kt_ref,
):
    heads = rel_ref.shape[0]
    tokens = mixed_ref.shape[0]
    width = heads * HD
    bf16 = jnp.bfloat16
    f32 = jnp.float32

    @pl.when(pl.program_id(0) == 0)
    def _():
        dkv_ref[...] = jnp.zeros_like(dkv_ref)
        lines = lines_ref[...]
        for h in range(heads):
            keys = mixed_ref[:, width + h * HD : width + (h + 1) * HD]
            k_ref[h] = jnp.concatenate([keys, lines, lines], axis=1)
            v_ref[h] = mixed_ref[:, 2 * width + h * HD : 2 * width + (h + 1) * HD]
            kt_ref[h] = jnp.concatenate([keys, lines], axis=1).T

    zero = jnp.zeros((TBLK, HD), bf16)
    query_grads = []
    for h in range(heads):
        q_here = query_rows(mixed_ref, rel_ref, h)
        g_here = g_ref[:, h * HD : (h + 1) * HD]
        weighed = g_here.astype(f32) * att_ref[:, h * HD : (h + 1) * HD].astype(f32)
        delta = jnp.sum(weighed.T, axis=0, keepdims=True)
        g_wide = jnp.concatenate([g_here, zero], axis=1)
        q_wide = jnp.concatenate([zero, q_here[:, :HD]], axis=1)
        lse = lse_ref[h]
        total = None
        for c in range(tokens // UBLK):
            span = pl.ds(c * UBLK, UBLK)
            scores = mm_nt(k_ref[h, span, :], q_here)
            probs = jnp.exp(scores - lse)
            pgrad = mm_nt(v_ref[h, span, :], g_here)
            sgrad = (probs * (pgrad - delta)).astype(bf16)
            dkv_ref[h, span, :] += mm(probs.astype(bf16), g_wide) + mm(sgrad, q_wide)
            part = mm(kt_ref[h, :, span], sgrad)
            total = part if total is None else total + part
        query_grads.append(total[:HD].T)
        rows_ref[h] = total[HD : HD + SMAX].T.astype(bf16)
        cols_ref[h] = total[HD + SMAX :].T.astype(bf16)
    dq_ref[...] = HD**-0.5 * jnp.concatenate(query_grads, axis=1)

    @pl.when(pl.program_id(0) == pl.num_programs(0) - 1)
    def _():
        keys = [dkv_ref[h, :, HD:] for h in range(heads)]
        values = [dkv_ref[h, :, :HD] for h in range(heads)]
        out_ref[...] = jnp.concatenate(keys + values, axis=1).astype(bf16)


def attend_backward(mixed, rel, lines, grads, attended, lse):
    heads, tokens, depth = rel.shape
    width = heads * HD
    return pl.pallas_call(
        backward_kernel,
        grid=(tokens // TBLK,),
        in_specs=[
            pl.BlockSpec(mixed.shape, lambda t: (0, 0)),
            pl.BlockSpec((heads, TBLK, depth), lambda t: (0, t, 0)),
            pl.BlockSpec(lines.shape, lambda t: (0, 0)),
            pl.BlockSpec((TBLK, width), lambda t: (t, 0)),
            pl.BlockSpec((TBLK, width), lambda t: (t, 0)),
            pl.BlockSpec((heads, 1, TBLK), lambda t: (0, 0, t)),
        ],
        out_specs=[
            pl.BlockSpec((TBLK, width), lambda t: (t, 0)),
            pl.BlockSpec((heads, TBLK, SMAX), lambda t: (0, t, 0)),
            pl.BlockSpec((heads, TBLK, SMAX), lambda t: (0, t, 0)),
            pl.BlockSpec((tokens, 2 * width), lambda t: (0, 0)),
        ],
        out_shape=[
            jax.ShapeDtypeStruct((tokens, width), jnp.float32),
            jax.ShapeDtypeStruct((heads, tokens, SMAX), jnp.bfloat16),
            jax.ShapeDtypeStruct((heads, tokens, SMAX), jnp.bfloat16),
            jax.ShapeDtypeStruct((tokens, 2 * width), jnp.bfloat16),
        ],
        scratch_shapes=[
            pltpu.VMEM((heads, tokens, 2 * HD), jnp.float32),
            pltpu.VMEM((heads, tokens, HD + depth), jnp.bfloat16),
            pltpu.VMEM((heads, tokens, HD), jnp.bfloat16),
            pltpu.VMEM((heads, HD + 2 * SMAX, tokens), jnp.bfloat16),
        ],
        name="attend_backward",
        compiler_params=pltpu.CompilerParams(dimension_semantics=("arbitrary",)),
    )(mixed, rel, lines, grads, attended, lse)


def norm_parts(values):
    center = values - jnp.mean(values, axis=-1, keepdims=True)
    scale = lax.rsqrt(jnp.mean(center * center, axis=-1, keepdims=True) + 1e-06)
    return center * scale, scale


def feed_kernel(
    mid_ref,
    cot_ref,
    mask_ref,
    vec_ref,
    shift_ref,
    up_ref,
    down_ref,
    out_ref,
    total_ref,
    branch_ref,
    sums_ref,
    up_bias_ref,
    up_grad_ref,
    down_grad_ref,
    normed_ref,
    turned_ref,
    down_in_ref,
    down_turn_ref,
    out_acc_ref,
    in_acc_ref,
    weight_ref,
):
    f32 = jnp.float32
    bf16 = jnp.bfloat16
    step = pl.program_id(0)
    groups, heads, height, width = up_ref.shape
    cols = weight_ref.shape[1] // groups
    folds = width // cols
    rows = height * folds
    pieces, _, out_cols, _ = down_ref.shape

    @pl.when(step == 0)
    def _():
        unit, _ = norm_parts(mid_ref[...])
        normed = (unit * vec_ref[1:2] + vec_ref[2:3]).astype(bf16)
        normed_ref[...] = normed
        turned_ref[...] = normed.T
        masked = mask_ref[...] * cot_ref[...].astype(f32)
        down_in_ref[...] = masked.astype(bf16)
        down_turn_ref[...] = masked.astype(bf16).T
        out_acc_ref[...] = jnp.zeros_like(out_acc_ref)
        in_acc_ref[...] = jnp.zeros_like(in_acc_ref)

    for g in range(groups):
        for h in range(heads):
            for s in range(folds):
                top = h * rows + s * height
                weight_ref[top : top + height, g * cols : (g + 1) * cols] = up_ref[
                    g, h, :, s * cols : (s + 1) * cols
                ]
    weight = weight_ref[...]
    down = down_ref[...].reshape(pieces * out_cols, width)
    hidden = mm(normed_ref[...], weight) + shift_ref[0]
    share = 0.5 * (1.0 + lax.erf(hidden * (0.5**0.5)))
    active = (hidden * share).astype(bf16)
    slope = share + hidden * jnp.exp(-0.5 * hidden * hidden) * 0.3989422804014327
    out_acc_ref[...] += mm_nt(active, down)
    hidden_grad = (mm(down_in_ref[...], down) * slope).astype(bf16)
    down_grad_ref[...] = (
        mm(down_turn_ref[...], active).astype(bf16).reshape(pieces, 1, out_cols, width)
    )
    in_acc_ref[...] += mm_nt(hidden_grad, weight)
    up_bias_ref[0] = jnp.sum(hidden_grad.astype(f32), axis=0, keepdims=True)
    up_grad = mm(turned_ref[...], hidden_grad).astype(bf16)
    for g in range(groups):
        for h in range(heads):
            for s in range(folds):
                top = h * rows + s * height
                up_grad_ref[g, h, :, s * cols : (s + 1) * cols] = up_grad[
                    top : top + height, g * cols : (g + 1) * cols
                ]

    @pl.when(step == pl.num_programs(0) - 1)
    def _():
        middle = mid_ref[...]
        mask = mask_ref[...]
        cot = cot_ref[...].astype(f32)
        out_ref[...] = (middle + mask * (out_acc_ref[...] + vec_ref[3:4])).astype(bf16)
        unit, scale = norm_parts(middle)
        grad_in = in_acc_ref[...]
        inner = grad_in * vec_ref[1:2]
        total = cot + scale * (
            inner
            - jnp.mean(inner, axis=-1, keepdims=True)
            - unit * jnp.mean(inner * unit, axis=-1, keepdims=True)
        )
        branch = (mask * total).astype(bf16)
        total_ref[...] = total
        branch_ref[...] = branch
        sums_ref[...] = jnp.concatenate(
            [
                jnp.sum(branch.astype(f32), axis=0, keepdims=True),
                jnp.sum(grad_in * unit, axis=0, keepdims=True),
                jnp.sum(grad_in, axis=0, keepdims=True),
                jnp.sum(mask * cot, axis=0, keepdims=True),
            ],
            axis=0,
        )


def feed_forward(middle, cot, mask, vectors, shift, gathered, up_height, up_cols, out_cols):
    tokens, width = middle.shape
    groups, heads = gathered.shape[:2]
    steps = shift.shape[0]
    per_step = groups // steps
    f32 = jnp.float32
    bf16 = jnp.bfloat16

    def whole(rows, cols):
        return pl.BlockSpec((rows, cols), lambda c: (0, 0))

    up_spec = (per_step, heads, up_height, width)
    down_spec = (groups, 1, out_cols, width)
    return pl.pallas_call(
        feed_kernel,
        grid=(steps,),
        in_specs=[
            whole(tokens, width),
            whole(tokens, width),
            whole(tokens, 1),
            whole(vectors.shape[0], width),
            pl.BlockSpec((1, 1, width), lambda c: (c, 0, 0)),
            pl.BlockSpec(up_spec, lambda c: (c, 0, 0, 0)),
            pl.BlockSpec(down_spec, lambda c: (0, c, 1, 0)),
        ],
        out_specs=[
            whole(tokens, width),
            whole(tokens, width),
            whole(tokens, width),
            whole(4, width),
            pl.BlockSpec((1, 1, width), lambda c: (c, 0, 0)),
            pl.BlockSpec(up_spec, lambda c: (c, 0, 0, 0)),
            pl.BlockSpec(down_spec, lambda c: (0, c, 0, 0)),
        ],
        out_shape=[
            jax.ShapeDtypeStruct((tokens, width), bf16),
            jax.ShapeDtypeStruct((tokens, width), f32),
            jax.ShapeDtypeStruct((tokens, width), bf16),
            jax.ShapeDtypeStruct((4, width), f32),
            jax.ShapeDtypeStruct((steps, 1, width), f32),
            jax.ShapeDtypeStruct((groups, heads, up_height, width), bf16),
            jax.ShapeDtypeStruct((groups, heads, out_cols, width), bf16),
        ],
        scratch_shapes=[
            pltpu.VMEM((tokens, width), bf16),
            pltpu.VMEM((width, tokens), bf16),
            pltpu.VMEM((tokens, width), bf16),
            pltpu.VMEM((width, tokens), bf16),
            pltpu.VMEM((tokens, width), f32),
            pltpu.VMEM((tokens, width), f32),
            pltpu.VMEM((width, width), bf16),
        ],
        name="feed_forward",
        compiler_params=pltpu.CompilerParams(dimension_semantics=("arbitrary",)),
    )(middle, cot, mask, vectors, shift, gathered, gathered)


def layer_norm(values, gain, shift):
    center = values - jnp.mean(values, axis=-1, keepdims=True)
    spread = jnp.mean(center * center, axis=-1, keepdims=True)
    return center * lax.rsqrt(spread + 1e-06) * gain + shift


def interp_matrix(img_side):
    coord = jnp.arange(SMAX, dtype=jnp.int32)
    length_in = 2 * SMAX - 1
    length_out = 2 * img_side - 1
    offset = jnp.clip(coord[:, None] - coord[None, :] + img_side - 1, 0, length_out - 1)
    numer = jnp.maximum((2 * offset + 1) * length_in - length_out, 0)
    lower = numer // (2 * length_out)
    weight_hi = (numer - lower * 2 * length_out).astype(jnp.float32) / (2 * length_out).astype(
        jnp.float32
    )
    upper = jnp.minimum(lower + 1, length_in - 1)
    target = jnp.arange(length_in, dtype=jnp.int32)
    lower_hot = (target == lower[..., None]).astype(jnp.float32)
    upper_hot = (target == upper[..., None]).astype(jnp.float32)
    return (1.0 - weight_hi)[..., None] * lower_hot + weight_hi[..., None] * upper_hot


def contract_rows(left, right):
    return lax.dot_general(
        left, right, (((0,), (0,)), ((), ())), preferred_element_type=jnp.float32
    )


def contract_cols(left, right):
    return lax.dot_general(
        left, right, (((1,), (1,)), ((), ())), preferred_element_type=jnp.float32
    )


def exchange(values, axis):
    return lax.all_to_all(values, axis, split_axis=0, concat_axis=0, tiled=True)


def spread(values, axis):
    count = lax.axis_size(axis)
    return exchange(jnp.broadcast_to(values, (count,) + values.shape), axis)


def swap(values, step):
    pairs = [(i, i ^ step) for i in range(lax.axis_size("ha"))]
    return lax.ppermute(values, "ha", pairs)


def gather_heads(values, beside):
    me = lax.axis_index("ha")
    far = swap(values, 2)
    near = swap(values, 1)
    far, near, beside = lax.optimization_barrier((far, near, beside))
    corner = swap(far, 1)
    blocks = jnp.stack([values, near, far, corner])
    ordered = [
        lax.dynamic_index_in_dim(blocks, jnp.bitwise_xor(me, i), 0, False) for i in range(4)
    ]
    return ordered, beside


def scatter_heads(parts):
    me = lax.axis_index("ha")
    other = [lax.dynamic_index_in_dim(parts, jnp.bitwise_xor(me, i), 0, False) for i in range(4)]
    arrived = swap(jnp.stack([other[3], other[1]]), 1).astype(jnp.float32)
    far = (other[2].astype(jnp.float32) + arrived[0]).astype(jnp.bfloat16)
    near = other[0].astype(jnp.float32) + arrived[1]
    return near + swap(far, 2).astype(jnp.float32)


def pack_up(piece):
    rows, width = piece.shape[-2:]
    lead = piece.shape[:-2]
    fold = 4 * rows // width
    cut = piece.reshape(lead + (fold, rows // fold, width))
    return jnp.swapaxes(cut, -3, -2).reshape(lead + (rows // fold, fold * width))


def unpack_up(packed, rows, width):
    fold = packed.shape[-1] // width
    lead = packed.shape[:-2]
    cut = packed.reshape(lead + (rows // fold, fold, width))
    return jnp.swapaxes(cut, -3, -2).reshape(lead + (rows, width))


def local(
    patches,
    cotangent,
    sides,
    norm1_gain,
    norm1_bias,
    qkv_weight,
    query_bias,
    value_bias,
    proj_weight,
    proj_bias,
    norm2_gain,
    norm2_bias,
    fc1_weight,
    fc1_bias,
    fc2_weight,
    fc2_bias,
    rel_height,
    rel_width,
):
    group_count = lax.axis_size("ga")
    head_groups = lax.axis_size("ha")
    group_index = lax.axis_index("ga")
    head_index = lax.axis_index("ha")
    device_count = group_count * head_groups
    block_len = patches.shape[1]
    model_width = patches.shape[2]
    hidden_width = fc1_bias.shape[0] * head_groups
    local_tokens = group_count * block_len
    group_width = model_width // head_groups
    group_heads = HEADS // head_groups
    cap_tokens = SMAX * SMAX
    f32 = jnp.float32
    bf16 = jnp.bfloat16

    triple_rows = lax.all_gather(qkv_weight, "ga", axis=1, tiled=True)
    up_rows, up_cols = fc1_weight.shape
    out_cols = fc2_weight.shape[1]
    packed = jnp.concatenate(
        [
            pack_up(fc1_weight),
            fc2_weight.T,
            proj_weight.T.reshape(out_cols // head_groups, model_width),
        ],
        axis=0,
    )
    pack_rows = packed.shape[0]
    up_height = up_rows * up_cols // model_width

    vectors = jnp.concatenate(
        [norm1_gain, norm1_bias, proj_bias, norm2_gain, norm2_bias, fc2_bias, fc1_bias]
    )
    vectors_all = lax.all_gather(vectors, "ha", axis=0, tiled=False)
    tokens_in = lax.all_to_all(patches, "ga", split_axis=0, concat_axis=1, tiled=True)[0]
    tokens_in, triple_rows, vectors_all, packed = lax.optimization_barrier(
        (tokens_in, triple_rows, vectors_all, packed)
    )
    cot_in = lax.all_to_all(cotangent, "ga", split_axis=0, concat_axis=1, tiled=True)[0]
    wide = model_width // head_groups

    def vector_at(slot, width):
        return vectors_all[:, slot * wide : slot * wide + width].reshape(-1)

    first_gain = vector_at(0, wide)
    first_shift = vector_at(1, wide)
    proj_shift = vector_at(2, wide)
    second_gain = vector_at(3, wide)
    second_shift = vector_at(4, wide)
    down_shift = vector_at(5, wide)
    up_shift = vector_at(6, 4 * wide)

    triple_cut = triple_rows.reshape(group_width, 3, head_groups, group_width).transpose(2, 0, 1, 3)
    triple_own = exchange(
        triple_cut.reshape(head_groups, group_width, 3 * group_width), "ha"
    ).reshape(model_width, 3 * group_width)
    tokens32 = tokens_in.astype(f32)
    slot_index = jnp.arange(local_tokens, dtype=jnp.int32)
    grid_index = (
        slot_index // block_len * head_groups + head_index
    ) * block_len + slot_index % block_len
    img_side = lax.dynamic_index_in_dim(sides, group_index, 0, keepdims=False)
    tok_mask = ((grid_index // SMAX < img_side) & (grid_index % SMAX < img_side)).astype(f32)[
        :, None
    ]
    all_index = jnp.arange(cap_tokens, dtype=jnp.int32)[:, None]
    line_index = jnp.arange(2 * SMAX, dtype=jnp.int32)[None, :]
    expand = jnp.where(
        line_index < SMAX,
        all_index // SMAX == line_index,
        all_index % SMAX == line_index - SMAX,
    ).astype(bf16)
    line_valid = line_index[0] % SMAX < img_side
    matrix = interp_matrix(img_side)
    table_h = jnp.einsum(
        "qkj,jd->qkd", matrix, rel_height.astype(f32), precision=exact_mode
    ).astype(bf16)
    table_w = jnp.einsum("qkj,jd->qkd", matrix, rel_width.astype(f32), precision=exact_mode).astype(
        bf16
    )

    blocks_all, triple_own = gather_heads(tokens_in, triple_own)
    tokens_all = (
        jnp.stack(
            [block.reshape(group_count, block_len, model_width) for block in blocks_all],
            axis=1,
        )
        .reshape(cap_tokens, model_width)
        .astype(f32)
    )
    gain32 = first_gain.astype(f32)
    shift32 = first_shift.astype(f32)
    normed_all = layer_norm(tokens_all, gain32, shift32).astype(bf16)
    bias_own = jnp.concatenate([query_bias, jnp.zeros_like(query_bias), value_bias]).astype(f32)
    mixed = (jnp.dot(normed_all, triple_own, preferred_element_type=f32) + bias_own).astype(bf16)
    q_grid = (
        mixed[:, :group_width].reshape(SMAX, SMAX, group_heads, HD).transpose(2, 0, 1, 3)
    )
    rel_h = jnp.einsum("hrwd,rkd->hrwk", q_grid, table_h, preferred_element_type=f32)
    rel_w = jnp.einsum("hrwd,wkd->hrwk", q_grid, table_w, preferred_element_type=f32)
    rel_both = jnp.concatenate([rel_h, rel_w], axis=-1).reshape(
        group_heads, cap_tokens, 2 * SMAX
    )
    rel_upper = lax.reduce_precision(rel_both, 8, 7)
    rel_lower = jnp.where(line_valid, rel_both - rel_upper, 0.0).astype(bf16)
    rel_upper = jnp.where(line_valid, rel_upper, -1e30).astype(bf16)
    rel_split = jnp.concatenate([rel_upper, rel_lower], axis=-1)
    rel_split, cot_in = lax.optimization_barrier((rel_split, cot_in))
    cot32 = cot_in.astype(f32)
    att_heads, log_sums = attend_forward(mixed, rel_split, expand)

    gathered = lax.all_gather(packed, BOTH, axis=0, tiled=False)
    att_heads, gathered = lax.optimization_barrier((att_heads, gathered))
    gathered = gathered.reshape(group_count, head_groups, pack_rows, model_width)
    proj_turn = (
        gathered[:, :, up_height + out_cols :]
        .reshape(group_count, head_groups, out_cols, group_width)
        .transpose(0, 2, 1, 3)
        .reshape(model_width, model_width)
    )

    att_back = lax.all_to_all(
        att_heads.reshape(group_count, head_groups, block_len, 1, group_width),
        "ha",
        split_axis=1,
        concat_axis=3,
        tiled=True,
    )
    att_tok = att_back.reshape(local_tokens, model_width)
    branch = contract_cols(att_tok, proj_turn) + proj_shift.astype(f32)
    middle = tokens32 + tok_mask * branch
    steps = hidden_width // model_width
    if out_cols % 16 == 0 and up_cols % 128 == 0 and up_height == out_cols and steps == head_groups:
        norm_vectors = jnp.stack([proj_shift, second_gain, second_shift, down_shift]).astype(f32)
        (
            block_out,
            mid_total,
            branch_grad,
            small_sums,
            up_bias_grad,
            up_packed,
            down_packed,
        ) = feed_forward(
            middle,
            cot_in,
            tok_mask,
            norm_vectors,
            up_shift.astype(f32).reshape(steps, 1, model_width),
            gathered,
            up_height,
            up_cols,
            out_cols,
        )
        up_bias_grad = up_bias_grad.reshape(-1)
        proj_bias_grad, second_gain_grad, second_shift_grad, down_bias_grad = small_sums
    else:
        up_full = (
            unpack_up(gathered[:, :, :up_height], up_rows, up_cols)
            .transpose(1, 2, 0, 3)
            .reshape(model_width, hidden_width)
        )
        down_turn = (
            gathered[:, :, up_height : up_height + out_cols]
            .transpose(0, 2, 1, 3)
            .reshape(model_width, hidden_width)
        )
        normed2 = layer_norm(middle, second_gain.astype(f32), second_shift.astype(f32)).astype(bf16)
        hidden = jnp.dot(normed2, up_full, preferred_element_type=f32) + up_shift.astype(f32)
        activated = jax.nn.gelu(hidden, approximate=False).astype(bf16)
        block_out = (
            middle + tok_mask * (contract_cols(activated, down_turn) + down_shift.astype(f32))
        ).astype(bf16)
        masked_cot = tok_mask * cot32
        down_in = masked_cot.astype(bf16)
        down_grad = contract_rows(down_in, activated).astype(bf16)
        down_bias_grad = jnp.sum(masked_cot, axis=0)
        act_grad = jnp.dot(down_in, down_turn, preferred_element_type=f32)
        gelu_value, gelu_pull = jax.vjp(partial(jax.nn.gelu, approximate=False), hidden)
        hidden_grad = gelu_pull(act_grad)[0].astype(bf16)
        up_grad = contract_rows(normed2, hidden_grad).astype(bf16)
        up_bias_grad = jnp.sum(hidden_grad.astype(f32), axis=0)
        norm2_in = contract_cols(hidden_grad, up_full)
        norm2_value, norm2_pull = jax.vjp(
            layer_norm, middle, second_gain.astype(f32), second_shift.astype(f32)
        )
        mid_grad, second_gain_grad, second_shift_grad = norm2_pull(norm2_in)
        mid_total = cot32 + mid_grad
        branch_grad = (tok_mask * mid_total).astype(bf16)
        up_packed = pack_up(
            up_grad.reshape(head_groups, up_rows, group_count, up_cols).transpose(2, 0, 1, 3)
        )
        down_packed = down_grad.reshape(group_count, out_cols, head_groups, model_width).transpose(
            0, 2, 1, 3
        )
        proj_bias_grad = jnp.sum(branch_grad.astype(f32), axis=0)

    att_grad_tok = jnp.dot(branch_grad, proj_turn, preferred_element_type=f32).astype(bf16)
    att_grad_tok, branch_turn, up_packed, down_packed = lax.optimization_barrier(
        (att_grad_tok, branch_grad, up_packed, down_packed)
    )
    att_grad = lax.all_to_all(
        att_grad_tok.reshape(group_count, 1, block_len, head_groups, group_width),
        "ha",
        split_axis=3,
        concat_axis=1,
        tiled=True,
    ).reshape(cap_tokens, group_width)
    att_grad, block_out = lax.optimization_barrier((att_grad, block_out))
    out_back = exchange(block_out.reshape(group_count, block_len, model_width), "ga")

    proj_grad = contract_rows(branch_turn, att_tok).astype(bf16)
    grads_packed = jnp.concatenate(
        [
            up_packed,
            down_packed,
            proj_grad.reshape(group_count, out_cols, head_groups, group_width)
            .transpose(0, 2, 1, 3)
            .reshape(group_count, head_groups, out_cols // head_groups, model_width),
        ],
        axis=2,
    ).reshape(device_count * pack_rows, model_width)
    grads_own = lax.psum_scatter(grads_packed, BOTH, scatter_dimension=0, tiled=True)
    up_own = unpack_up(grads_own[:up_height], up_rows, up_cols).astype(f32)
    down_own = grads_own[up_height : up_height + out_cols].T.astype(f32)
    proj_own = grads_own[up_height + out_cols :].reshape(out_cols, group_width).T.astype(f32)

    query_part, height_grad, width_grad, key_value_grad = attend_backward(
        mixed, rel_split, expand, att_grad, att_heads, log_sums
    )
    query_part, height_grad, width_grad, key_value_grad, out_back = lax.optimization_barrier(
        (query_part, height_grad, width_grad, key_value_grad, out_back)
    )
    height_grad = height_grad.reshape(group_heads, SMAX, SMAX, SMAX)
    width_grad = width_grad.reshape(group_heads, SMAX, SMAX, SMAX)
    query_grad = (
        query_part
        + jnp.einsum(
            "hrwj,rjd->rwhd", height_grad, table_h, preferred_element_type=f32
        ).reshape(cap_tokens, group_width)
        + jnp.einsum(
            "hrwj,wjd->rwhd", width_grad, table_w, preferred_element_type=f32
        ).reshape(cap_tokens, group_width)
    )
    mixed_grad = jnp.concatenate(
        [
            query_grad.astype(bf16),
            key_value_grad,
        ],
        axis=1,
    )
    triple_part = contract_rows(normed_all, mixed_grad).astype(bf16)
    mixed_grad, triple_part, height_grad, width_grad = lax.optimization_barrier(
        (mixed_grad, triple_part, height_grad, width_grad)
    )
    norm1_wide = contract_cols(mixed_grad, triple_own)
    h_table_grad = jnp.einsum("hrwj,hrwd->rjd", height_grad, q_grid, preferred_element_type=f32)
    w_table_grad = jnp.einsum("hrwj,hrwd->wjd", width_grad, q_grid, preferred_element_type=f32)
    norm1_part = (
        norm1_wide.astype(bf16)
        .reshape(group_count, head_groups, block_len, model_width)
        .transpose(1, 0, 2, 3)
        .reshape(head_groups, local_tokens, model_width)
    )
    norm1_in = scatter_heads(norm1_part)
    triple_rows_grad = (
        exchange(triple_part.reshape(head_groups, group_width, 3 * group_width), "ha")
        .reshape(head_groups, group_width, 3, group_width)
        .transpose(1, 2, 0, 3)
        .reshape(group_width, group_count, 3 * model_width // group_count)
        .transpose(1, 0, 2)
    )
    triple_grad = jnp.sum(exchange(triple_rows_grad, "ga").astype(f32), axis=0)

    center = tokens_all - jnp.mean(tokens_all, axis=-1, keepdims=True)
    unit = center * lax.rsqrt(jnp.mean(center * center, axis=-1, keepdims=True) + 1e-06)
    first_gain_grad = jnp.sum(norm1_wide * unit, axis=0)
    first_shift_grad = jnp.sum(norm1_wide, axis=0)
    mixed_float = mixed_grad.astype(f32)
    height_rel = jnp.einsum("qkj,qkd->jd", matrix, h_table_grad, precision=exact_mode)
    width_rel = jnp.einsum("qkj,qkd->jd", matrix, w_table_grad, precision=exact_mode)
    rel_flat = jnp.concatenate([height_rel, width_rel]).reshape(-1)
    rel_size = rel_flat.shape[0]
    grouped = [
        first_gain_grad,
        first_shift_grad,
        proj_bias_grad,
        second_gain_grad,
        second_shift_grad,
        down_bias_grad,
        up_bias_grad,
    ]
    small = jnp.concatenate(
        [vector.reshape(head_groups, -1) for vector in grouped]
        + [rel_flat.reshape(head_groups, -1)],
        axis=1,
    )
    small = small + swap(small, 1)
    small = small + swap(small, 2)
    own_part = lax.dynamic_index_in_dim(small, head_index, 0, False)
    own_size = own_part.shape[0] - rel_size // head_groups
    last_part = jnp.concatenate(
        [
            own_part[:own_size],
            jnp.sum(mixed_float[:, :group_width], axis=0),
            jnp.sum(mixed_float[:, 2 * group_width :], axis=0),
            small[:, own_size:].reshape(-1),
        ]
    )
    last_size = last_part.shape[0]
    last_part = jnp.pad(last_part, (0, -last_size % 128)).reshape(-1, 128)
    last_sum = jnp.sum(spread(last_part, "ga"), axis=0).reshape(-1)[:last_size]
    rel_sum = last_sum[last_size - rel_size :].reshape(2, 2 * SMAX - 1, HD)
    late = []
    at = 0
    for size in [group_width] * 6 + [hidden_width // head_groups] + [group_width] * 2:
        late.append(last_sum[at : at + size])
        at += size

    norm1_value, norm1_pull = jax.vjp(lambda tokens: layer_norm(tokens, gain32, shift32), tokens32)
    input_grad = (mid_total + norm1_pull(norm1_in)[0]).astype(bf16)
    in_back = exchange(input_grad.reshape(group_count, block_len, model_width), "ga")
    return (
        out_back,
        in_back,
        late[0],
        late[1],
        triple_grad,
        late[7],
        late[8],
        proj_own,
        late[2],
        late[3],
        late[4],
        up_own,
        late[6],
        down_own,
        late[5],
        rel_sum[0],
        rel_sum[1],
    )


def solution(mesh):
    placed = (
        P(None, ("ga", "ha"), None),
        P(None, ("ga", "ha"), None),
        P(),
        P("ha"),
        P("ha"),
        P("ha", "ga"),
        P("ha"),
        P("ha"),
        P("ha", "ga"),
        P("ha"),
        P("ha"),
        P("ha"),
        P("ha", "ga"),
        P("ha"),
        P("ha", "ga"),
        P("ha"),
        P(),
        P(),
    )
    return jax.shard_map(
        local,
        mesh=mesh,
        in_specs=placed,
        out_specs=(
            P(None, ("ga", "ha"), None),
            P(None, ("ga", "ha"), None),
            P("ha"),
            P("ha"),
            P("ha", "ga"),
            P("ha"),
            P("ha"),
            P("ha", "ga"),
            P("ha"),
            P("ha"),
            P("ha"),
            P("ha", "ga"),
            P("ha"),
            P("ha", "ga"),
            P("ha"),
            P(),
            P(),
        ),
        check_vma=False,
    )
```

```python
from functools import partial

import jax
import jax.numpy as jnp
from jax import lax
from jax.experimental import pallas as pl
from jax.experimental.pallas import tpu as pltpu
from jax.sharding import PartitionSpec as P

HEADS = 12
HD = 64
SMAX = 48
BOTH = ("ga", "ha")


exact_mode = lax.Precision.HIGHEST


TBLK = 256
UBLK = 768

NT = (((1,), (1,)), ((), ()))


def mm(left, right):
    return jnp.dot(left, right, preferred_element_type=jnp.float32)


def mm_nt(left, right):
    return lax.dot_general(left, right, NT, preferred_element_type=jnp.float32)


def query_rows(mixed_ref, rel_ref, head):
    start = pl.multiple_of(pl.program_id(0) * TBLK, TBLK)
    rows = mixed_ref[pl.ds(start, TBLK), head * HD : (head + 1) * HD]
    return jnp.concatenate([rows * jnp.asarray(HD**-0.5, rows.dtype), rel_ref[head]], axis=1)


def forward_kernel(mixed_ref, rel_ref, lines_ref, out_ref, lse_ref, k_ref, v_ref):
    heads = rel_ref.shape[0]
    tokens = mixed_ref.shape[0]
    width = heads * HD
    bf16 = jnp.bfloat16

    @pl.when(pl.program_id(0) == 0)
    def _():
        lines = lines_ref[...]
        for h in range(heads):
            keys = mixed_ref[:, width + h * HD : width + (h + 1) * HD]
            values = mixed_ref[:, 2 * width + h * HD : 2 * width + (h + 1) * HD]
            k_ref[h] = jnp.concatenate([keys, lines, lines], axis=1)
            v_ref[h, :HD] = values.T
            v_ref[h, HD:] = jnp.ones((16, tokens), bf16)

    outs = []
    for h in range(heads):
        scores = mm_nt(k_ref[h], query_rows(mixed_ref, rel_ref, h))
        top = jnp.max(scores, axis=0, keepdims=True)
        expo = jnp.exp(scores - top).astype(bf16)
        mixed = mm(v_ref[h], expo)
        total = mixed[HD : HD + 1]
        outs.append((mixed[:HD] / total).T.astype(bf16))
        lse_ref[h] = top + jnp.log(total)
    out_ref[...] = jnp.concatenate(outs, axis=1)


def attend_forward(mixed, rel, lines):
    heads, tokens, depth = rel.shape
    return pl.pallas_call(
        forward_kernel,
        grid=(tokens // TBLK,),
        in_specs=[
            pl.BlockSpec(mixed.shape, lambda t: (0, 0)),
            pl.BlockSpec((heads, TBLK, depth), lambda t: (0, t, 0)),
            pl.BlockSpec(lines.shape, lambda t: (0, 0)),
        ],
        out_specs=[
            pl.BlockSpec((TBLK, heads * HD), lambda t: (t, 0)),
            pl.BlockSpec((heads, 1, TBLK), lambda t: (0, 0, t)),
        ],
        out_shape=[
            jax.ShapeDtypeStruct((tokens, heads * HD), jnp.bfloat16),
            jax.ShapeDtypeStruct((heads, 1, tokens), jnp.float32),
        ],
        scratch_shapes=[
            pltpu.VMEM((heads, tokens, HD + depth), jnp.bfloat16),
            pltpu.VMEM((heads, HD + 16, tokens), jnp.bfloat16),
        ],
        name="attend_forward",
        compiler_params=pltpu.CompilerParams(dimension_semantics=("arbitrary",)),
    )(mixed, rel, lines)


def backward_kernel(
    mixed_ref,
    rel_ref,
    lines_ref,
    g_ref,
    att_ref,
    lse_ref,
    dq_ref,
    rows_ref,
    cols_ref,
    out_ref,
    dkv_ref,
    k_ref,
    v_ref,
    kt_ref,
):
    heads = rel_ref.shape[0]
    tokens = mixed_ref.shape[0]
    width = heads * HD
    bf16 = jnp.bfloat16
    f32 = jnp.float32

    @pl.when(pl.program_id(0) == 0)
    def _():
        dkv_ref[...] = jnp.zeros_like(dkv_ref)
        lines = lines_ref[...]
        for h in range(heads):
            keys = mixed_ref[:, width + h * HD : width + (h + 1) * HD]
            k_ref[h] = jnp.concatenate([keys, lines, lines], axis=1)
            v_ref[h] = mixed_ref[:, 2 * width + h * HD : 2 * width + (h + 1) * HD]
            kt_ref[h] = jnp.concatenate([keys, lines], axis=1).T

    zero = jnp.zeros((TBLK, HD), bf16)
    query_grads = []
    for h in range(heads):
        q_here = query_rows(mixed_ref, rel_ref, h)
        g_here = g_ref[:, h * HD : (h + 1) * HD]
        weighed = g_here.astype(f32) * att_ref[:, h * HD : (h + 1) * HD].astype(f32)
        delta = jnp.sum(weighed.T, axis=0, keepdims=True)
        g_wide = jnp.concatenate([g_here, zero], axis=1)
        q_wide = jnp.concatenate([zero, q_here[:, :HD]], axis=1)
        lse = lse_ref[h]
        total = None
        for c in range(tokens // UBLK):
            span = pl.ds(c * UBLK, UBLK)
            scores = mm_nt(k_ref[h, span, :], q_here)
            probs = jnp.exp(scores - lse)
            pgrad = mm_nt(v_ref[h, span, :], g_here)
            sgrad = (probs * (pgrad - delta)).astype(bf16)
            dkv_ref[h, span, :] += mm(probs.astype(bf16), g_wide) + mm(sgrad, q_wide)
            part = mm(kt_ref[h, :, span], sgrad)
            total = part if total is None else total + part
        query_grads.append(total[:HD].T)
        rows_ref[h] = total[HD : HD + SMAX].T.astype(bf16)
        cols_ref[h] = total[HD + SMAX :].T.astype(bf16)
    dq_ref[...] = HD**-0.5 * jnp.concatenate(query_grads, axis=1)

    @pl.when(pl.program_id(0) == pl.num_programs(0) - 1)
    def _():
        keys = [dkv_ref[h, :, HD:] for h in range(heads)]
        values = [dkv_ref[h, :, :HD] for h in range(heads)]
        out_ref[...] = jnp.concatenate(keys + values, axis=1).astype(bf16)


def attend_backward(mixed, rel, lines, grads, attended, lse):
    heads, tokens, depth = rel.shape
    width = heads * HD
    return pl.pallas_call(
        backward_kernel,
        grid=(tokens // TBLK,),
        in_specs=[
            pl.BlockSpec(mixed.shape, lambda t: (0, 0)),
            pl.BlockSpec((heads, TBLK, depth), lambda t: (0, t, 0)),
            pl.BlockSpec(lines.shape, lambda t: (0, 0)),
            pl.BlockSpec((TBLK, width), lambda t: (t, 0)),
            pl.BlockSpec((TBLK, width), lambda t: (t, 0)),
            pl.BlockSpec((heads, 1, TBLK), lambda t: (0, 0, t)),
        ],
        out_specs=[
            pl.BlockSpec((TBLK, width), lambda t: (t, 0)),
            pl.BlockSpec((heads, TBLK, SMAX), lambda t: (0, t, 0)),
            pl.BlockSpec((heads, TBLK, SMAX), lambda t: (0, t, 0)),
            pl.BlockSpec((tokens, 2 * width), lambda t: (0, 0)),
        ],
        out_shape=[
            jax.ShapeDtypeStruct((tokens, width), jnp.float32),
            jax.ShapeDtypeStruct((heads, tokens, SMAX), jnp.bfloat16),
            jax.ShapeDtypeStruct((heads, tokens, SMAX), jnp.bfloat16),
            jax.ShapeDtypeStruct((tokens, 2 * width), jnp.bfloat16),
        ],
        scratch_shapes=[
            pltpu.VMEM((heads, tokens, 2 * HD), jnp.float32),
            pltpu.VMEM((heads, tokens, HD + depth), jnp.bfloat16),
            pltpu.VMEM((heads, tokens, HD), jnp.bfloat16),
            pltpu.VMEM((heads, HD + 2 * SMAX, tokens), jnp.bfloat16),
        ],
        name="attend_backward",
        compiler_params=pltpu.CompilerParams(dimension_semantics=("arbitrary",)),
    )(mixed, rel, lines, grads, attended, lse)


def norm_parts(values):
    center = values - jnp.mean(values, axis=-1, keepdims=True)
    scale = lax.rsqrt(jnp.mean(center * center, axis=-1, keepdims=True) + 1e-06)
    return center * scale, scale


def feed_kernel(
    mid_ref,
    cot_ref,
    mask_ref,
    vec_ref,
    shift_ref,
    up_ref,
    down_ref,
    out_ref,
    total_ref,
    branch_ref,
    sums_ref,
    up_bias_ref,
    up_grad_ref,
    down_grad_ref,
    normed_ref,
    turned_ref,
    down_in_ref,
    down_turn_ref,
    out_acc_ref,
    in_acc_ref,
    weight_ref,
):
    f32 = jnp.float32
    bf16 = jnp.bfloat16
    step = pl.program_id(0)
    groups, heads, height, width = up_ref.shape
    cols = weight_ref.shape[1] // groups
    folds = width // cols
    rows = height * folds
    pieces, _, out_cols, _ = down_ref.shape

    @pl.when(step == 0)
    def _():
        unit, _ = norm_parts(mid_ref[...])
        normed = (unit * vec_ref[1:2] + vec_ref[2:3]).astype(bf16)
        normed_ref[...] = normed
        turned_ref[...] = normed.T
        masked = mask_ref[...] * cot_ref[...].astype(f32)
        down_in_ref[...] = masked.astype(bf16)
        down_turn_ref[...] = masked.astype(bf16).T
        out_acc_ref[...] = jnp.zeros_like(out_acc_ref)
        in_acc_ref[...] = jnp.zeros_like(in_acc_ref)

    for g in range(groups):
        for h in range(heads):
            for s in range(folds):
                top = h * rows + s * height
                weight_ref[top : top + height, g * cols : (g + 1) * cols] = up_ref[
                    g, h, :, s * cols : (s + 1) * cols
                ]
    weight = weight_ref[...]
    down = down_ref[...].reshape(pieces * out_cols, width)
    hidden = mm(normed_ref[...], weight) + shift_ref[0]
    share = 0.5 * (1.0 + lax.erf(hidden * (0.5**0.5)))
    active = (hidden * share).astype(bf16)
    slope = share + hidden * jnp.exp(-0.5 * hidden * hidden) * 0.3989422804014327
    out_acc_ref[...] += mm_nt(active, down)
    hidden_grad = (mm(down_in_ref[...], down) * slope).astype(bf16)
    down_grad_ref[...] = (
        mm(down_turn_ref[...], active).astype(bf16).reshape(pieces, 1, out_cols, width)
    )
    in_acc_ref[...] += mm_nt(hidden_grad, weight)
    up_bias_ref[0] = jnp.sum(hidden_grad.astype(f32), axis=0, keepdims=True)
    up_grad = mm(turned_ref[...], hidden_grad).astype(bf16)
    for g in range(groups):
        for h in range(heads):
            for s in range(folds):
                top = h * rows + s * height
                up_grad_ref[g, h, :, s * cols : (s + 1) * cols] = up_grad[
                    top : top + height, g * cols : (g + 1) * cols
                ]

    @pl.when(step == pl.num_programs(0) - 1)
    def _():
        middle = mid_ref[...]
        mask = mask_ref[...]
        cot = cot_ref[...].astype(f32)
        out_ref[...] = (middle + mask * (out_acc_ref[...] + vec_ref[3:4])).astype(bf16)
        unit, scale = norm_parts(middle)
        grad_in = in_acc_ref[...]
        inner = grad_in * vec_ref[1:2]
        total = cot + scale * (
            inner
            - jnp.mean(inner, axis=-1, keepdims=True)
            - unit * jnp.mean(inner * unit, axis=-1, keepdims=True)
        )
        branch = (mask * total).astype(bf16)
        total_ref[...] = total
        branch_ref[...] = branch
        sums_ref[...] = jnp.concatenate(
            [
                jnp.sum(branch.astype(f32), axis=0, keepdims=True),
                jnp.sum(grad_in * unit, axis=0, keepdims=True),
                jnp.sum(grad_in, axis=0, keepdims=True),
                jnp.sum(mask * cot, axis=0, keepdims=True),
            ],
            axis=0,
        )


def feed_forward(middle, cot, mask, vectors, shift, gathered, up_height, out_cols):
    tokens, width = middle.shape
    groups, heads = gathered.shape[:2]
    steps = shift.shape[0]
    per_step = groups // steps
    f32 = jnp.float32
    bf16 = jnp.bfloat16

    def whole(rows, cols):
        return pl.BlockSpec((rows, cols), lambda c: (0, 0))

    up_spec = (per_step, heads, up_height, width)
    down_spec = (groups, 1, out_cols, width)
    return pl.pallas_call(
        feed_kernel,
        grid=(steps,),
        in_specs=[
            whole(tokens, width),
            whole(tokens, width),
            whole(tokens, 1),
            whole(vectors.shape[0], width),
            pl.BlockSpec((1, 1, width), lambda c: (c, 0, 0)),
            pl.BlockSpec(up_spec, lambda c: (c, 0, 0, 0)),
            pl.BlockSpec(down_spec, lambda c: (0, c, 1, 0)),
        ],
        out_specs=[
            whole(tokens, width),
            whole(tokens, width),
            whole(tokens, width),
            whole(4, width),
            pl.BlockSpec((1, 1, width), lambda c: (c, 0, 0)),
            pl.BlockSpec(up_spec, lambda c: (c, 0, 0, 0)),
            pl.BlockSpec(down_spec, lambda c: (0, c, 0, 0)),
        ],
        out_shape=[
            jax.ShapeDtypeStruct((tokens, width), bf16),
            jax.ShapeDtypeStruct((tokens, width), f32),
            jax.ShapeDtypeStruct((tokens, width), bf16),
            jax.ShapeDtypeStruct((4, width), f32),
            jax.ShapeDtypeStruct((steps, 1, width), f32),
            jax.ShapeDtypeStruct((groups, heads, up_height, width), bf16),
            jax.ShapeDtypeStruct((groups, heads, out_cols, width), bf16),
        ],
        scratch_shapes=[
            pltpu.VMEM((tokens, width), bf16),
            pltpu.VMEM((width, tokens), bf16),
            pltpu.VMEM((tokens, width), bf16),
            pltpu.VMEM((width, tokens), bf16),
            pltpu.VMEM((tokens, width), f32),
            pltpu.VMEM((tokens, width), f32),
            pltpu.VMEM((width, width), bf16),
        ],
        name="feed_forward",
        compiler_params=pltpu.CompilerParams(dimension_semantics=("arbitrary",)),
    )(middle, cot, mask, vectors, shift, gathered, gathered)


def layer_norm(values, gain, shift):
    center = values - jnp.mean(values, axis=-1, keepdims=True)
    spread = jnp.mean(center * center, axis=-1, keepdims=True)
    return center * lax.rsqrt(spread + 1e-06) * gain + shift


def interp_matrix(img_side):
    coord = jnp.arange(SMAX, dtype=jnp.int32)
    length_in = 2 * SMAX - 1
    length_out = 2 * img_side - 1
    offset = jnp.clip(coord[:, None] - coord[None, :] + img_side - 1, 0, length_out - 1)
    numer = jnp.maximum((2 * offset + 1) * length_in - length_out, 0)
    lower = numer // (2 * length_out)
    weight_hi = (numer - lower * 2 * length_out).astype(jnp.float32) / (2 * length_out).astype(
        jnp.float32
    )
    upper = jnp.minimum(lower + 1, length_in - 1)
    target = jnp.arange(length_in, dtype=jnp.int32)
    lower_hot = (target == lower[..., None]).astype(jnp.float32)
    upper_hot = (target == upper[..., None]).astype(jnp.float32)
    return (1.0 - weight_hi)[..., None] * lower_hot + weight_hi[..., None] * upper_hot


def contract_rows(left, right):
    return lax.dot_general(
        left, right, (((0,), (0,)), ((), ())), preferred_element_type=jnp.float32
    )


def contract_cols(left, right):
    return lax.dot_general(
        left, right, (((1,), (1,)), ((), ())), preferred_element_type=jnp.float32
    )


def exchange(values, axis):
    return lax.all_to_all(values, axis, split_axis=0, concat_axis=0, tiled=True)


def spread(values, axis):
    count = lax.axis_size(axis)
    return exchange(jnp.broadcast_to(values, (count,) + values.shape), axis)


def swap(values, step):
    pairs = [(i, i ^ step) for i in range(lax.axis_size("ha"))]
    return lax.ppermute(values, "ha", pairs)


def gather_heads(values, beside):
    me = lax.axis_index("ha")
    far = swap(values, 2)
    near = swap(values, 1)
    far, near, beside = lax.optimization_barrier((far, near, beside))
    corner = swap(far, 1)
    blocks = jnp.stack([values, near, far, corner])
    ordered = [
        lax.dynamic_index_in_dim(blocks, jnp.bitwise_xor(me, i), 0, False) for i in range(4)
    ]
    return ordered, beside


def exchange_heads(parts):
    me = lax.axis_index("ha")
    arrived = [
        swap(lax.dynamic_index_in_dim(parts, jnp.bitwise_xor(me, i), 0, False), i)
        for i in range(1, 4)
    ]
    blocks = jnp.stack([lax.dynamic_index_in_dim(parts, me, 0, False)] + arrived)
    return jnp.stack(
        [lax.dynamic_index_in_dim(blocks, jnp.bitwise_xor(me, i), 0, False) for i in range(4)]
    )


def scatter_heads(parts):
    me = lax.axis_index("ha")
    other = [lax.dynamic_index_in_dim(parts, jnp.bitwise_xor(me, i), 0, False) for i in range(4)]
    arrived = swap(jnp.stack([other[3], other[1]]), 1).astype(jnp.float32)
    far = (other[2].astype(jnp.float32) + arrived[0]).astype(jnp.bfloat16)
    near = other[0].astype(jnp.float32) + arrived[1]
    return near + swap(far, 2).astype(jnp.float32)


def pack_up(piece):
    rows, width = piece.shape[-2:]
    lead = piece.shape[:-2]
    fold = 4 * rows // width
    cut = piece.reshape(lead + (fold, rows // fold, width))
    return jnp.swapaxes(cut, -3, -2).reshape(lead + (rows // fold, fold * width))


def unpack_up(packed, rows, width):
    fold = packed.shape[-1] // width
    lead = packed.shape[:-2]
    cut = packed.reshape(lead + (rows // fold, fold, width))
    return jnp.swapaxes(cut, -3, -2).reshape(lead + (rows, width))


def local(
    patches,
    cotangent,
    sides,
    norm1_gain,
    norm1_bias,
    qkv_weight,
    query_bias,
    value_bias,
    proj_weight,
    proj_bias,
    norm2_gain,
    norm2_bias,
    fc1_weight,
    fc1_bias,
    fc2_weight,
    fc2_bias,
    rel_height,
    rel_width,
):
    group_count = lax.axis_size("ga")
    head_groups = lax.axis_size("ha")
    group_index = lax.axis_index("ga")
    head_index = lax.axis_index("ha")
    device_count = group_count * head_groups
    block_len = patches.shape[1]
    model_width = patches.shape[2]
    hidden_width = fc1_bias.shape[0] * head_groups
    local_tokens = group_count * block_len
    group_width = model_width // head_groups
    group_heads = HEADS // head_groups
    cap_tokens = SMAX * SMAX
    f32 = jnp.float32
    bf16 = jnp.bfloat16

    triple_rows = lax.all_gather(qkv_weight, "ga", axis=1, tiled=True)
    up_rows, up_cols = fc1_weight.shape
    out_cols = fc2_weight.shape[1]
    up_height = up_rows * up_cols // model_width
    out_share = out_cols // head_groups
    pack_rows = up_height + out_cols + out_share

    vectors = jnp.concatenate(
        [norm1_gain, norm1_bias, proj_bias, norm2_gain, norm2_bias, fc2_bias, fc1_bias]
    )
    vector_size = vectors.shape[0]
    vectors_all = lax.all_gather(
        jnp.concatenate([vectors, proj_weight.T.reshape(-1)]), "ha", axis=0, tiled=False
    )
    proj_rows = vectors_all[:, vector_size:].reshape(head_groups, head_groups, -1)
    proj_mine = lax.dynamic_index_in_dim(proj_rows, head_index, 1, False)
    packed = jnp.concatenate(
        [
            pack_up(fc1_weight),
            fc2_weight.T,
            proj_mine.reshape(head_groups, out_share, group_width)
            .transpose(1, 0, 2)
            .reshape(out_share, model_width),
        ],
        axis=0,
    )
    tokens_in = lax.all_to_all(patches, "ga", split_axis=0, concat_axis=1, tiled=True)[0]
    tokens_in, triple_rows, vectors_all, packed = lax.optimization_barrier(
        (tokens_in, triple_rows, vectors_all, packed)
    )
    cot_in = lax.all_to_all(cotangent, "ga", split_axis=0, concat_axis=1, tiled=True)[0]
    wide = model_width // head_groups

    def vector_at(slot, width):
        return vectors_all[:, slot * wide : slot * wide + width].reshape(-1)

    first_gain = vector_at(0, wide)
    first_shift = vector_at(1, wide)
    proj_shift = vector_at(2, wide)
    second_gain = vector_at(3, wide)
    second_shift = vector_at(4, wide)
    down_shift = vector_at(5, wide)
    up_shift = vector_at(6, 4 * wide)

    triple_cut = triple_rows.reshape(group_width, 3, head_groups, group_width).transpose(2, 0, 1, 3)
    triple_own = exchange(
        triple_cut.reshape(head_groups, group_width, 3 * group_width), "ha"
    ).reshape(model_width, 3 * group_width)
    tokens32 = tokens_in.astype(f32)
    slot_index = jnp.arange(local_tokens, dtype=jnp.int32)
    grid_index = (
        slot_index // block_len * head_groups + head_index
    ) * block_len + slot_index % block_len
    img_side = lax.dynamic_index_in_dim(sides, group_index, 0, keepdims=False)
    tok_mask = ((grid_index // SMAX < img_side) & (grid_index % SMAX < img_side)).astype(f32)[
        :, None
    ]
    all_index = jnp.arange(cap_tokens, dtype=jnp.int32)[:, None]
    line_index = jnp.arange(2 * SMAX, dtype=jnp.int32)[None, :]
    expand = jnp.where(
        line_index < SMAX,
        all_index // SMAX == line_index,
        all_index % SMAX == line_index - SMAX,
    ).astype(bf16)
    line_valid = line_index[0] % SMAX < img_side
    matrix = interp_matrix(img_side)
    table_h = jnp.einsum(
        "qkj,jd->qkd", matrix, rel_height.astype(f32), precision=exact_mode
    ).astype(bf16)
    table_w = jnp.einsum("qkj,jd->qkd", matrix, rel_width.astype(f32), precision=exact_mode).astype(
        bf16
    )

    blocks_all, triple_own = gather_heads(tokens_in, triple_own)
    tokens_all = (
        jnp.stack(
            [block.reshape(group_count, block_len, model_width) for block in blocks_all],
            axis=1,
        )
        .reshape(cap_tokens, model_width)
        .astype(f32)
    )
    gain32 = first_gain.astype(f32)
    shift32 = first_shift.astype(f32)
    normed_all = layer_norm(tokens_all, gain32, shift32).astype(bf16)
    bias_own = jnp.concatenate([query_bias, jnp.zeros_like(query_bias), value_bias]).astype(f32)
    mixed = (jnp.dot(normed_all, triple_own, preferred_element_type=f32) + bias_own).astype(bf16)
    q_grid = (
        mixed[:, :group_width].reshape(SMAX, SMAX, group_heads, HD).transpose(2, 0, 1, 3)
    )
    rel_h = jnp.einsum("hrwd,rkd->hrwk", q_grid, table_h, preferred_element_type=f32)
    rel_w = jnp.einsum("hrwd,wkd->hrwk", q_grid, table_w, preferred_element_type=f32)
    rel_both = jnp.concatenate([rel_h, rel_w], axis=-1).reshape(
        group_heads, cap_tokens, 2 * SMAX
    )
    rel_upper = lax.reduce_precision(rel_both, 8, 7)
    rel_lower = jnp.where(line_valid, rel_both - rel_upper, 0.0).astype(bf16)
    rel_upper = jnp.where(line_valid, rel_upper, -1e30).astype(bf16)
    rel_split = jnp.concatenate([rel_upper, rel_lower], axis=-1)
    rel_split, cot_in = lax.optimization_barrier((rel_split, cot_in))
    cot32 = cot_in.astype(f32)
    att_heads, log_sums = attend_forward(mixed, rel_split, expand)

    gathered = lax.all_gather(packed, BOTH, axis=0, tiled=False)
    att_heads, gathered = lax.optimization_barrier((att_heads, gathered))
    gathered = gathered.reshape(group_count, head_groups, pack_rows, model_width)
    proj_turn = gathered[:, :, up_height + out_cols :].reshape(model_width, model_width)

    att_back = lax.all_to_all(
        att_heads.reshape(group_count, head_groups, block_len, 1, group_width),
        "ha",
        split_axis=1,
        concat_axis=3,
        tiled=True,
    )
    att_tok = att_back.reshape(local_tokens, model_width)
    branch = contract_cols(att_tok, proj_turn) + proj_shift.astype(f32)
    middle = tokens32 + tok_mask * branch
    steps = hidden_width // model_width
    if out_cols % 16 == 0 and up_cols % 128 == 0 and up_height == out_cols and steps == head_groups:
        norm_vectors = jnp.stack([proj_shift, second_gain, second_shift, down_shift]).astype(f32)
        (
            block_out,
            mid_total,
            branch_grad,
            small_sums,
            up_bias_grad,
            up_packed,
            down_packed,
        ) = feed_forward(
            middle,
            cot_in,
            tok_mask,
            norm_vectors,
            up_shift.astype(f32).reshape(steps, 1, model_width),
            gathered,
            up_height,
            out_cols,
        )
        up_bias_grad = up_bias_grad.reshape(-1)
        proj_bias_grad, second_gain_grad, second_shift_grad, down_bias_grad = small_sums
    else:
        up_full = (
            unpack_up(gathered[:, :, :up_height], up_rows, up_cols)
            .transpose(1, 2, 0, 3)
            .reshape(model_width, hidden_width)
        )
        down_turn = (
            gathered[:, :, up_height : up_height + out_cols]
            .transpose(0, 2, 1, 3)
            .reshape(model_width, hidden_width)
        )
        normed2 = layer_norm(middle, second_gain.astype(f32), second_shift.astype(f32)).astype(bf16)
        hidden = jnp.dot(normed2, up_full, preferred_element_type=f32) + up_shift.astype(f32)
        activated = jax.nn.gelu(hidden, approximate=False).astype(bf16)
        block_out = (
            middle + tok_mask * (contract_cols(activated, down_turn) + down_shift.astype(f32))
        ).astype(bf16)
        masked_cot = tok_mask * cot32
        down_in = masked_cot.astype(bf16)
        down_grad = contract_rows(down_in, activated).astype(bf16)
        down_bias_grad = jnp.sum(masked_cot, axis=0)
        act_grad = jnp.dot(down_in, down_turn, preferred_element_type=f32)
        _, gelu_pull = jax.vjp(partial(jax.nn.gelu, approximate=False), hidden)
        hidden_grad = gelu_pull(act_grad)[0].astype(bf16)
        up_grad = contract_rows(normed2, hidden_grad).astype(bf16)
        up_bias_grad = jnp.sum(hidden_grad.astype(f32), axis=0)
        norm2_in = contract_cols(hidden_grad, up_full)
        _, norm2_pull = jax.vjp(
            layer_norm, middle, second_gain.astype(f32), second_shift.astype(f32)
        )
        mid_grad, second_gain_grad, second_shift_grad = norm2_pull(norm2_in)
        mid_total = cot32 + mid_grad
        branch_grad = (tok_mask * mid_total).astype(bf16)
        up_packed = pack_up(
            up_grad.reshape(head_groups, up_rows, group_count, up_cols).transpose(2, 0, 1, 3)
        )
        down_packed = down_grad.reshape(group_count, out_cols, head_groups, model_width).transpose(
            0, 2, 1, 3
        )
        proj_bias_grad = jnp.sum(branch_grad.astype(f32), axis=0)

    att_grad_tok = jnp.dot(branch_grad, proj_turn, preferred_element_type=f32).astype(bf16)
    att_grad_tok, branch_turn, up_packed, down_packed = lax.optimization_barrier(
        (att_grad_tok, branch_grad, up_packed, down_packed)
    )
    att_grad = lax.all_to_all(
        att_grad_tok.reshape(group_count, 1, block_len, head_groups, group_width),
        "ha",
        split_axis=3,
        concat_axis=1,
        tiled=True,
    ).reshape(cap_tokens, group_width)
    att_grad, block_out = lax.optimization_barrier((att_grad, block_out))
    out_back = exchange(block_out.reshape(group_count, block_len, model_width), "ga")

    proj_grad = contract_rows(branch_turn, att_tok).astype(bf16)
    grads_packed = jnp.concatenate(
        [
            up_packed,
            down_packed,
            proj_grad.reshape(group_count, head_groups, out_share, model_width),
        ],
        axis=2,
    ).reshape(device_count * pack_rows, model_width)
    grads_own = lax.psum_scatter(grads_packed, BOTH, scatter_dimension=0, tiled=True)
    up_own = unpack_up(grads_own[:up_height], up_rows, up_cols).astype(f32)
    down_own = grads_own[up_height : up_height + out_cols].T.astype(f32)
    proj_own = (
        exchange_heads(
            grads_own[up_height + out_cols :]
            .reshape(out_share, head_groups, group_width)
            .transpose(1, 0, 2)
        )
        .reshape(out_cols, group_width)
        .T.astype(f32)
    )

    query_part, height_grad, width_grad, key_value_grad = attend_backward(
        mixed, rel_split, expand, att_grad, att_heads, log_sums
    )
    query_part, height_grad, width_grad, key_value_grad, out_back = lax.optimization_barrier(
        (query_part, height_grad, width_grad, key_value_grad, out_back)
    )
    height_grad = height_grad.reshape(group_heads, SMAX, SMAX, SMAX)
    width_grad = width_grad.reshape(group_heads, SMAX, SMAX, SMAX)
    query_grad = (
        query_part
        + jnp.einsum(
            "hrwj,rjd->rwhd", height_grad, table_h, preferred_element_type=bf16
        ).reshape(cap_tokens, group_width)
        + jnp.einsum(
            "hrwj,wjd->rwhd", width_grad, table_w, preferred_element_type=bf16
        ).reshape(cap_tokens, group_width)
    )
    mixed_grad = jnp.concatenate(
        [
            query_grad.astype(bf16),
            key_value_grad,
        ],
        axis=1,
    )
    triple_part = contract_rows(normed_all, mixed_grad).astype(bf16)
    mixed_grad, triple_part, height_grad, width_grad = lax.optimization_barrier(
        (mixed_grad, triple_part, height_grad, width_grad)
    )
    norm1_wide = contract_cols(mixed_grad, triple_own)
    h_table_grad = jnp.einsum("hrwj,hrwd->rjd", height_grad, q_grid, preferred_element_type=f32)
    w_table_grad = jnp.einsum("hrwj,hrwd->wjd", width_grad, q_grid, preferred_element_type=f32)
    norm1_part = (
        norm1_wide.astype(bf16)
        .reshape(group_count, head_groups, block_len, model_width)
        .transpose(1, 0, 2, 3)
        .reshape(head_groups, local_tokens, model_width)
    )
    norm1_in = scatter_heads(norm1_part)
    triple_rows_grad = (
        exchange(triple_part.reshape(head_groups, group_width, 3 * group_width), "ha")
        .reshape(head_groups, group_width, 3, group_width)
        .transpose(1, 2, 0, 3)
        .reshape(group_width, group_count, 3 * model_width // group_count)
        .transpose(1, 0, 2)
    )
    triple_grad = jnp.sum(exchange(triple_rows_grad, "ga").astype(f32), axis=0)

    center = tokens_all - jnp.mean(tokens_all, axis=-1, keepdims=True)
    unit = center * lax.rsqrt(jnp.mean(center * center, axis=-1, keepdims=True) + 1e-06)
    first_gain_grad = jnp.sum(norm1_wide * unit, axis=0)
    first_shift_grad = jnp.sum(norm1_wide, axis=0)
    mixed_float = mixed_grad.astype(f32)
    height_rel = jnp.einsum("qkj,qkd->jd", matrix, h_table_grad, precision=exact_mode)
    width_rel = jnp.einsum("qkj,qkd->jd", matrix, w_table_grad, precision=exact_mode)
    rel_flat = jnp.concatenate([height_rel, width_rel]).reshape(-1)
    rel_size = rel_flat.shape[0]
    grouped = [
        first_gain_grad,
        first_shift_grad,
        proj_bias_grad,
        second_gain_grad,
        second_shift_grad,
        down_bias_grad,
        up_bias_grad,
    ]
    small = jnp.concatenate(
        [vector.reshape(head_groups, -1) for vector in grouped]
        + [rel_flat.reshape(head_groups, -1)],
        axis=1,
    )
    small = small + swap(small, 1)
    small = small + swap(small, 2)
    own_part = lax.dynamic_index_in_dim(small, head_index, 0, False)
    own_size = own_part.shape[0] - rel_size // head_groups
    last_part = jnp.concatenate(
        [
            own_part[:own_size],
            jnp.sum(mixed_float[:, :group_width], axis=0),
            jnp.sum(mixed_float[:, 2 * group_width :], axis=0),
            small[:, own_size:].reshape(-1),
        ]
    )
    last_size = last_part.shape[0]
    last_part = jnp.pad(last_part, (0, -last_size % 128)).reshape(-1, 128)
    last_sum = jnp.sum(spread(last_part, "ga"), axis=0).reshape(-1)[:last_size]
    rel_sum = last_sum[last_size - rel_size :].reshape(2, 2 * SMAX - 1, HD)
    late = []
    at = 0
    for size in [group_width] * 6 + [hidden_width // head_groups] + [group_width] * 2:
        late.append(last_sum[at : at + size])
        at += size

    _, norm1_pull = jax.vjp(lambda tokens: layer_norm(tokens, gain32, shift32), tokens32)
    input_grad = (mid_total + norm1_pull(norm1_in)[0]).astype(bf16)
    in_back = exchange(input_grad.reshape(group_count, block_len, model_width), "ga")
    return (
        out_back,
        in_back,
        late[0],
        late[1],
        triple_grad,
        late[7],
        late[8],
        proj_own,
        late[2],
        late[3],
        late[4],
        up_own,
        late[6],
        down_own,
        late[5],
        rel_sum[0],
        rel_sum[1],
    )


def solution(mesh):
    placed = (
        P(None, ("ga", "ha"), None),
        P(None, ("ga", "ha"), None),
        P(),
        P("ha"),
        P("ha"),
        P("ha", "ga"),
        P("ha"),
        P("ha"),
        P("ha", "ga"),
        P("ha"),
        P("ha"),
        P("ha"),
        P("ha", "ga"),
        P("ha"),
        P("ha", "ga"),
        P("ha"),
        P(),
        P(),
    )
    return jax.shard_map(
        local,
        mesh=mesh,
        in_specs=placed,
        out_specs=(
            P(None, ("ga", "ha"), None),
            P(None, ("ga", "ha"), None),
            P("ha"),
            P("ha"),
            P("ha", "ga"),
            P("ha"),
            P("ha"),
            P("ha", "ga"),
            P("ha"),
            P("ha"),
            P("ha"),
            P("ha", "ga"),
            P("ha"),
            P("ha", "ga"),
            P("ha"),
            P(),
            P(),
        ),
        check_vma=False,
    )
```

```python
from functools import partial

import jax
import jax.numpy as jnp
from jax import lax
from jax.experimental import pallas as pl
from jax.experimental.pallas import tpu as pltpu
from jax.sharding import PartitionSpec as P

HEADS = 12
HD = 64
SMAX = 48
BOTH = ("ga", "ha")


exact_mode = lax.Precision.HIGHEST


TBLK = 256
UBLK = 768

NT = (((1,), (1,)), ((), ()))


def mm(left, right):
    return jnp.dot(left, right, preferred_element_type=jnp.float32)


def mm_nt(left, right):
    return lax.dot_general(left, right, NT, preferred_element_type=jnp.float32)


def query_rows(mixed_ref, rel_ref, head):
    start = pl.multiple_of(pl.program_id(0) * TBLK, TBLK)
    rows = mixed_ref[pl.ds(start, TBLK), head * HD : (head + 1) * HD]
    return jnp.concatenate([rows * jnp.asarray(HD**-0.5, rows.dtype), rel_ref[head]], axis=1)


def forward_kernel(mixed_ref, rel_ref, lines_ref, out_ref, lse_ref, k_ref, v_ref):
    heads = rel_ref.shape[0]
    tokens = mixed_ref.shape[0]
    width = heads * HD
    bf16 = jnp.bfloat16

    @pl.when(pl.program_id(0) == 0)
    def _():
        lines = lines_ref[...]
        for h in range(heads):
            keys = mixed_ref[:, width + h * HD : width + (h + 1) * HD]
            values = mixed_ref[:, 2 * width + h * HD : 2 * width + (h + 1) * HD]
            k_ref[h] = jnp.concatenate([keys, lines, lines], axis=1)
            v_ref[h, :HD] = values.T
            v_ref[h, HD:] = jnp.ones((16, tokens), bf16)

    outs = []
    for h in range(heads):
        scores = mm_nt(k_ref[h], query_rows(mixed_ref, rel_ref, h))
        top = jnp.max(scores, axis=0, keepdims=True)
        expo = jnp.exp(scores - top).astype(bf16)
        mixed = mm(v_ref[h], expo)
        total = mixed[HD : HD + 1]
        outs.append((mixed[:HD] / total).T.astype(bf16))
        lse_ref[h] = top + jnp.log(total)
    out_ref[...] = jnp.concatenate(outs, axis=1)


def attend_forward(mixed, rel, lines):
    heads, tokens, depth = rel.shape
    return pl.pallas_call(
        forward_kernel,
        grid=(tokens // TBLK,),
        in_specs=[
            pl.BlockSpec(mixed.shape, lambda t: (0, 0)),
            pl.BlockSpec((heads, TBLK, depth), lambda t: (0, t, 0)),
            pl.BlockSpec(lines.shape, lambda t: (0, 0)),
        ],
        out_specs=[
            pl.BlockSpec((TBLK, heads * HD), lambda t: (t, 0)),
            pl.BlockSpec((heads, 1, TBLK), lambda t: (0, 0, t)),
        ],
        out_shape=[
            jax.ShapeDtypeStruct((tokens, heads * HD), jnp.bfloat16),
            jax.ShapeDtypeStruct((heads, 1, tokens), jnp.float32),
        ],
        scratch_shapes=[
            pltpu.VMEM((heads, tokens, HD + depth), jnp.bfloat16),
            pltpu.VMEM((heads, HD + 16, tokens), jnp.bfloat16),
        ],
        name="attend_forward",
        compiler_params=pltpu.CompilerParams(dimension_semantics=("arbitrary",)),
    )(mixed, rel, lines)


def backward_kernel(
    mixed_ref,
    rel_ref,
    lines_ref,
    g_ref,
    att_ref,
    lse_ref,
    dq_ref,
    rows_ref,
    cols_ref,
    out_ref,
    dkv_ref,
    k_ref,
    v_ref,
    kt_ref,
):
    heads = rel_ref.shape[0]
    tokens = mixed_ref.shape[0]
    width = heads * HD
    bf16 = jnp.bfloat16
    f32 = jnp.float32

    @pl.when(pl.program_id(0) == 0)
    def _():
        dkv_ref[...] = jnp.zeros_like(dkv_ref)
        lines = lines_ref[...]
        for h in range(heads):
            keys = mixed_ref[:, width + h * HD : width + (h + 1) * HD]
            k_ref[h] = jnp.concatenate([keys, lines, lines], axis=1)
            v_ref[h] = mixed_ref[:, 2 * width + h * HD : 2 * width + (h + 1) * HD]
            kt_ref[h] = jnp.concatenate([keys, lines], axis=1).T

    zero = jnp.zeros((TBLK, HD), bf16)
    for h in range(heads):
        q_here = query_rows(mixed_ref, rel_ref, h)
        g_here = g_ref[:, h * HD : (h + 1) * HD]
        weighed = g_here.astype(f32) * att_ref[:, h * HD : (h + 1) * HD].astype(f32)
        delta = jnp.sum(weighed.T, axis=0, keepdims=True)
        g_wide = jnp.concatenate([g_here, zero], axis=1)
        q_wide = jnp.concatenate([zero, q_here[:, :HD]], axis=1)
        lse = lse_ref[h]
        total = None
        for c in range(tokens // UBLK):
            span = pl.ds(c * UBLK, UBLK)
            scores = mm_nt(k_ref[h, span, :], q_here)
            probs = jnp.exp(scores - lse)
            pgrad = mm_nt(v_ref[h, span, :], g_here)
            sgrad = (probs * (pgrad - delta)).astype(bf16)
            dkv_ref[h, span, :] += mm(probs.astype(bf16), g_wide) + mm(sgrad, q_wide)
            part = mm(kt_ref[h, :, span], sgrad)
            total = part if total is None else total + part
        dq_ref[h] = HD**-0.5 * total[:HD].T
        rows_ref[h] = total[HD : HD + SMAX].T.astype(bf16)
        cols_ref[h] = total[HD + SMAX :].T.astype(bf16)

    @pl.when(pl.program_id(0) == pl.num_programs(0) - 1)
    def _():
        keys = [dkv_ref[h, :, HD:] for h in range(heads)]
        values = [dkv_ref[h, :, :HD] for h in range(heads)]
        out_ref[...] = jnp.concatenate(keys + values, axis=1).astype(bf16)


def attend_backward(mixed, rel, lines, grads, attended, lse):
    heads, tokens, depth = rel.shape
    width = heads * HD
    return pl.pallas_call(
        backward_kernel,
        grid=(tokens // TBLK,),
        in_specs=[
            pl.BlockSpec(mixed.shape, lambda t: (0, 0)),
            pl.BlockSpec((heads, TBLK, depth), lambda t: (0, t, 0)),
            pl.BlockSpec(lines.shape, lambda t: (0, 0)),
            pl.BlockSpec((TBLK, width), lambda t: (t, 0)),
            pl.BlockSpec((TBLK, width), lambda t: (t, 0)),
            pl.BlockSpec((heads, 1, TBLK), lambda t: (0, 0, t)),
        ],
        out_specs=[
            pl.BlockSpec((heads, TBLK, HD), lambda t: (0, t, 0)),
            pl.BlockSpec((heads, TBLK, SMAX), lambda t: (0, t, 0)),
            pl.BlockSpec((heads, TBLK, SMAX), lambda t: (0, t, 0)),
            pl.BlockSpec((tokens, 2 * width), lambda t: (0, 0)),
        ],
        out_shape=[
            jax.ShapeDtypeStruct((heads, tokens, HD), jnp.float32),
            jax.ShapeDtypeStruct((heads, tokens, SMAX), jnp.bfloat16),
            jax.ShapeDtypeStruct((heads, tokens, SMAX), jnp.bfloat16),
            jax.ShapeDtypeStruct((tokens, 2 * width), jnp.bfloat16),
        ],
        scratch_shapes=[
            pltpu.VMEM((heads, tokens, 2 * HD), jnp.float32),
            pltpu.VMEM((heads, tokens, HD + depth), jnp.bfloat16),
            pltpu.VMEM((heads, tokens, HD), jnp.bfloat16),
            pltpu.VMEM((heads, HD + 2 * SMAX, tokens), jnp.bfloat16),
        ],
        name="attend_backward",
        compiler_params=pltpu.CompilerParams(dimension_semantics=("arbitrary",)),
    )(mixed, rel, lines, grads, attended, lse)


def norm_parts(values):
    center = values - jnp.mean(values, axis=-1, keepdims=True)
    scale = lax.rsqrt(jnp.mean(center * center, axis=-1, keepdims=True) + 1e-06)
    return center * scale, scale


def feed_kernel(
    mid_ref,
    cot_ref,
    mask_ref,
    vec_ref,
    shift_ref,
    up_ref,
    down_ref,
    out_ref,
    total_ref,
    branch_ref,
    sums_ref,
    up_bias_ref,
    up_grad_ref,
    down_grad_ref,
    normed_ref,
    turned_ref,
    down_in_ref,
    down_turn_ref,
    out_acc_ref,
    in_acc_ref,
    weight_ref,
):
    f32 = jnp.float32
    bf16 = jnp.bfloat16
    step = pl.program_id(0)
    groups, heads, height, width = up_ref.shape
    cols = weight_ref.shape[1] // groups
    folds = width // cols
    rows = height * folds
    pieces, _, out_cols, _ = down_ref.shape

    @pl.when(step == 0)
    def _():
        unit, _ = norm_parts(mid_ref[...])
        normed = (unit * vec_ref[1:2] + vec_ref[2:3]).astype(bf16)
        normed_ref[...] = normed
        turned_ref[...] = normed.T
        masked = mask_ref[...] * cot_ref[...].astype(f32)
        down_in_ref[...] = masked.astype(bf16)
        down_turn_ref[...] = masked.astype(bf16).T
        out_acc_ref[...] = jnp.zeros_like(out_acc_ref)
        in_acc_ref[...] = jnp.zeros_like(in_acc_ref)

    for g in range(groups):
        for h in range(heads):
            for s in range(folds):
                top = h * rows + s * height
                weight_ref[top : top + height, g * cols : (g + 1) * cols] = up_ref[
                    g, h, :, s * cols : (s + 1) * cols
                ]
    weight = weight_ref[...]
    down = down_ref[...].reshape(pieces * out_cols, width)
    hidden = mm(normed_ref[...], weight) + shift_ref[0]
    share = 0.5 * (1.0 + lax.erf(hidden * (0.5**0.5)))
    active = (hidden * share).astype(bf16)
    slope = share + hidden * jnp.exp(-0.5 * hidden * hidden) * 0.3989422804014327
    out_acc_ref[...] += mm_nt(active, down)
    hidden_grad = (mm(down_in_ref[...], down) * slope).astype(bf16)
    down_grad_ref[...] = (
        mm(down_turn_ref[...], active).astype(bf16).reshape(pieces, 1, out_cols, width)
    )
    in_acc_ref[...] += mm_nt(hidden_grad, weight)
    up_bias_ref[0] = jnp.sum(hidden_grad.astype(f32), axis=0, keepdims=True)
    up_grad = mm(turned_ref[...], hidden_grad).astype(bf16)
    for g in range(groups):
        for h in range(heads):
            for s in range(folds):
                top = h * rows + s * height
                up_grad_ref[g, h, :, s * cols : (s + 1) * cols] = up_grad[
                    top : top + height, g * cols : (g + 1) * cols
                ]

    @pl.when(step == pl.num_programs(0) - 1)
    def _():
        middle = mid_ref[...]
        mask = mask_ref[...]
        cot = cot_ref[...].astype(f32)
        out_ref[...] = (middle + mask * (out_acc_ref[...] + vec_ref[3:4])).astype(bf16)
        unit, scale = norm_parts(middle)
        grad_in = in_acc_ref[...]
        inner = grad_in * vec_ref[1:2]
        total = cot + scale * (
            inner
            - jnp.mean(inner, axis=-1, keepdims=True)
            - unit * jnp.mean(inner * unit, axis=-1, keepdims=True)
        )
        branch = (mask * total).astype(bf16)
        total_ref[...] = total
        branch_ref[...] = branch
        sums_ref[...] = jnp.concatenate(
            [
                jnp.sum(branch.astype(f32), axis=0, keepdims=True),
                jnp.sum(grad_in * unit, axis=0, keepdims=True),
                jnp.sum(grad_in, axis=0, keepdims=True),
                jnp.sum(mask * cot, axis=0, keepdims=True),
            ],
            axis=0,
        )


def feed_forward(middle, cot, mask, vectors, shift, gathered, up_height, out_cols):
    tokens, width = middle.shape
    groups, heads = gathered.shape[:2]
    steps = shift.shape[0]
    per_step = groups // steps
    f32 = jnp.float32
    bf16 = jnp.bfloat16

    def whole(rows, cols):
        return pl.BlockSpec((rows, cols), lambda c: (0, 0))

    up_spec = (per_step, heads, up_height, width)
    down_spec = (groups, 1, out_cols, width)
    return pl.pallas_call(
        feed_kernel,
        grid=(steps,),
        in_specs=[
            whole(tokens, width),
            whole(tokens, width),
            whole(tokens, 1),
            whole(vectors.shape[0], width),
            pl.BlockSpec((1, 1, width), lambda c: (c, 0, 0)),
            pl.BlockSpec(up_spec, lambda c: (c, 0, 0, 0)),
            pl.BlockSpec(down_spec, lambda c: (0, c, 1, 0)),
        ],
        out_specs=[
            whole(tokens, width),
            whole(tokens, width),
            whole(tokens, width),
            whole(4, width),
            pl.BlockSpec((1, 1, width), lambda c: (c, 0, 0)),
            pl.BlockSpec(up_spec, lambda c: (c, 0, 0, 0)),
            pl.BlockSpec(down_spec, lambda c: (0, c, 0, 0)),
        ],
        out_shape=[
            jax.ShapeDtypeStruct((tokens, width), bf16),
            jax.ShapeDtypeStruct((tokens, width), f32),
            jax.ShapeDtypeStruct((tokens, width), bf16),
            jax.ShapeDtypeStruct((4, width), f32),
            jax.ShapeDtypeStruct((steps, 1, width), f32),
            jax.ShapeDtypeStruct((groups, heads, up_height, width), bf16),
            jax.ShapeDtypeStruct((groups, heads, out_cols, width), bf16),
        ],
        scratch_shapes=[
            pltpu.VMEM((tokens, width), bf16),
            pltpu.VMEM((width, tokens), bf16),
            pltpu.VMEM((tokens, width), bf16),
            pltpu.VMEM((width, tokens), bf16),
            pltpu.VMEM((tokens, width), f32),
            pltpu.VMEM((tokens, width), f32),
            pltpu.VMEM((width, width), bf16),
        ],
        name="feed_forward",
        compiler_params=pltpu.CompilerParams(dimension_semantics=("arbitrary",)),
    )(middle, cot, mask, vectors, shift, gathered, gathered)


def layer_norm(values, gain, shift):
    center = values - jnp.mean(values, axis=-1, keepdims=True)
    spread = jnp.mean(center * center, axis=-1, keepdims=True)
    return center * lax.rsqrt(spread + 1e-06) * gain + shift


def interp_matrix(img_side):
    coord = jnp.arange(SMAX, dtype=jnp.int32)
    length_in = 2 * SMAX - 1
    length_out = 2 * img_side - 1
    offset = jnp.clip(coord[:, None] - coord[None, :] + img_side - 1, 0, length_out - 1)
    numer = jnp.maximum((2 * offset + 1) * length_in - length_out, 0)
    lower = numer // (2 * length_out)
    weight_hi = (numer - lower * 2 * length_out).astype(jnp.float32) / (2 * length_out).astype(
        jnp.float32
    )
    upper = jnp.minimum(lower + 1, length_in - 1)
    target = jnp.arange(length_in, dtype=jnp.int32)
    lower_hot = (target == lower[..., None]).astype(jnp.float32)
    upper_hot = (target == upper[..., None]).astype(jnp.float32)
    return (1.0 - weight_hi)[..., None] * lower_hot + weight_hi[..., None] * upper_hot


def contract_rows(left, right):
    return lax.dot_general(
        left, right, (((0,), (0,)), ((), ())), preferred_element_type=jnp.float32
    )


def contract_cols(left, right):
    return lax.dot_general(
        left, right, (((1,), (1,)), ((), ())), preferred_element_type=jnp.float32
    )


def exchange(values, axis):
    return lax.all_to_all(values, axis, split_axis=0, concat_axis=0, tiled=True)


def spread(values, axis):
    count = lax.axis_size(axis)
    return exchange(jnp.broadcast_to(values, (count,) + values.shape), axis)


def swap(values, step):
    pairs = [(i, i ^ step) for i in range(lax.axis_size("ha"))]
    return lax.ppermute(values, "ha", pairs)


def gather_heads(values, beside, later):
    me = lax.axis_index("ha")
    far = swap(values, 2)
    near = swap(values, 1)
    far, near, beside, later = lax.optimization_barrier((far, near, beside, later))
    corner = swap(far, 1)
    blocks = jnp.stack([values, near, far, corner])
    ordered = [
        lax.dynamic_index_in_dim(blocks, jnp.bitwise_xor(me, i), 0, False) for i in range(4)
    ]
    return ordered, beside, later


def exchange_heads(parts):
    me = lax.axis_index("ha")
    arrived = [
        swap(lax.dynamic_index_in_dim(parts, jnp.bitwise_xor(me, i), 0, False), i)
        for i in range(1, 4)
    ]
    blocks = jnp.stack([lax.dynamic_index_in_dim(parts, me, 0, False)] + arrived)
    return jnp.stack(
        [lax.dynamic_index_in_dim(blocks, jnp.bitwise_xor(me, i), 0, False) for i in range(4)]
    )


def scatter_heads(parts):
    me = lax.axis_index("ha")
    other = [lax.dynamic_index_in_dim(parts, jnp.bitwise_xor(me, i), 0, False) for i in range(4)]
    arrived = swap(jnp.stack([other[3], other[1]]), 1).astype(jnp.float32)
    far = (other[2].astype(jnp.float32) + arrived[0]).astype(jnp.bfloat16)
    near = other[0].astype(jnp.float32) + arrived[1]
    return near + swap(far, 2).astype(jnp.float32)


def pack_up(piece):
    rows, width = piece.shape[-2:]
    lead = piece.shape[:-2]
    fold = 4 * rows // width
    cut = piece.reshape(lead + (fold, rows // fold, width))
    return jnp.swapaxes(cut, -3, -2).reshape(lead + (rows // fold, fold * width))


def unpack_up(packed, rows, width):
    fold = packed.shape[-1] // width
    lead = packed.shape[:-2]
    cut = packed.reshape(lead + (rows // fold, fold, width))
    return jnp.swapaxes(cut, -3, -2).reshape(lead + (rows, width))


def local(
    patches,
    cotangent,
    sides,
    norm1_gain,
    norm1_bias,
    qkv_weight,
    query_bias,
    value_bias,
    proj_weight,
    proj_bias,
    norm2_gain,
    norm2_bias,
    fc1_weight,
    fc1_bias,
    fc2_weight,
    fc2_bias,
    rel_height,
    rel_width,
):
    group_count = lax.axis_size("ga")
    head_groups = lax.axis_size("ha")
    group_index = lax.axis_index("ga")
    head_index = lax.axis_index("ha")
    device_count = group_count * head_groups
    block_len = patches.shape[1]
    model_width = patches.shape[2]
    hidden_width = fc1_bias.shape[0] * head_groups
    local_tokens = group_count * block_len
    group_width = model_width // head_groups
    group_heads = HEADS // head_groups
    cap_tokens = SMAX * SMAX
    f32 = jnp.float32
    bf16 = jnp.bfloat16

    triple_rows = lax.all_gather(qkv_weight, "ga", axis=1, tiled=True)
    up_rows, up_cols = fc1_weight.shape
    out_cols = fc2_weight.shape[1]
    up_height = up_rows * up_cols // model_width
    out_share = out_cols // head_groups
    pack_rows = up_height + out_cols + out_share

    vectors = jnp.concatenate(
        [norm1_gain, norm1_bias, proj_bias, norm2_gain, norm2_bias, fc2_bias, fc1_bias]
    )
    vector_size = vectors.shape[0]
    vectors_all = lax.all_gather(
        jnp.concatenate([vectors, proj_weight.T.reshape(-1)]), "ha", axis=0, tiled=False
    )
    proj_rows = vectors_all[:, vector_size:].reshape(head_groups, head_groups, -1)
    proj_mine = lax.dynamic_index_in_dim(proj_rows, head_index, 1, False)
    packed = jnp.concatenate(
        [
            pack_up(fc1_weight),
            fc2_weight.T,
            proj_mine.reshape(head_groups, out_share, group_width)
            .transpose(1, 0, 2)
            .reshape(out_share, model_width),
        ],
        axis=0,
    )
    tokens_in = lax.all_to_all(patches, "ga", split_axis=0, concat_axis=1, tiled=True)[0]
    tokens_in, triple_rows, vectors_all = lax.optimization_barrier(
        (tokens_in, triple_rows, vectors_all)
    )
    cot_in = lax.all_to_all(cotangent, "ga", split_axis=0, concat_axis=1, tiled=True)[0]
    wide = model_width // head_groups

    def vector_at(slot, width):
        return vectors_all[:, slot * wide : slot * wide + width].reshape(-1)

    first_gain = vector_at(0, wide)
    first_shift = vector_at(1, wide)
    proj_shift = vector_at(2, wide)
    second_gain = vector_at(3, wide)
    second_shift = vector_at(4, wide)
    down_shift = vector_at(5, wide)
    up_shift = vector_at(6, 4 * wide)

    triple_cut = triple_rows.reshape(group_width, 3, head_groups, group_width).transpose(2, 0, 1, 3)
    triple_own = exchange(
        triple_cut.reshape(head_groups, group_width, 3 * group_width), "ha"
    ).reshape(model_width, 3 * group_width)
    tokens32 = tokens_in.astype(f32)
    slot_index = jnp.arange(local_tokens, dtype=jnp.int32)
    grid_index = (
        slot_index // block_len * head_groups + head_index
    ) * block_len + slot_index % block_len
    img_side = lax.dynamic_index_in_dim(sides, group_index, 0, keepdims=False)
    tok_mask = ((grid_index // SMAX < img_side) & (grid_index % SMAX < img_side)).astype(f32)[
        :, None
    ]
    all_index = jnp.arange(cap_tokens, dtype=jnp.int32)[:, None]
    line_index = jnp.arange(2 * SMAX, dtype=jnp.int32)[None, :]
    expand = jnp.where(
        line_index < SMAX,
        all_index // SMAX == line_index,
        all_index % SMAX == line_index - SMAX,
    ).astype(bf16)
    line_valid = line_index[0] % SMAX < img_side
    matrix = interp_matrix(img_side)
    table_h = jnp.einsum(
        "qkj,jd->qkd", matrix, rel_height.astype(f32), precision=exact_mode
    ).astype(bf16)
    table_w = jnp.einsum("qkj,jd->qkd", matrix, rel_width.astype(f32), precision=exact_mode).astype(
        bf16
    )

    blocks_all, triple_own, packed = gather_heads(tokens_in, triple_own, packed)
    tokens_all = (
        jnp.stack(
            [block.reshape(group_count, block_len, model_width) for block in blocks_all],
            axis=1,
        )
        .reshape(cap_tokens, model_width)
        .astype(f32)
    )
    gain32 = first_gain.astype(f32)
    shift32 = first_shift.astype(f32)
    normed_all = layer_norm(tokens_all, gain32, shift32).astype(bf16)
    bias_own = jnp.concatenate([query_bias, jnp.zeros_like(query_bias), value_bias]).astype(f32)
    mixed = (jnp.dot(normed_all, triple_own, preferred_element_type=f32) + bias_own).astype(bf16)
    q_grid = (
        mixed[:, :group_width].reshape(SMAX, SMAX, group_heads, HD).transpose(2, 0, 1, 3)
    )
    rel_h = jnp.einsum("hrwd,rkd->hrwk", q_grid, table_h, preferred_element_type=f32)
    rel_w = jnp.einsum("hrwd,wkd->hrwk", q_grid, table_w, preferred_element_type=f32)
    rel_both = jnp.concatenate([rel_h, rel_w], axis=-1).reshape(
        group_heads, cap_tokens, 2 * SMAX
    )
    rel_upper = lax.reduce_precision(rel_both, 8, 7)
    rel_lower = jnp.where(line_valid, rel_both - rel_upper, 0.0).astype(bf16)
    rel_upper = jnp.where(line_valid, rel_upper, -1e30).astype(bf16)
    rel_split = jnp.concatenate([rel_upper, rel_lower], axis=-1)
    rel_split, cot_in = lax.optimization_barrier((rel_split, cot_in))
    cot32 = cot_in.astype(f32)
    att_heads, log_sums = attend_forward(mixed, rel_split, expand)

    gathered = lax.all_gather(packed, BOTH, axis=0, tiled=False)
    att_heads, gathered = lax.optimization_barrier((att_heads, gathered))
    gathered = gathered.reshape(group_count, head_groups, pack_rows, model_width)
    proj_turn = gathered[:, :, up_height + out_cols :].reshape(model_width, model_width)

    att_back = lax.all_to_all(
        att_heads.reshape(group_count, head_groups, block_len, 1, group_width),
        "ha",
        split_axis=1,
        concat_axis=3,
        tiled=True,
    )
    att_tok = att_back.reshape(local_tokens, model_width)
    branch = contract_cols(att_tok, proj_turn) + proj_shift.astype(f32)
    middle = tokens32 + tok_mask * branch
    steps = hidden_width // model_width
    if out_cols % 16 == 0 and up_cols % 128 == 0 and up_height == out_cols and steps == head_groups:
        norm_vectors = jnp.stack([proj_shift, second_gain, second_shift, down_shift]).astype(f32)
        (
            block_out,
            mid_total,
            branch_grad,
            small_sums,
            up_bias_grad,
            up_packed,
            down_packed,
        ) = feed_forward(
            middle,
            cot_in,
            tok_mask,
            norm_vectors,
            up_shift.astype(f32).reshape(steps, 1, model_width),
            gathered,
            up_height,
            out_cols,
        )
        up_bias_grad = up_bias_grad.reshape(-1)
        proj_bias_grad, second_gain_grad, second_shift_grad, down_bias_grad = small_sums
    else:
        up_full = (
            unpack_up(gathered[:, :, :up_height], up_rows, up_cols)
            .transpose(1, 2, 0, 3)
            .reshape(model_width, hidden_width)
        )
        down_turn = (
            gathered[:, :, up_height : up_height + out_cols]
            .transpose(0, 2, 1, 3)
            .reshape(model_width, hidden_width)
        )
        normed2 = layer_norm(middle, second_gain.astype(f32), second_shift.astype(f32)).astype(bf16)
        hidden = jnp.dot(normed2, up_full, preferred_element_type=f32) + up_shift.astype(f32)
        activated = jax.nn.gelu(hidden, approximate=False).astype(bf16)
        block_out = (
            middle + tok_mask * (contract_cols(activated, down_turn) + down_shift.astype(f32))
        ).astype(bf16)
        masked_cot = tok_mask * cot32
        down_in = masked_cot.astype(bf16)
        down_grad = contract_rows(down_in, activated).astype(bf16)
        down_bias_grad = jnp.sum(masked_cot, axis=0)
        act_grad = jnp.dot(down_in, down_turn, preferred_element_type=f32)
        _, gelu_pull = jax.vjp(partial(jax.nn.gelu, approximate=False), hidden)
        hidden_grad = gelu_pull(act_grad)[0].astype(bf16)
        up_grad = contract_rows(normed2, hidden_grad).astype(bf16)
        up_bias_grad = jnp.sum(hidden_grad.astype(f32), axis=0)
        norm2_in = contract_cols(hidden_grad, up_full)
        _, norm2_pull = jax.vjp(
            layer_norm, middle, second_gain.astype(f32), second_shift.astype(f32)
        )
        mid_grad, second_gain_grad, second_shift_grad = norm2_pull(norm2_in)
        mid_total = cot32 + mid_grad
        branch_grad = (tok_mask * mid_total).astype(bf16)
        up_packed = pack_up(
            up_grad.reshape(head_groups, up_rows, group_count, up_cols).transpose(2, 0, 1, 3)
        )
        down_packed = down_grad.reshape(group_count, out_cols, head_groups, model_width).transpose(
            0, 2, 1, 3
        )
        proj_bias_grad = jnp.sum(branch_grad.astype(f32), axis=0)

    att_grad_tok = jnp.dot(branch_grad, proj_turn, preferred_element_type=f32).astype(bf16)
    att_grad_tok, branch_turn, up_packed, down_packed = lax.optimization_barrier(
        (att_grad_tok, branch_grad, up_packed, down_packed)
    )
    att_grad = lax.all_to_all(
        att_grad_tok.reshape(group_count, 1, block_len, head_groups, group_width),
        "ha",
        split_axis=3,
        concat_axis=1,
        tiled=True,
    ).reshape(cap_tokens, group_width)
    att_grad, block_out = lax.optimization_barrier((att_grad, block_out))
    out_back = exchange(block_out.reshape(group_count, block_len, model_width), "ga")

    proj_grad = contract_rows(branch_turn, att_tok).astype(bf16)
    grads_packed = jnp.concatenate(
        [
            up_packed,
            down_packed,
            proj_grad.reshape(group_count, head_groups, out_share, model_width),
        ],
        axis=2,
    ).reshape(device_count * pack_rows, model_width)
    grads_own = lax.psum_scatter(grads_packed, BOTH, scatter_dimension=0, tiled=True)
    query_part, height_grad, width_grad, key_value_grad = attend_backward(
        mixed, rel_split, expand, att_grad, att_heads, log_sums
    )
    query_part, height_grad, width_grad, key_value_grad, out_back = lax.optimization_barrier(
        (query_part, height_grad, width_grad, key_value_grad, out_back)
    )
    height_grad = height_grad.reshape(group_heads, SMAX, SMAX, SMAX)
    width_grad = width_grad.reshape(group_heads, SMAX, SMAX, SMAX)
    query_grad = (
        query_part.reshape(group_heads, SMAX, SMAX, HD)
        + jnp.einsum("hrwj,rjd->hrwd", height_grad, table_h, preferred_element_type=f32)
        + jnp.einsum("hrwj,wjd->hrwd", width_grad, table_w, preferred_element_type=f32)
    ).astype(bf16)
    mixed_grad = jnp.concatenate(
        [query_grad[i].reshape(cap_tokens, HD) for i in range(group_heads)] + [key_value_grad],
        axis=1,
    )
    triple_part = contract_rows(normed_all, mixed_grad).astype(bf16)
    mixed_grad, triple_part, height_grad, width_grad = lax.optimization_barrier(
        (mixed_grad, triple_part, height_grad, width_grad)
    )
    norm1_wide = contract_cols(mixed_grad, triple_own)
    h_table_grad = jnp.einsum("hrwj,hrwd->rjd", height_grad, q_grid, preferred_element_type=f32)
    w_table_grad = jnp.einsum("hrwj,hrwd->wjd", width_grad, q_grid, preferred_element_type=f32)
    norm1_part = (
        norm1_wide.astype(bf16)
        .reshape(group_count, head_groups, block_len, model_width)
        .transpose(1, 0, 2, 3)
        .reshape(head_groups, local_tokens, model_width)
    )
    norm1_in = scatter_heads(norm1_part)
    norm1_in, grads_own = lax.optimization_barrier((norm1_in, grads_own))
    triple_rows_grad = (
        exchange_heads(triple_part.reshape(head_groups, group_width, 3 * group_width))
        .reshape(head_groups, group_width, 3, group_width)
        .transpose(1, 2, 0, 3)
        .reshape(group_width, group_count, 3 * model_width // group_count)
        .transpose(1, 0, 2)
    )
    triple_grad = jnp.sum(exchange(triple_rows_grad, "ga").astype(f32), axis=0)

    center = tokens_all - jnp.mean(tokens_all, axis=-1, keepdims=True)
    unit = center * lax.rsqrt(jnp.mean(center * center, axis=-1, keepdims=True) + 1e-06)
    first_gain_grad = jnp.sum(norm1_wide * unit, axis=0)
    first_shift_grad = jnp.sum(norm1_wide, axis=0)
    mixed_float = mixed_grad.astype(f32)
    height_rel = jnp.einsum("qkj,qkd->jd", matrix, h_table_grad, precision=exact_mode)
    width_rel = jnp.einsum("qkj,qkd->jd", matrix, w_table_grad, precision=exact_mode)
    rel_flat = jnp.concatenate([height_rel, width_rel]).reshape(-1)
    rel_size = rel_flat.shape[0]
    grouped = [
        first_gain_grad,
        first_shift_grad,
        proj_bias_grad,
        second_gain_grad,
        second_shift_grad,
        down_bias_grad,
        up_bias_grad,
    ]
    small = jnp.concatenate(
        [vector.reshape(head_groups, -1) for vector in grouped]
        + [rel_flat.reshape(head_groups, -1)],
        axis=1,
    )
    small = small + swap(small, 1)
    small = small + swap(small, 2)
    own_part = lax.dynamic_index_in_dim(small, head_index, 0, False)
    own_size = own_part.shape[0] - rel_size // head_groups
    last_part = jnp.concatenate(
        [
            own_part[:own_size],
            jnp.sum(mixed_float[:, :group_width], axis=0),
            jnp.sum(mixed_float[:, 2 * group_width :], axis=0),
            small[:, own_size:].reshape(-1),
        ]
    )
    last_size = last_part.shape[0]
    last_part = jnp.pad(last_part, (0, -last_size % 128)).reshape(-1, 128)
    last_sum = jnp.sum(spread(last_part, "ga"), axis=0).reshape(-1)[:last_size]
    rel_sum = last_sum[last_size - rel_size :].reshape(2, 2 * SMAX - 1, HD)
    late = []
    at = 0
    for size in [group_width] * 6 + [hidden_width // head_groups] + [group_width] * 2:
        late.append(last_sum[at : at + size])
        at += size

    up_own = unpack_up(grads_own[:up_height], up_rows, up_cols).astype(f32)
    down_own = grads_own[up_height : up_height + out_cols].T.astype(f32)
    proj_own = (
        exchange_heads(
            grads_own[up_height + out_cols :]
            .reshape(out_share, head_groups, group_width)
            .transpose(1, 0, 2)
        )
        .reshape(out_cols, group_width)
        .T.astype(f32)
    )

    _, norm1_pull = jax.vjp(lambda tokens: layer_norm(tokens, gain32, shift32), tokens32)
    input_grad = (mid_total + norm1_pull(norm1_in)[0]).astype(bf16)
    in_back = exchange(input_grad.reshape(group_count, block_len, model_width), "ga")
    return (
        out_back,
        in_back,
        late[0],
        late[1],
        triple_grad,
        late[7],
        late[8],
        proj_own,
        late[2],
        late[3],
        late[4],
        up_own,
        late[6],
        down_own,
        late[5],
        rel_sum[0],
        rel_sum[1],
    )


def solution(mesh):
    placed = (
        P(None, ("ga", "ha"), None),
        P(None, ("ga", "ha"), None),
        P(),
        P("ha"),
        P("ha"),
        P("ha", "ga"),
        P("ha"),
        P("ha"),
        P("ha", "ga"),
        P("ha"),
        P("ha"),
        P("ha"),
        P("ha", "ga"),
        P("ha"),
        P("ha", "ga"),
        P("ha"),
        P(),
        P(),
    )
    return jax.shard_map(
        local,
        mesh=mesh,
        in_specs=placed,
        out_specs=(
            P(None, ("ga", "ha"), None),
            P(None, ("ga", "ha"), None),
            P("ha"),
            P("ha"),
            P("ha", "ga"),
            P("ha"),
            P("ha"),
            P("ha", "ga"),
            P("ha"),
            P("ha"),
            P("ha"),
            P("ha", "ga"),
            P("ha"),
            P("ha", "ga"),
            P("ha"),
            P(),
            P(),
        ),
        check_vma=False,
    )
```
